32 devices in a mesh: gx: 4 (over z), gy: 2 (over x), gz: 4 (over y, core).
Axes of the slice: x: 2, y: 2, z: 4, core: 2. Of those that a mesh axis runs over, the one named last changes fastest.
Arguments:
- fine_rhs: float32 [96, 32, 1024], P(('gx', 'gy', 'gz')), may hold values from -6 to 6
- coarse_rhs: float32 [128, 64, 512], P('gx', 'gy', 'gz'), may hold values from -6 to 6
- patch_count: int32 [32], P(('gx', 'gy', 'gz')), may hold values from 2 to 3, as said below
- patch_corner: int32 [96, 3], P(('gx', 'gy', 'gz')), may hold values from 0 to 496, as said below
Outputs:
- fine_solution: float32 [96, 32, 1024], P(('gx', 'gy', 'gz'))
- coarse_solution: float32 [128, 64, 512], P('gx', 'gy', 'gz')
The draws below stay inside these ranges and needn't reach their ends.
Inputs may be any that keep to these rules, and one draw needn't show every extreme that they name: Slots 0 to patch_count[d] - 1 of device d hold live patches, the others are unused. `patch_corner`: A live patch's footprint starts at a multiple of 16 in each dimension and lies inside the coarse block of one device with the same gx and gy indices as the patch's owner; live footprints never intersect; at most 2 live patches of one device lie in the block of any one device. Rows of unused slots are zero.
All inputs are finite; a program needn't handle non-finite values.
Results may differ from the reference program's by a relative error of at most 0.00007.
Values sent between devices are 32-bit elements; how exact they have to be, the bound alone decides.
No kernel may reach another device: no remote copies, remote signals or barrier semaphores. Data moves between devices by JAX's collectives and lax.ppermute only.
A program may use at most 64 MiB of HBM per device.

```python
import jax
import jax.numpy as jnp
from jax import lax

PATCH = 32
FOOT = 16
SLOTS = 3
CAP = 2
CX = 32
CY = 32
CZ = 128
SWEEPS = 3
FINE_SWEEPS = 2
NX = 128
NY = 64
NZ = 512
PATCHES = 96
N_GX = 4
N_GY = 2
N_GZ = 4


def patch_layout(key):
    base_key = jax.random.fold_in(key, 4242)
    key_hot, key_count, key_busy, key_order, key_place = jax.random.split(base_key, 5)
    columns = N_GX * N_GY
    group_size = N_GZ
    spots_first = CX // FOOT
    spots_second = CY // FOOT
    spots_third = CZ // FOOT
    spot_total = spots_first * spots_second * spots_third
    hottest = jax.random.randint(key_hot, (columns,), 0, group_size)
    counts = jax.random.randint(key_count, (columns, group_size), CAP, max(SLOTS // 2, CAP) + 1)
    busiest = jax.random.randint(key_busy, (columns,), 0, group_size)
    owners = jnp.arange(group_size, dtype=jnp.int32)
    counts = jnp.where(owners[None, :] == busiest[:, None], SLOTS, counts)
    scores = jax.random.randint(key_order, (columns, group_size, group_size), 0, 1 << 20) * group_size + owners[None, None, :]
    scores = jnp.where(owners[None, None, :] == hottest[:, None, None], -1, scores)
    home_order = jnp.argsort(scores, axis=2)
    slot_range = jnp.arange(SLOTS, dtype=jnp.int32)
    home_slot = home_order[:, :, slot_range // CAP]
    spot_range = jnp.arange(spot_total, dtype=jnp.int32)
    spot_scores = jax.random.randint(key_place, (columns, group_size, spot_total), 0, 1 << 20) * spot_total + spot_range[None, None, :]
    places = jnp.argsort(spot_scores, axis=2)
    pick_rank = owners[None, :, None] * CAP + (slot_range % CAP)[None, None, :]
    pick_rank = jnp.broadcast_to(pick_rank, (columns, group_size, SLOTS))
    column_index = jnp.broadcast_to(jnp.arange(columns, dtype=jnp.int32)[:, None, None], (columns, group_size, SLOTS))
    spot_index = places[column_index, home_slot, pick_rank]
    spot_first = spot_index // (spots_second * spots_third)
    spot_second = spot_index // spots_third % spots_second
    spot_third = spot_index % spots_third
    column_range = jnp.arange(columns, dtype=jnp.int32)
    base_first = column_range // N_GY * CX
    base_second = column_range % N_GY * CY
    corner_first = base_first[:, None, None] + spot_first * FOOT
    corner_second = base_second[:, None, None] + spot_second * FOOT
    corner_third = home_slot * CZ + spot_third * FOOT
    alive_mask = slot_range[None, None, :] < counts[:, :, None]
    corners = jnp.stack([corner_first, corner_second, corner_third], -1) * alive_mask[:, :, :, None].astype(jnp.int32)
    return (counts.reshape(-1).astype(jnp.int32), corners.reshape(-1, 3).astype(jnp.int32))


def draw_patch_count(key, part):
    return patch_layout(key)[0]


def draw_patch_corner(key, part):
    return patch_layout(key)[1]


def draw_coarse_rhs(key, part):
    key_noise = jax.random.fold_in(key, 17)
    return jnp.clip(jax.random.normal(key_noise, (NX, NY, NZ), jnp.float32), -6.0, 6.0)


def steps_of(rng, dims, pieces, least, high):
    level, own = 1.0, jax.random.fold_in(rng, 6)
    for dim, parts in pieces:
        draws = jnp.exp(jax.random.uniform(jax.random.fold_in(own, dim), (parts,), jnp.float32, least / len(pieces), high / len(pieces)))
        level = level * jnp.repeat(draws, dims[dim] // parts).reshape([-1 if axis == dim else 1 for axis in range(len(dims))])
    return level


def bell_draw(rng, extent, width, bound, cuts=(), held_as=jnp.bfloat16):
    level = steps_of(rng, extent, cuts, -0.22, 0.18) if cuts else 1.0
    entries = jax.random.normal(rng, extent, jnp.float32) * width * level
    return jnp.minimum(jnp.maximum(entries, -bound), bound).astype(held_as)


def setup_inputs(seed: int = 0) -> dict:
    streams_of = jax.random.split(jax.random.key(seed), 5)
    fine_rhs = bell_draw(streams_of[0], (PATCHES, PATCH, PATCH * PATCH), 1.0, 6.0, ((0, 32),), jnp.float32)
    coarse_rhs = draw_coarse_rhs(jax.random.fold_in(streams_of[4], 71), 0)
    patch_count = draw_patch_count(jax.random.fold_in(streams_of[4], 71), 0)
    patch_corner = draw_patch_corner(jax.random.fold_in(streams_of[4], 71), 0)
    return {"fine_rhs": fine_rhs, "coarse_rhs": coarse_rhs, "patch_count": patch_count, "patch_corner": patch_corner}


RELAX_WEIGHT = 0.9


def neighbors(padded):
    total = padded[2:, 1:-1, 1:-1] + padded[:-2, 1:-1, 1:-1]
    total = total + padded[1:-1, 2:, 1:-1] + padded[1:-1, :-2, 1:-1]
    return total + padded[1:-1, 1:-1, 2:] + padded[1:-1, 1:-1, :-2]


def relax_step(values_now, right_side, rim_values):
    total = neighbors(jnp.pad(values_now, 1) + rim_values)
    return values_now + RELAX_WEIGHT * (right_side - (6.0 * values_now - total)) / 6.0


def broaden(face_rows):
    return jnp.repeat(jnp.repeat(face_rows, 2, 0), 2, 1)


def pre_patch(right_side):
    rim_values = jnp.zeros_like(jnp.pad(right_side, 1))
    values_now = jnp.zeros_like(right_side)
    for iteration in range(FINE_SWEEPS):
        values_now = relax_step(values_now, right_side, rim_values)
    residual = right_side - (6.0 * values_now - neighbors(jnp.pad(values_now, 1)))
    averages = 0.5 * residual.reshape(FOOT, 2, FOOT, 2, FOOT, 2).sum(axis=(1, 3, 5))
    return values_now, averages


def post_patch(right_side, start_values, coarse_cube):
    parent = coarse_cube[1:-1, 1:-1, 1:-1]
    lifted = jnp.repeat(jnp.repeat(jnp.repeat(parent, 2, 0), 2, 1), 2, 2)
    rim_values = jnp.zeros_like(jnp.pad(right_side, 1))
    rim_values = rim_values.at[0, 1:-1, 1:-1].set(broaden(coarse_cube[0, 1:-1, 1:-1]))
    rim_values = rim_values.at[-1, 1:-1, 1:-1].set(broaden(coarse_cube[-1, 1:-1, 1:-1]))
    rim_values = rim_values.at[1:-1, 0, 1:-1].set(broaden(coarse_cube[1:-1, 0, 1:-1]))
    rim_values = rim_values.at[1:-1, -1, 1:-1].set(broaden(coarse_cube[1:-1, -1, 1:-1]))
    rim_values = rim_values.at[1:-1, 1:-1, 0].set(broaden(coarse_cube[1:-1, 1:-1, 0]))
    rim_values = rim_values.at[1:-1, 1:-1, -1].set(broaden(coarse_cube[1:-1, 1:-1, -1]))
    values_now = start_values + lifted
    for iteration in range(FINE_SWEEPS):
        values_now = relax_step(values_now, right_side, rim_values)
    return values_now


def reference(fine_rhs, coarse_rhs, patch_count, patch_corner):
    patch_total = fine_rhs.shape[0]
    owners = patch_total // SLOTS
    cubes_in = fine_rhs.reshape(owners, SLOTS, PATCH, PATCH, PATCH)
    fine_pre, averages = lax.map(jax.vmap(pre_patch), cubes_in)
    patch_range = jnp.arange(patch_total, dtype=jnp.int32)
    alive_mask = (patch_range % SLOTS) < patch_count[patch_range // SLOTS]
    cells_first, cells_second, cells_third = coarse_rhs.shape
    spots_first = cells_first // FOOT
    spots_second = cells_second // FOOT
    spots_third = cells_third // FOOT
    spot_coords = patch_corner // FOOT
    spot_first = jnp.where(alive_mask, spot_coords[:, 0], spots_first).astype(jnp.int32)
    spot_second = jnp.where(alive_mask, spot_coords[:, 1], spots_second).astype(jnp.int32)
    spot_third = jnp.where(alive_mask, spot_coords[:, 2], spots_third).astype(jnp.int32)
    placed = jnp.zeros((spots_first, spots_second, spots_third, FOOT, FOOT, FOOT), jnp.float32)
    placed = placed.at[spot_first, spot_second, spot_third].set(averages.reshape(patch_total, FOOT, FOOT, FOOT), mode="drop")
    covered = jnp.zeros((spots_first, spots_second, spots_third), jnp.float32)
    covered = covered.at[spot_first, spot_second, spot_third].set(1.0, mode="drop")
    blocks = coarse_rhs.reshape(spots_first, FOOT, spots_second, FOOT, spots_third, FOOT).transpose(0, 2, 4, 1, 3, 5)
    blocks = jnp.where(covered[:, :, :, None, None, None] > 0.5, placed, blocks)
    composite = blocks.transpose(0, 3, 1, 4, 2, 5).reshape(cells_first, cells_second, cells_third)
    solution = RELAX_WEIGHT * composite / 6.0
    for iteration in range(SWEEPS - 1):
        solution = solution + RELAX_WEIGHT * (composite - (6.0 * solution - neighbors(jnp.pad(solution, 1)))) / 6.0
    padded = jnp.pad(solution, 1)

    def cut_cube(corner_row):
        return lax.dynamic_slice(padded, (corner_row[0], corner_row[1], corner_row[2]), (FOOT + 2, FOOT + 2, FOOT + 2))

    def finish_patches(packed):
        right_rows, start_rows, corner_rows, alive_rows = packed
        coarse_cubes = jax.vmap(cut_cube)(corner_rows)
        results = jax.vmap(post_patch)(right_rows, start_rows, coarse_cubes)
        return results * alive_rows.astype(jnp.float32)[:, None, None, None]

    finished = lax.map(finish_patches, (cubes_in, fine_pre, patch_corner.reshape(owners, SLOTS, 3), alive_mask.reshape(owners, SLOTS)))
    return finished.reshape(fine_rhs.shape), solution
```

```python
import functools

import jax
import jax.numpy as jnp
from jax import lax
from jax.experimental import pallas as pl
from jax.experimental.pallas import tpu as pltpu
from jax.sharding import PartitionSpec as P

LANES = 128
SUB = 8
RIM = 3
CAP = 2
F32 = jnp.float32
BF16 = jnp.bfloat16


def iota(shape, dim):
    return lax.broadcasted_iota(jnp.int32, shape, dim)


def split3(x):
    high = x.astype(BF16)
    rest = x - high.astype(F32)
    middle = rest.astype(BF16)
    low = (rest - middle.astype(F32)).astype(BF16)
    return high, middle, low


def dot3(x, table):
    return sum(jnp.dot(part, table, preferred_element_type=F32) for part in split3(x))


class Plan:
    def __init__(self, fine_shape, coarse_shape):
        self.slots, self.pe, self.merged = fine_shape
        self.foot = self.pe // 2
        self.cx, self.cy, self.cz = coarse_shape
        assert self.cz == LANES and self.merged == self.pe * self.pe
        assert self.foot * self.foot == 2 * LANES and self.pe * 4 == LANES
        self.tiles = self.merged // LANES
        self.fpitch = self.pe + SUB
        self.frows = SUB + self.slots * self.fpitch
        self.nx, self.ny, self.nz = (lax.axis_size(a) for a in ("gx", "gy", "gz"))
        self.pitch = self.cy + SUB
        self.crows = SUB + (self.cx + 2 * RIM) * self.pitch + SUB
        self.spots_y = self.cy // self.foot
        self.spots_z = self.cz // self.foot
        self.avg_rows = self.slots * 2 * self.foot
        self.zrows = self.cy
        assert self.cx * 4 == LANES
        self.erows = CAP * self.foot
        self.elanes = 3 * LANES
        self.yrows = RIM * self.cx
        self.xrows = 3 * self.pitch + SUB
        assert self.xrows == LANES

    def row(self, x, y):
        return SUB + (x + RIM) * self.pitch + y

    def faces(self, shift):
        return shift == 1, shift == self.nz - 1

    def msg_rows(self, shift):
        high, low = self.faces(shift)
        return self.avg_rows + SUB + self.zrows * (int(high) + int(low))


def fine_neighbors(ref, t, row, tiles):
    lane = iota((SUB, LANES), 1)
    mid = ref[t, pl.ds(row, SUB), :]
    total = ref[t, pl.ds(row - 1, SUB), :] + ref[t, pl.ds(row + 1, SUB), :]
    total += jnp.where(lane % 32 == 0, 0.0, pltpu.roll(mid, 1, 1))
    total += jnp.where(lane % 32 == 31, 0.0, pltpu.roll(mid, LANES - 1, 1))
    before = ref[t - 1, pl.ds(row, SUB), :] if t else jnp.zeros_like(mid)
    after = ref[t + 1, pl.ds(row, SUB), :] if t + 1 < tiles else jnp.zeros_like(mid)
    total += pltpu.roll(jnp.where(lane >= LANES - 32, before, mid), 32, 1)
    total += pltpu.roll(jnp.where(lane < 32, after, mid), LANES - 32, 1)
    return mid, total


def zero_gaps(ref, plan):
    gap = jnp.zeros((SUB, LANES), F32)
    for t in range(plan.tiles):
        for p in range(plan.slots + 1):
            row = p * plan.fpitch
            if row + SUB <= plan.frows:
                ref[t, pl.ds(row, SUB), :] = gap


def pack_face(ref, plan, low):
    outs = []
    lane = iota((SUB, LANES), 1)
    start = 0 if low else plan.cz - RIM
    for j in range(plan.cy // SUB):
        acc = jnp.zeros((SUB, LANES), F32)
        for x in range(plan.cx):
            v = pltpu.roll(ref[pl.ds(x * plan.cy + j * SUB, SUB), :], (4 * x - start) % LANES, 1)
            acc = jnp.where(lane // 4 == x, v, acc)
        outs.append(acc)
    return outs


def pre_kernel(plan, count_ref, corner_ref, fine_ref, coarse_ref, pre_ref, *rest):
    msg_refs, (rhs, res) = rest[:-2], rest[-2:]
    pe, foot, tiles = plan.pe, plan.foot, plan.tiles
    zero_gaps(rhs, plan)
    zero_gaps(pre_ref, plan)
    chunks = [(p, j) for p in range(plan.slots) for j in range(pe // SUB)]
    for p, j in chunks:
        row = SUB + p * plan.fpitch + j * SUB
        for t in range(tiles):
            rhs[t, pl.ds(row, SUB), :] = fine_ref[p, pl.ds(j * SUB, SUB), t * LANES : (t + 1) * LANES]
    for p, j in chunks:
        row = SUB + p * plan.fpitch + j * SUB
        for t in range(tiles):
            mid, total = fine_neighbors(rhs, t, row, tiles)
            pre_ref[t, pl.ds(row, SUB), :] = 0.165 * mid + 0.0225 * total
    for p, j in chunks:
        row = SUB + p * plan.fpitch + j * SUB
        for t in range(tiles):
            mid, total = fine_neighbors(pre_ref, t, row, tiles)
            res[t, pl.ds(row, SUB), :] = rhs[t, pl.ds(row, SUB), :] - (6.0 * mid - total)
    source, target = iota((4 * LANES, LANES), 0), iota((4 * LANES, LANES), 1)
    place = (source // LANES) * 32 + (source % LANES) // 64 * 16 + source % 32 // 2
    table = jnp.where(place == target, 0.5, 0.0).astype(BF16)
    for p in range(plan.slots):
        start = SUB + p * plan.fpitch
        rows = []
        for half in range(2):
            cols = []
            for k in range(4):
                t = 4 * half + k
                cols.append(
                    res[t, pl.ds(start, foot, stride=2), :]
                    + res[t, pl.ds(start + 1, foot, stride=2), :]
                )
            rows.append(jnp.concatenate(cols, 1))
        value = dot3(jnp.concatenate(rows, 0), table)
        for ref in msg_refs:
            ref[pl.ds(p * 2 * foot, 2 * foot), :] = value
    lane = iota((SUB, LANES), 1)
    tags = jnp.zeros((SUB, LANES), F32)
    for p in range(plan.slots):
        code = patch_code(plan, count_ref, corner_ref, p)
        tags = jnp.where(lane == p, code.astype(F32), tags)
    packed = {}
    for shift, ref in enumerate(msg_refs, 1):
        at = plan.avg_rows
        ref[pl.ds(at, SUB), :] = tags
        at += SUB
        for low, wanted in enumerate(plan.faces(shift)):
            if wanted:
                if low not in packed:
                    packed[low] = pack_face(coarse_ref, plan, low)
                for j, v in enumerate(packed[low]):
                    ref[pl.ds(at + j * SUB, SUB), :] = v
                at += plan.zrows


def patch_code(plan, count_ref, corner_ref, p):
    spot_x = corner_ref[p, 0] % plan.cx // plan.foot
    spot_y = corner_ref[p, 1] % plan.cy // plan.foot
    spot_z = corner_ref[p, 2] // plan.foot
    code = (spot_x * plan.spots_y + spot_y) * (plan.spots_z * plan.nz) + spot_z
    return jnp.where(p < count_ref[0], code, -1)


def decode(plan, code):
    total_z = plan.spots_z * plan.nz
    spot_z = code % total_z
    spot = code // total_z
    return (
        spot // plan.spots_y * plan.foot,
        spot % plan.spots_y * plan.foot,
        spot_z // plan.spots_z,
        spot_z * plan.foot,
    )


def message_code(plan, ref, p):
    return ref[plan.avg_rows, p].astype(jnp.int32)


def place_patch(plan, ref, base, code, comp):
    me = lax.axis_index("gz")
    x0, y0, home, z0 = decode(plan, code)
    dz = z0 - me * plan.cz

    @pl.when((code >= 0) & (dz >= -plan.foot) & (dz <= plan.cz))
    def _():
        inside = (dz >= 0) & (dz < plan.cz)
        offset = jnp.where(inside, 0, plan.crows)
        lane0 = (dz + plan.cz) % plan.cz
        lane = iota((plan.foot, LANES), 1)
        window = (lane >= lane0) & (lane < lane0 + plan.foot)
        first = offset + plan.row(x0, y0)
        for y in range(plan.foot):
            half, k = divmod(y * plan.foot, LANES)
            v = ref[pl.ds(base + half * plan.foot, plan.foot), :]
            v = pltpu.roll(v, (lane0 + LANES - k) % LANES, 1)
            rows = pl.ds(first + y, plan.foot, stride=plan.pitch)
            comp[rows, :] = jnp.where(window, v, comp[rows, :])


def flags(axis, size):
    index = lax.axis_index(axis)
    return index > 0, index < size - 1


def compose_kernel(plan, count_ref, corner_ref, coarse_ref, own_ref, *rest):
    msg_refs, (comp, yface_lo, yface_hi) = rest[: plan.nz - 1], rest[plan.nz - 1 :]
    cx, cy = plan.cx, plan.cy
    lane = iota((SUB, LANES), 1)
    zero = jnp.zeros((SUB, LANES), F32)
    for base in (0, plan.crows):
        comp[pl.ds(base, SUB + RIM * plan.pitch), :] = jnp.zeros((SUB + RIM * plan.pitch, LANES), F32)
        tail = SUB + RIM * plan.pitch
        comp[pl.ds(base + plan.crows - tail, tail), :] = jnp.zeros((tail, LANES), F32)
        for x in range(cx):
            comp[pl.ds(base + plan.row(x, cy), SUB), :] = zero
    for x in range(cx):
        comp[pl.ds(plan.row(x, 0), cy), :] = coarse_ref[pl.ds(x * cy, cy), :]
    lo_face, hi_face = [zero] * (cy // SUB), [zero] * (cy // SUB)
    has_lo, has_hi = flags("gz", plan.nz)
    for shift, ref in enumerate(msg_refs, 1):
        at = plan.avg_rows + SUB
        for low, wanted in enumerate(plan.faces(shift)):
            if wanted:
                got = [ref[pl.ds(at + j * SUB, SUB), :] for j in range(cy // SUB)]
                if low:
                    hi_face = got
                else:
                    lo_face = got
                at += plan.zrows
    for x in range(cx):
        for j in range(cy // SUB):
            lo = pltpu.roll(lo_face[j], (plan.cz - RIM - 4 * x) % LANES, 1)
            hi = pltpu.roll(hi_face[j], (-4 * x) % LANES, 1)
            v = jnp.where(lane >= plan.cz - RIM, lo, jnp.where(lane < RIM, hi, 0.0))
            comp[pl.ds(plan.crows + plan.row(x, j * SUB), SUB), :] = v
    for p in range(plan.slots):
        code = patch_code(plan, count_ref, corner_ref, p)
        place_patch(plan, own_ref, p * 2 * plan.foot, code, comp)
        for ref in msg_refs:
            place_patch(plan, ref, p * 2 * plan.foot, message_code(plan, ref, p), comp)
    keep = ((lane >= plan.cz - RIM) & has_lo) | ((lane < RIM) & has_hi)
    for x in range(cx):
        for j in range(cy // SUB):
            rows = pl.ds(plan.crows + plan.row(x, j * SUB), SUB)
            comp[rows, :] = jnp.where(keep, comp[rows, :], 0.0)
    for ref, y in ((yface_lo, 0), (yface_hi, cy - RIM)):
        rims = []
        for k in range(RIM):
            ref[pl.ds(k * cx, cx), :] = comp[pl.ds(plan.row(0, y + k), cx, stride=plan.pitch), :]
            v = comp[pl.ds(plan.crows + plan.row(0, y + k), cx, stride=plan.pitch), :]
            rims += [v[j * SUB : (j + 1) * SUB] for j in range(cx // SUB)]
        ref[pl.ds(RIM * cx, SUB), :] = pack_rims(rims)


def pack_rims(rims):
    lane = iota((SUB, LANES), 1)
    acc = jnp.zeros((SUB, LANES), F32)
    for i, v in enumerate(rims):
        acc = jnp.where(lane // SUB == i, pltpu.roll(v, (SUB * i + 4) % LANES, 1), acc)
    return acc


def unpack_rim(packed, i):
    lane = iota((SUB, LANES), 1)
    v = pltpu.roll(packed, (-(SUB * i + 4)) % LANES, 1)
    return jnp.where((lane < RIM) | (lane >= LANES - RIM), v, 0.0)


def put_yface(plan, msg, comp, y):
    for k in range(RIM):
        comp[pl.ds(plan.row(0, y + k), plan.cx, stride=plan.pitch), :] = msg[pl.ds(k * plan.cx, plan.cx), :]
        packed = msg[pl.ds(RIM * plan.cx, SUB), :]
        n = plan.cx // SUB
        rims = jnp.concatenate([unpack_rim(packed, k * n + j) for j in range(n)], 0)
        comp[pl.ds(plan.crows + plan.row(0, y + k), plan.cx, stride=plan.pitch), :] = rims


def xface_kernel(plan, n_y, comp_in, *rest):
    y_refs, (comp, xface_lo, xface_hi) = rest[:n_y], rest[n_y:]
    del comp_in
    put_yfaces(plan, y_refs, comp)
    for ref, x in ((xface_lo, 0), (xface_hi, plan.cx - RIM)):
        first = plan.row(x, 0) - SUB
        ref[pl.ds(0, plan.xrows), :] = comp[pl.ds(first, plan.xrows), :]
        rims = [
            comp[pl.ds(plan.crows + first + i * SUB, SUB), :] for i in range(plan.xrows // SUB)
        ]
        ref[pl.ds(plan.xrows, SUB), :] = pack_rims(rims)


def put_yfaces(plan, y_refs, comp):
    odd = lax.axis_index("gy") % 2
    for i, ref in enumerate(y_refs):
        at_high = (odd == 0) if i == 0 else (odd == 1)
        put_yface(plan, ref, comp, jnp.where(at_high, plan.cy, -RIM))


def put_xfaces(plan, x_refs, comp):
    odd = lax.axis_index("gx") % 2
    for i, ref in enumerate(x_refs):
        at_high = (odd == 0) if i == 0 else (odd == 1)
        first = plan.row(jnp.where(at_high, plan.cx, -RIM), 0) - SUB
        packed = ref[pl.ds(plan.xrows, SUB), :]
        row = iota((SUB, LANES), 0)
        n = plan.xrows // SUB
        for k in range(n):
            for tile in range(2):
                v = ref[pl.ds(k * SUB, SUB), :] if tile == 0 else unpack_rim(packed, k)
                rows = pl.ds(tile * plan.crows + first + k * SUB, SUB)
                if k == 0:
                    v = jnp.where(row >= SUB - RIM, v, comp[rows, :])
                if k == n - 1:
                    v = jnp.where(row < RIM, v, comp[rows, :])
                comp[rows, :] = v


def coarse_kernel(plan, n_x, count_ref, corner_ref, comp_in, *rest):
    x_refs, tag_refs = rest[:n_x], rest[n_x : n_x + plan.nz - 1]
    rest = rest[n_x + plan.nz - 1 :]
    comp, out_ref, e_refs = rest[0], rest[1], rest[2 : 2 + plan.nz]
    second, third = rest[2 + plan.nz :]
    del comp_in
    cx, cy, foot, pitch, crows = plan.cx, plan.cy, plan.foot, plan.pitch, plan.crows
    put_xfaces(plan, x_refs, comp)
    lane, row = iota((SUB, LANES), 1), iota((SUB, LANES), 0)
    z_lo, z_hi = flags("gz", plan.nz)
    y_lo, y_hi = flags("gy", plan.ny)
    x_lo, x_hi = flags("gx", plan.nx)
    zmask = jnp.where(((lane >= LANES - RIM) & z_lo) | ((lane < RIM) & z_hi), 1.0, 0.0)
    ymask = jnp.where(((row >= SUB - RIM) & y_lo) | ((row < RIM) & y_hi), 1.0, 0.0)

    def stencil(ref, at):
        mids, sums = [], []
        for base in (0, crows):
            mids.append(ref[pl.ds(base + at, SUB), :])
            total = ref[pl.ds(base + at - 1, SUB), :] + ref[pl.ds(base + at + 1, SUB), :]
            total += ref[pl.ds(base + at - pitch, SUB), :] + ref[pl.ds(base + at + pitch, SUB), :]
            sums.append(total)
        for i in range(2):
            sums[i] += pltpu.roll(jnp.where(lane == LANES - 1, mids[1 - i], mids[i]), 1, 1)
            sums[i] += pltpu.roll(jnp.where(lane == 0, mids[1 - i], mids[i]), LANES - 1, 1)
        return mids, sums

    def step2(at, edge):
        mids, sums = stencil(comp, at)
        for i in range(2):
            v = 0.165 * mids[i] + 0.0225 * sums[i]
            v = v * ymask if edge else v
            second[pl.ds(i * crows + at, SUB), :] = v * zmask if i else v

    def step3(at, edge):
        mids, sums = stencil(second, at)
        outs = []
        for i in range(2):
            v = 0.1 * mids[i] + 0.15 * (comp[pl.ds(i * crows + at, SUB), :] + sums[i])
            v = v * ymask if edge else v
            v = v * zmask if i else v
            third[pl.ds(i * crows + at, SUB), :] = v
            outs.append(v)
        return outs[0]

    for base in (0, crows):
        head = SUB + pitch
        second[pl.ds(base, head), :] = jnp.zeros((head, LANES), F32)
        second[pl.ds(base + crows - head, head), :] = jnp.zeros((head, LANES), F32)
    step2(pitch, True)

    def plane2(i, carry):
        at = pl.multiple_of(SUB + i * pitch, SUB)
        for j in range(pitch // SUB):
            step2(at + j * SUB, j == cy // SUB)
        return carry

    lax.fori_loop(1, cx + 2 * RIM - 1, plane2, 0)
    for has, x in ((x_lo, 1 - RIM), (x_hi, cx)):

        @pl.when(jnp.logical_not(has))
        def _():
            for base in (0, crows):
                second[pl.ds(base + plan.row(x, -RIM), 2 * pitch), :] = jnp.zeros((2 * pitch, LANES), F32)

    step3(SUB + (RIM - 1) * pitch - SUB, True)

    def plane3(i, carry):
        at = pl.multiple_of(SUB + i * pitch, SUB)
        for j in range(pitch // SUB):
            step3(at + j * SUB, j == cy // SUB)
        return carry

    def plane3_out(i, carry):
        at = pl.multiple_of(SUB + i * pitch, SUB)
        to = pl.multiple_of((i - RIM) * cy, SUB)
        for j in range(pitch // SUB):
            v = step3(at + j * SUB, j == cy // SUB)
            if j < cy // SUB:
                out_ref[pl.ds(to + j * SUB, SUB), :] = v
        return carry

    plane3(RIM - 1, 0)
    lax.fori_loop(RIM, cx + RIM, plane3_out, 0)
    plane3(cx + RIM, 0)
    for has, x in ((x_lo, -1), (x_hi, cx)):

        @pl.when(jnp.logical_not(has))
        def _():
            for base in (0, crows):
                third[pl.ds(base + plan.row(x, -RIM), pitch), :] = jnp.zeros((pitch, LANES), F32)

    me = lax.axis_index("gz")
    for shift in range(plan.nz):
        used = 0
        for p in range(plan.slots):
            if shift == 0:
                code = patch_code(plan, count_ref, corner_ref, p)
            else:
                code = tag_refs[plan.nz - shift - 1][0, p].astype(jnp.int32)
            x0, y0, home, z0 = decode(plan, code)
            here = (code >= 0) & (home == me)

            @pl.when(here)
            def _():
                cut_patch(plan, third, e_refs[shift], jnp.minimum(used, CAP - 1) * foot, x0, y0, z0 % plan.cz)

            used = used + here.astype(jnp.int32)


def cut_patch(plan, third, out, base, x0, y0, z0):
    foot, pitch, crows = plan.foot, plan.pitch, plan.crows
    base = pl.multiple_of(base, SUB)
    lane = iota((foot, LANES), 1)
    off_lo = jnp.where(z0 == 0, crows, 0)
    off_hi = jnp.where(z0 == plan.cz - foot, crows, 0)

    def put(acc, v, source, target, width):
        v = pltpu.roll(v, (target - source + LANES) % LANES, 1)
        return jnp.where((lane >= target) & (lane < target + width), v, acc)

    def column(y, offset=0):
        return third[pl.ds(offset + plan.row(x0, y0 + y), foot, stride=pitch), :]

    zero = jnp.zeros((foot, LANES), F32)
    halves, faces = [zero, zero], zero
    for y in range(foot):
        half, k = divmod(y * foot, LANES)
        halves[half] = put(halves[half], column(y), z0, k, foot)
        faces = put(faces, column(y, off_lo), (z0 + LANES - 1) % LANES, 2 * foot + y, 1)
        faces = put(faces, column(y, off_hi), (z0 + foot) % LANES, 3 * foot + y, 1)
    faces = put(faces, column(-1), z0, 0, foot)
    faces = put(faces, column(foot), z0, foot, foot)
    for i, x in enumerate((-1, foot)):
        v = third[pl.ds(pl.multiple_of(plan.row(x0 + x, y0), SUB), foot), :]
        faces = put(faces, v, z0, (4 + i) * foot, foot)
    out[pl.ds(base, foot), 0:LANES] = halves[0]
    out[pl.ds(base, foot), LANES : 2 * LANES] = halves[1]
    out[pl.ds(base, foot), 2 * LANES : 3 * LANES] = faces


def post_kernel(plan, count_ref, corner_ref, fine_ref, pre_ref, *rest):
    e_refs, (out_ref, base_ref, value, first) = rest[: plan.nz], rest[plan.nz :]
    pe, foot, tiles, slots = plan.pe, plan.foot, plan.tiles, plan.slots
    me = lax.axis_index("gz")
    codes = [patch_code(plan, count_ref, corner_ref, p) for p in range(slots)]
    homes = [decode(plan, c)[2] for c in codes]
    packed = []
    for p in range(slots):
        rank = 0
        for q in range(p):
            rank = rank + ((homes[q] == homes[p]) & (codes[q] >= 0)).astype(jnp.int32)
        rank = jnp.minimum(rank, CAP - 1)
        shift = (me - homes[p] + plan.nz) % plan.nz
        got = jnp.zeros((foot, plan.elanes), F32)
        for s in range(plan.nz):
            rows = pl.ds(pl.multiple_of(rank * foot, SUB), foot)
            got = jnp.where((shift == s) & (codes[p] >= 0), e_refs[s][rows, :], got)
        packed.append(got)
    parents = jnp.concatenate([g[:, 0:LANES] for g in packed] + [g[:, LANES : 2 * LANES] for g in packed], 0)
    faces = jnp.concatenate([g[:, 2 * LANES :] for g in packed], 0)
    source, target = iota((LANES, 4 * LANES), 0), iota((LANES, 4 * LANES), 1)
    place = (target // LANES) * 32 + (target % LANES) // 64 * 16 + target % 32 // 2
    lifted = dot3(parents, jnp.where(place == source, 1.0, 0.0).astype(BF16))
    source, target = iota((LANES, LANES), 0), iota((LANES, LANES), 1)
    z = target % 32
    pick = jnp.where(
        z == 0,
        source - 2 * foot - target // 64,
        jnp.where(z == pe - 1, source - 3 * foot - target // 64, -1),
    )
    pick = jnp.where((source < 2 * foot) | (source >= 4 * foot), -1, pick)
    tables = []
    for t in range(tiles):
        table = pick == 2 * t
        if t == 0:
            table = table | ((target < 32) & (source == z // 2))
        if t == tiles - 1:
            table = table | ((target >= LANES - 32) & (source == foot + z // 2))
        tables.append(jnp.where(table, 1.0, 0.0).astype(BF16))
    for side in (4, 5):
        tables.append(jnp.where(source == side * foot + z // 2, 1.0, 0.0).astype(BF16))
    parts = split3(faces)
    table = jnp.concatenate(tables, 1)
    ghosts = sum(jnp.dot(part, table, preferred_element_type=F32) for part in parts)
    lane1 = iota((1, LANES), 1)
    zero_gaps(value, plan)
    zero_gaps(first, plan)
    for p in range(slots):
        start = SUB + p * plan.fpitch
        for t in range(tiles):
            half, k = divmod(t, 4)
            up = lifted[(half * slots + p) * foot : (half * slots + p + 1) * foot, k * LANES : (k + 1) * LANES]
            ghost = ghosts[p * foot : (p + 1) * foot, t * LANES : (t + 1) * LANES]
            for i in range(2):
                value[t, pl.ds(start + i, foot, stride=2), :] = up
                base_ref[t, pl.ds(start + i, foot, stride=2), :] = ghost
            for i, x in enumerate((0, pe - 1)):
                face = ghosts[p * foot : (p + 1) * foot, (tiles + i) * LANES : (tiles + i + 1) * LANES]
                line = jnp.where(lane1 < 64, face[2 * t : 2 * t + 1], face[2 * t + 1 : 2 * t + 2])
                base_ref[t, pl.ds(start + x, 1), :] = base_ref[t, pl.ds(start + x, 1), :] + line
    chunks = [(p, j) for p in range(slots) for j in range(pe // SUB)]
    for p, j in chunks:
        row = SUB + p * plan.fpitch + j * SUB
        for t in range(tiles):
            rows = pl.ds(row, SUB)
            value[t, rows, :] = value[t, rows, :] + pre_ref[t, rows, :]
            rhs = fine_ref[p, pl.ds(j * SUB, SUB), t * LANES : (t + 1) * LANES]
            base_ref[t, rows, :] = 0.15 * (base_ref[t, rows, :] + rhs)
    for p, j in chunks:
        row = SUB + p * plan.fpitch + j * SUB
        for t in range(tiles):
            mid, total = fine_neighbors(value, t, row, tiles)
            first[t, pl.ds(row, SUB), :] = 0.1 * mid + base_ref[t, pl.ds(row, SUB), :] + 0.15 * total
    for p, j in chunks:
        row = SUB + p * plan.fpitch + j * SUB
        for t in range(tiles):
            mid, total = fine_neighbors(first, t, row, tiles)
            v = 0.1 * mid + base_ref[t, pl.ds(row, SUB), :] + 0.15 * total
            out_ref[p, pl.ds(j * SUB, SUB), t * LANES : (t + 1) * LANES] = jnp.where(codes[p] >= 0, v, 0.0)


VMEM = pl.BlockSpec(memory_space=pltpu.VMEM)
SMEM = pl.BlockSpec(memory_space=pltpu.SMEM)


def call(kernel, name, outs, n_smem, args, scratch=(), aliases=None):
    return pl.pallas_call(
        kernel,
        name=name,
        out_shape=[jax.ShapeDtypeStruct(s, F32) for s in outs],
        in_specs=[SMEM] * n_smem + [VMEM] * (len(args) - n_smem),
        out_specs=[VMEM] * len(outs),
        scratch_shapes=[pltpu.VMEM(s, F32) for s in scratch],
        input_output_aliases=aliases or {},
        compiler_params=pltpu.CompilerParams(vmem_limit_bytes=24 << 20),
    )(*args)


def swap_pairs(axis, size, low, high):
    odd = lax.axis_index(axis) % 2
    got = []
    for start in range(2):
        pairs = [(i, i + 1) for i in range(start, size - 1, 2)]
        if pairs:
            send = jnp.where(odd == start, high, low)
            got.append(lax.ppermute(send, axis, pairs + [(b, a) for a, b in pairs]))
    return got


def per_device(fine_rhs, coarse_rhs, patch_count, patch_corner):
    plan = Plan(fine_rhs.shape, coarse_rhs.shape)
    block = coarse_rhs.reshape(plan.cx * plan.cy, plan.cz)
    fine_shape = (plan.tiles, plan.frows, LANES)
    scalars = (patch_count, patch_corner)
    shifts = range(1, plan.nz)
    pre, *sends = call(
        functools.partial(pre_kernel, plan),
        "pre",
        [fine_shape] + [(plan.msg_rows(s), LANES) for s in shifts],
        2,
        (*scalars, fine_rhs, block),
        scratch=(fine_shape, fine_shape),
    )

    def ring(s):
        return [(i, (i + s) % plan.nz) for i in range(plan.nz)]

    msgs = [lax.ppermute(m, "gz", ring(s)) for s, m in zip(shifts, sends)]
    comp_shape = (2 * plan.crows, LANES)
    yshape = (plan.yrows + SUB, LANES)
    comp, ylow, yhigh = call(
        functools.partial(compose_kernel, plan),
        "compose",
        [comp_shape, yshape, yshape],
        2,
        (*scalars, block, sends[0], *msgs),
    )
    ygot = swap_pairs("gy", plan.ny, ylow, yhigh)
    xshape = (plan.xrows + SUB, LANES)
    comp, xlow, xhigh = call(
        functools.partial(xface_kernel, plan, len(ygot)),
        "xface",
        [comp_shape, xshape, xshape],
        0,
        (comp, *ygot),
        aliases={0: 0},
    )
    xgot = swap_pairs("gx", plan.nx, xlow, xhigh)
    tags = [lax.slice_in_dim(m, plan.avg_rows, plan.avg_rows + SUB, axis=0) for m in msgs]
    eshape = (plan.erows, plan.elanes)
    _, out, *cuts = call(
        functools.partial(coarse_kernel, plan, len(xgot)),
        "coarse",
        [comp_shape, block.shape] + [eshape] * plan.nz,
        2,
        (*scalars, comp, *xgot, *tags),
        scratch=(comp_shape, comp_shape),
        aliases={2: 0},
    )
    back = [cuts[0]] + [lax.ppermute(cuts[s], "gz", ring(s)) for s in shifts]
    (fine,) = call(
        functools.partial(post_kernel, plan),
        "post",
        [fine_rhs.shape],
        2,
        (*scalars, fine_rhs, pre, *back),
        scratch=(fine_shape,) * 3,
    )
    return fine, out.reshape(coarse_rhs.shape)


def solution(mesh):
    return jax.shard_map(
        per_device,
        mesh=mesh,
        in_specs=(
            P(("gx", "gy", "gz"), None, None),
            P("gx", "gy", "gz"),
            P(("gx", "gy", "gz")),
            P(("gx", "gy", "gz"), None),
        ),
        out_specs=(P(("gx", "gy", "gz"), None, None), P("gx", "gy", "gz")),
        check_vma=False,
    )
```

```python
import functools

import jax
import jax.numpy as jnp
from jax import lax
from jax.experimental import pallas as pl
from jax.experimental.pallas import tpu as pltpu
from jax.sharding import PartitionSpec as P

LANES = 128
SUB = 8
RIM = 3
CAP = 2
F32 = jnp.float32
BF16 = jnp.bfloat16


def iota(shape, dim):
    return lax.broadcasted_iota(jnp.int32, shape, dim)


def dot2(x, table):
    high = x.astype(BF16)
    low = (x - high.astype(F32)).astype(BF16)
    both = jnp.concatenate([high, low], 1)
    return jnp.dot(both, jnp.concatenate([table, table], 0), preferred_element_type=F32)


class Plan:
    def __init__(self, fine_shape, coarse_shape):
        self.slots, self.pe, self.merged = fine_shape
        self.foot = self.pe // 2
        self.cx, self.cy, self.cz = coarse_shape
        assert self.cz == LANES and self.merged == self.pe * self.pe
        assert self.foot * self.foot == 2 * LANES and self.pe * 4 == LANES
        self.tiles = self.merged // LANES
        self.fpitch = self.pe + SUB
        self.frows = SUB + self.slots * self.fpitch
        self.nx, self.ny, self.nz = (lax.axis_size(a) for a in ("gx", "gy", "gz"))
        self.pitch = self.cy + SUB
        self.crows = SUB + (self.cx + 2 * RIM) * self.pitch + SUB
        self.spots_y = self.cy // self.foot
        self.spots_z = self.cz // self.foot
        self.avg_rows = self.slots * 2 * self.foot
        self.zrows = self.cy
        assert self.cx * 4 == LANES
        self.erows = CAP * self.foot
        self.elanes = 3 * LANES
        self.win = self.foot + 2
        self.elow = self.win * self.win
        assert self.elow + 2 * self.foot <= self.elanes
        self.yrows = RIM * self.cx
        self.xrows = 3 * self.pitch + SUB
        assert self.xrows == LANES

    def row(self, x, y):
        return SUB + (x + RIM) * self.pitch + y

    def faces(self, shift):
        return shift == 1, shift == self.nz - 1

    def msg_rows(self, shift):
        high, low = self.faces(shift)
        return self.avg_rows + SUB + self.zrows * (int(high) + int(low))


def fine_neighbors(ref, t, row, tiles):
    lane = iota((SUB, LANES), 1)
    mid = ref[t, pl.ds(row, SUB), :]
    total = ref[t, pl.ds(row - 1, SUB), :] + ref[t, pl.ds(row + 1, SUB), :]
    total += jnp.where(lane % 32 == 0, 0.0, pltpu.roll(mid, 1, 1))
    total += jnp.where(lane % 32 == 31, 0.0, pltpu.roll(mid, LANES - 1, 1))
    before = ref[t - 1, pl.ds(row, SUB), :] if t else jnp.zeros_like(mid)
    after = ref[t + 1, pl.ds(row, SUB), :] if t + 1 < tiles else jnp.zeros_like(mid)
    total += pltpu.roll(jnp.where(lane >= LANES - 32, before, mid), 32, 1)
    total += pltpu.roll(jnp.where(lane < 32, after, mid), LANES - 32, 1)
    return mid, total


def zero_gaps(ref, plan):
    gap = jnp.zeros((SUB, LANES), F32)
    for t in range(plan.tiles):
        for p in range(plan.slots + 1):
            row = p * plan.fpitch
            if row + SUB <= plan.frows:
                ref[t, pl.ds(row, SUB), :] = gap


def pack_face(ref, plan, low):
    outs = []
    lane = iota((SUB, LANES), 1)
    start = 0 if low else plan.cz - RIM
    for j in range(plan.cy // SUB):
        acc = jnp.zeros((SUB, LANES), F32)
        for x in range(plan.cx):
            v = pltpu.roll(ref[pl.ds(x * plan.cy + j * SUB, SUB), :], (4 * x - start) % LANES, 1)
            acc = jnp.where(lane // 4 == x, v, acc)
        outs.append(acc)
    return outs


def patch_code(plan, count, corner_ref, p):
    spot_x = corner_ref[p, 0] % plan.cx // plan.foot
    spot_y = corner_ref[p, 1] % plan.cy // plan.foot
    spot_z = corner_ref[p, 2] // plan.foot
    code = (spot_x * plan.spots_y + spot_y) * (plan.spots_z * plan.nz) + spot_z
    return jnp.where(p < count, code, -1)


def pre_kernel(plan, count_ref, corner_hbm, fine_hbm, coarse_hbm, rhs, pre_ref, blk, *rest):
    msg_refs, (fine_ref, res, corner_ref, sems) = rest[:-4], rest[-4:]
    pe, foot, tiles = plan.pe, plan.foot, plan.tiles
    copies = [pltpu.make_async_copy(fine_hbm.at[p], fine_ref.at[p], sems.at[p]) for p in range(plan.slots)]
    at = plan.slots
    copies.append(pltpu.make_async_copy(coarse_hbm, blk, sems.at[at]))
    copies.append(pltpu.make_async_copy(corner_hbm, corner_ref, sems.at[at + 1]))
    for copy in copies:
        copy.start()
    zero_gaps(rhs, plan)
    zero_gaps(pre_ref, plan)
    source, target = iota((4 * LANES, LANES), 0), iota((4 * LANES, LANES), 1)
    place = (source // LANES) * 32 + (source % LANES) // 64 * 16 + source % 32 // 2
    table = jnp.where(place == target, 0.5, 0.0).astype(BF16)
    for p in range(plan.slots):
        copies[p].wait()
        start = SUB + p * plan.fpitch
        for j in range(pe // SUB):
            for t in range(tiles):
                rhs[t, pl.ds(start + j * SUB, SUB), :] = fine_ref[
                    p, pl.ds(j * SUB, SUB), t * LANES : (t + 1) * LANES
                ]
        for j in range(pe // SUB):
            for t in range(tiles):
                mid, total = fine_neighbors(rhs, t, start + j * SUB, tiles)
                pre_ref[t, pl.ds(start + j * SUB, SUB), :] = 0.165 * mid + 0.0225 * total
        for j in range(pe // SUB):
            for t in range(tiles):
                mid, total = fine_neighbors(pre_ref, t, start + j * SUB, tiles)
                rows = pl.ds(start + j * SUB, SUB)
                res[t, rows, :] = rhs[t, rows, :] - (6.0 * mid - total)
        lines = []
        for half in range(2):
            cols = []
            for k in range(4):
                t = 4 * half + k
                cols.append(
                    res[t, pl.ds(start, foot, stride=2), :]
                    + res[t, pl.ds(start + 1, foot, stride=2), :]
                )
            lines.append(jnp.concatenate(cols, 1))
        value = dot2(jnp.concatenate(lines, 0), table)
        for ref in msg_refs:
            ref[pl.ds(p * 2 * foot, 2 * foot), :] = value
    for copy in copies[at:]:
        copy.wait()
    lane = iota((SUB, LANES), 1)
    tags = jnp.zeros((SUB, LANES), F32)
    for p in range(plan.slots):
        code = patch_code(plan, count_ref[0], corner_ref, p)
        tags = jnp.where(lane == p, code.astype(F32), tags)
    packed = {}
    for shift, ref in enumerate(msg_refs, 1):
        at = plan.avg_rows
        ref[pl.ds(at, SUB), :] = tags
        at += SUB
        for low, wanted in enumerate(plan.faces(shift)):
            if wanted:
                if low not in packed:
                    packed[low] = pack_face(blk, plan, low)
                for j, v in enumerate(packed[low]):
                    ref[pl.ds(at + j * SUB, SUB), :] = v
                at += plan.zrows


def decode(plan, code):
    total_z = plan.spots_z * plan.nz
    spot_z = code % total_z
    spot = code // total_z
    return (
        spot // plan.spots_y * plan.foot,
        spot % plan.spots_y * plan.foot,
        spot_z // plan.spots_z,
        spot_z * plan.foot,
    )


def message_code(plan, ref, p):
    return ref[plan.avg_rows, p].astype(jnp.int32)


def place_patch(plan, ref, base, code, comp, block=True, rims=True):
    me = lax.axis_index("gz")
    x0, y0, home, z0 = decode(plan, code)
    dz = z0 - me * plan.cz

    inside = (dz >= 0) & (dz < plan.cz)
    wanted = (code >= 0) & (dz >= -plan.foot) & (dz <= plan.cz)
    if not rims:
        wanted = wanted & inside
    if not block:
        wanted = wanted & jnp.logical_not(inside)

    @pl.when(wanted)
    def _():
        offset = jnp.where(inside, 0, plan.crows)
        lane0 = (dz + plan.cz) % plan.cz
        lane = iota((plan.foot, LANES), 1)
        window = (lane >= lane0) & (lane < lane0 + plan.foot)
        first = offset + plan.row(x0, y0)
        for y in range(plan.foot):
            half, k = divmod(y * plan.foot, LANES)
            v = ref[pl.ds(base + half * plan.foot, plan.foot), :]
            v = pltpu.roll(v, (lane0 + LANES - k) % LANES, 1)
            rows = pl.ds(first + y, plan.foot, stride=plan.pitch)
            comp[rows, :] = jnp.where(window, v, comp[rows, :])


def flags(axis, size):
    index = lax.axis_index(axis)
    return index > 0, index < size - 1


def fixed_kernel(plan, rhs, pre_ref, out, work):
    zero_gaps(work, plan)
    for source, target in ((pre_ref, work), (work, out)):

        def rows8(i, carry):
            p, j = i // (plan.pe // SUB), i % (plan.pe // SUB)
            row = pl.multiple_of(SUB + p * plan.fpitch + j * SUB, SUB)
            for t in range(plan.tiles):
                mid, total = fine_neighbors(source, t, row, plan.tiles)
                rows = pl.ds(row, SUB)
                target[t, rows, :] = 0.1 * mid + 0.15 * (rhs[t, rows, :] + total)
            return carry

        lax.fori_loop(0, plan.slots * (plan.pe // SUB), rows8, 0)


def base_kernel(plan, blk, own_ref, comp):
    cx, cy = plan.cx, plan.cy
    end = SUB + RIM * plan.pitch
    for base in (0, plan.crows):
        comp[pl.ds(base, end), :] = jnp.zeros((end, LANES), F32)
        comp[pl.ds(base + plan.crows - end, end), :] = jnp.zeros((end, LANES), F32)
        for x in range(cx):
            comp[pl.ds(base + plan.row(x, cy), SUB), :] = jnp.zeros((SUB, LANES), F32)
    for x in range(cx):
        comp[pl.ds(plan.row(x, 0), cy), :] = blk[pl.ds(x * cy, cy), :]
        comp[pl.ds(plan.crows + plan.row(x, 0), cy), :] = jnp.zeros((cy, LANES), F32)
    for p in range(plan.slots):
        place_patch(plan, own_ref, p * 2 * plan.foot, message_code(plan, own_ref, p), comp, rims=False)


def compose_kernel(plan, n_y, comp_in, own_ref, *rest):
    msg_refs, (comp, *y_sends) = rest[: plan.nz - 1], rest[plan.nz - 1 :]
    del comp_in
    cx, cy = plan.cx, plan.cy
    lane = iota((SUB, LANES), 1)
    zero = jnp.zeros((SUB, LANES), F32)
    lo_face, hi_face = [zero] * (cy // SUB), [zero] * (cy // SUB)
    has_lo, has_hi = flags("gz", plan.nz)
    for shift, ref in enumerate(msg_refs, 1):
        at = plan.avg_rows + SUB
        for low, wanted in enumerate(plan.faces(shift)):
            if wanted:
                got = [ref[pl.ds(at + j * SUB, SUB), :] for j in range(cy // SUB)]
                if low:
                    hi_face = [jnp.where(has_hi, v, 0.0) for v in got]
                else:
                    lo_face = [jnp.where(has_lo, v, 0.0) for v in got]
                at += plan.zrows
    for x in range(cx):
        for j in range(cy // SUB):
            rows = pl.ds(plan.crows + plan.row(x, j * SUB), SUB)
            lo = pltpu.roll(lo_face[j], (plan.cz - RIM - 4 * x) % LANES, 1)
            hi = pltpu.roll(hi_face[j], (-4 * x) % LANES, 1)
            v = jnp.where(lane < RIM, hi, comp[rows, :])
            comp[rows, :] = jnp.where(lane >= plan.cz - RIM, lo, v)
    for p in range(plan.slots):
        for ref in (own_ref, *msg_refs):
            code = message_code(plan, ref, p)
            place_patch(plan, ref, p * 2 * plan.foot, code, comp, block=ref is not own_ref)
    odd = lax.axis_index("gy") % 2
    for start, ref in enumerate(y_sends):
        y0 = jnp.where(odd == start, cy - RIM, 0)
        rims = []
        for k in range(RIM):
            ref[pl.ds(k * cx, cx), :] = comp[pl.ds(plan.row(0, y0 + k), cx, stride=plan.pitch), :]
            v = comp[pl.ds(plan.crows + plan.row(0, y0 + k), cx, stride=plan.pitch), :]
            rims += [v[j * SUB : (j + 1) * SUB] for j in range(cx // SUB)]
        ref[pl.ds(RIM * cx, SUB), :] = pack_rims(rims)


def pack_rims(rims):
    lane = iota((SUB, LANES), 1)
    acc = jnp.zeros((SUB, LANES), F32)
    for i, v in enumerate(rims):
        acc = jnp.where(lane // SUB == i, pltpu.roll(v, (SUB * i + 4) % LANES, 1), acc)
    return acc


def unpack_rim(packed, i):
    lane = iota((SUB, LANES), 1)
    v = pltpu.roll(packed, (-(SUB * i + 4)) % LANES, 1)
    return jnp.where((lane < RIM) | (lane >= LANES - RIM), v, 0.0)


def put_yface(plan, msg, comp, y):
    for k in range(RIM):
        comp[pl.ds(plan.row(0, y + k), plan.cx, stride=plan.pitch), :] = msg[pl.ds(k * plan.cx, plan.cx), :]
        packed = msg[pl.ds(RIM * plan.cx, SUB), :]
        n = plan.cx // SUB
        rims = jnp.concatenate([unpack_rim(packed, k * n + j) for j in range(n)], 0)
        comp[pl.ds(plan.crows + plan.row(0, y + k), plan.cx, stride=plan.pitch), :] = rims


def xface_kernel(plan, n_y, n_x, comp_in, second_in, *rest):
    y_refs, (comp, second, *x_sends) = rest[:n_y], rest[n_y:]
    del comp_in, second_in, second
    put_yfaces(plan, y_refs, comp)
    odd = lax.axis_index("gx") % 2
    for start, ref in enumerate(x_sends):
        first = pl.multiple_of(plan.row(jnp.where(odd == start, plan.cx - RIM, 0), 0) - SUB, SUB)
        ref[pl.ds(0, plan.xrows), :] = comp[pl.ds(first, plan.xrows), :]
        rims = [
            comp[pl.ds(plan.crows + first + i * SUB, SUB), :] for i in range(plan.xrows // SUB)
        ]
        ref[pl.ds(plan.xrows, SUB), :] = pack_rims(rims)


def put_yfaces(plan, y_refs, comp):
    odd = lax.axis_index("gy") % 2
    for i, ref in enumerate(y_refs):
        at_high = (odd == 0) if i == 0 else (odd == 1)
        put_yface(plan, ref, comp, jnp.where(at_high, plan.cy, -RIM))


def put_xfaces(plan, x_refs, comp):
    odd = lax.axis_index("gx") % 2
    for i, ref in enumerate(x_refs):
        at_high = (odd == 0) if i == 0 else (odd == 1)
        first = plan.row(jnp.where(at_high, plan.cx, -RIM), 0) - SUB
        packed = ref[pl.ds(plan.xrows, SUB), :]
        row = iota((SUB, LANES), 0)
        n = plan.xrows // SUB
        for k in range(n):
            for tile in range(2):
                v = ref[pl.ds(k * SUB, SUB), :] if tile == 0 else unpack_rim(packed, k)
                rows = pl.ds(tile * plan.crows + first + k * SUB, SUB)
                if k == 0:
                    v = jnp.where(row >= SUB - RIM, v, comp[rows, :])
                if k == n - 1:
                    v = jnp.where(row < RIM, v, comp[rows, :])
                comp[rows, :] = v


class Sweeps:
    def __init__(self, plan, comp, second, third=None):
        self.plan, self.comp, self.second, self.third = plan, comp, second, third
        self.lane, row = iota((SUB, LANES), 1), iota((SUB, LANES), 0)
        z_lo, z_hi = flags("gz", plan.nz)
        y_lo, y_hi = flags("gy", plan.ny)
        lane = self.lane
        self.zmask = jnp.where(((lane >= LANES - RIM) & z_lo) | ((lane < RIM) & z_hi), 1.0, 0.0)
        self.ymask = jnp.where(((row >= SUB - RIM) & y_lo) | ((row < RIM) & y_hi), 1.0, 0.0)
        self.main = plan.cy // SUB

    def at(self, x, j):
        return pl.multiple_of(self.plan.row(x, j * SUB), SUB)

    def stencil(self, ref, at):
        crows, pitch, lane = self.plan.crows, self.plan.pitch, self.lane
        mids, sums = [], []
        for base in (0, crows):
            mids.append(ref[pl.ds(base + at, SUB), :])
            total = ref[pl.ds(base + at - 1, SUB), :] + ref[pl.ds(base + at + 1, SUB), :]
            total += ref[pl.ds(base + at - pitch, SUB), :] + ref[pl.ds(base + at + pitch, SUB), :]
            sums.append(total)
        for i in range(2):
            sums[i] += pltpu.roll(jnp.where(lane == LANES - 1, mids[1 - i], mids[i]), 1, 1)
            sums[i] += pltpu.roll(jnp.where(lane == 0, mids[1 - i], mids[i]), LANES - 1, 1)
        return mids, sums

    def step2(self, x, j):
        at = self.at(x, j)
        mids, sums = self.stencil(self.comp, at)
        for i in range(2):
            v = 0.165 * mids[i] + 0.0225 * sums[i]
            v = v * self.ymask if j == self.main else v
            self.second[pl.ds(i * self.plan.crows + at, SUB), :] = v * self.zmask if i else v

    def step3(self, x, j):
        at, crows, lane = self.at(x, j), self.plan.crows, self.lane
        mids, sums = self.stencil(self.second, at)
        outs = []
        for i in range(2):
            v = 0.1 * mids[i] + 0.15 * (self.comp[pl.ds(i * crows + at, SUB), :] + sums[i])
            v = v * self.ymask if j == self.main else v
            outs.append(v * self.zmask if i else v)
        self.third[pl.ds(at, SUB), :] = outs[0]
        self.third[pl.ds(crows + at, SUB), :] = jnp.where(lane >= LANES - 2, outs[1], outs[0])
        self.third[pl.ds(2 * crows + at, SUB), :] = jnp.where(lane < 2, outs[1], outs[0])

    def planes(self, step, first, last, tiles, unroll=2):
        def body(x, carry):
            for j in tiles:
                step(x, j)
            return carry

        lax.fori_loop(first, last + 1, body, 0, unroll=unroll)


def inner_kernel(plan, comp, second):
    s = Sweeps(plan, comp, second)
    s.planes(s.step2, 1, plan.cx - 2, range(1, s.main - 1), unroll=3)


def middle_kernel(plan, comp, second_in, second, third):
    del second_in
    s = Sweeps(plan, comp, second, third)
    s.step2(0, s.main)
    s.planes(s.step2, 1, plan.cx - 2, (0, s.main - 1, s.main))
    s.planes(s.step3, 2, plan.cx - 3, range(s.main + 1))


def put_xfaces(plan, x_refs, comp):
    odd = lax.axis_index("gx") % 2
    for i, ref in enumerate(x_refs):
        at_high = (odd == 0) if i == 0 else (odd == 1)
        first = pl.multiple_of(plan.row(jnp.where(at_high, plan.cx, -RIM), 0) - SUB, SUB)
        packed = ref[pl.ds(plan.xrows, SUB), :]
        row = iota((SUB, LANES), 0)
        n = plan.xrows // SUB
        for k in range(n):
            for tile in range(2):
                v = ref[pl.ds(k * SUB, SUB), :] if tile == 0 else unpack_rim(packed, k)
                rows = pl.ds(tile * plan.crows + first + k * SUB, SUB)
                if k == 0:
                    v = jnp.where(row >= SUB - RIM, v, comp[rows, :])
                if k == n - 1:
                    v = jnp.where(row < RIM, v, comp[rows, :])
                comp[rows, :] = v


def edge_kernel(plan, n_x, comp_in, second_in, third_in, own_ref, *rest):
    x_refs, msg_refs = rest[:n_x], rest[n_x : n_x + plan.nz - 1]
    comp, second, third, *e_refs = rest[n_x + plan.nz - 1 :]
    del comp_in, second_in, third_in
    cx, pitch, crows = plan.cx, plan.pitch, plan.crows
    put_xfaces(plan, x_refs, comp)
    s = Sweeps(plan, comp, second, third)
    x_lo, x_hi = flags("gx", plan.nx)
    every = range(s.main + 1)
    s.step2(-RIM, s.main)
    s.step2(cx - 2, s.main)
    for x in (-2, -1, 0, cx - 1, cx, cx + 1):
        for j in every:
            s.step2(x, j)
    for has, x in ((x_lo, 1 - RIM), (x_hi, cx)):

        @pl.when(jnp.logical_not(has))
        def _():
            for base in (0, crows):
                second[pl.ds(base + plan.row(x, -RIM), 2 * pitch), :] = jnp.zeros((2 * pitch, LANES), F32)

    s.step3(1 - RIM, s.main)
    s.step3(cx - 3, s.main)
    for x in (-1, 0, 1, cx - 2, cx - 1, cx):
        for j in every:
            s.step3(x, j)
    for has, x in ((x_lo, -1), (x_hi, cx)):

        @pl.when(jnp.logical_not(has))
        def _():
            for base in (0, crows, 2 * crows):
                third[pl.ds(base + plan.row(x, -RIM), pitch), :] = jnp.zeros((pitch, LANES), F32)

    me = lax.axis_index("gz")
    for shift in range(plan.nz):
        tags = msg_refs[plan.nz - shift - 1] if shift else own_ref
        used = 0
        for p in range(plan.slots):
            code = message_code(plan, tags, p)
            x0, y0, home, z0 = decode(plan, code)
            here = (code >= 0) & (home == me)

            @pl.when(here)
            def _():
                cut_patch(
                    plan, third, e_refs[shift], jnp.minimum(used, CAP - 1) * plan.foot, x0, y0, z0 % plan.cz
                )

            used = used + here.astype(jnp.int32)


def cut_patch(plan, third, out, base, x0, y0, z0):
    foot, pitch, crows, win = plan.foot, plan.pitch, plan.crows, plan.win
    base = pl.multiple_of(base, SUB)
    lane = iota((foot, LANES), 1)
    offset = jnp.where(z0 == 0, crows, jnp.where(z0 == plan.cz - foot, 2 * crows, 0))
    outs = [jnp.zeros((foot, LANES), F32) for _ in range(plan.elanes // LANES)]

    def put(v, source, target, width):
        tile, k = divmod(target, LANES)
        v = pltpu.roll(v, (k - source + 2 * LANES) % LANES, 1)
        outs[tile] = jnp.where((lane >= k) & (lane < k + width), v, outs[tile])
        if k + width > LANES:
            outs[tile + 1] = jnp.where(lane < k + width - LANES, v, outs[tile + 1])

    for y in range(-1, foot + 1):
        v = third[pl.ds(offset + plan.row(x0, y0 + y), foot, stride=pitch), :]
        put(v, z0 - 1, (y + 1) * win, win)
    for i, x in enumerate((-1, foot)):
        v = third[pl.ds(pl.multiple_of(plan.row(x0 + x, y0), SUB), foot), :]
        put(v, z0, plan.elow + i * foot, foot)
    for i, v in enumerate(outs):
        out[pl.ds(base, foot), i * LANES : (i + 1) * LANES] = v


def emit_kernel(plan, third, out_ref):
    for x in range(plan.cx):
        out_ref[pl.ds(x * plan.cy, plan.cy), :] = third[pl.ds(plan.row(x, 0), plan.cy), :]


def post_kernel(plan, own_ref, fixed, *rest):
    e_refs, (out_hbm, out_ref, ups, first, ghost, yghost, sems) = rest[: plan.nz], rest[plan.nz :]
    pe, foot, tiles, slots, win = plan.pe, plan.foot, plan.tiles, plan.slots, plan.win
    me = lax.axis_index("gz")
    codes = [message_code(plan, own_ref, p) for p in range(slots)]
    homes = [decode(plan, c)[2] for c in codes]
    cuts = []
    for p in range(slots):
        rank = 0
        for q in range(p):
            rank = rank + ((homes[q] == homes[p]) & (codes[q] >= 0)).astype(jnp.int32)
        rank = jnp.minimum(rank, CAP - 1)
        shift = (me - homes[p] + plan.nz) % plan.nz
        got = [jnp.zeros((foot, LANES), F32)] * 3
        for s in range(plan.nz):
            rows = pl.ds(pl.multiple_of(rank * foot, SUB), foot)
            take = (shift == s) & (codes[p] >= 0)
            got = [
                jnp.where(take, e_refs[s][rows, i * LANES : (i + 1) * LANES], g)
                for i, g in enumerate(got)
            ]
        cuts.append(got)
    lane16 = iota((foot, LANES), 1)

    def lanes_from(got, at):
        tile, k = divmod(at, LANES)
        v = pltpu.roll(got[tile], (LANES - k) % LANES, 1)
        if k and tile + 1 < len(got):
            v = jnp.where(lane16 < LANES - k, v, pltpu.roll(got[tile + 1], LANES - k, 1))
        return v

    source, target = iota((LANES, LANES), 0), iota((LANES, LANES), 1)
    q, fz = target // 32, target % 32
    a = 1 + q // 2
    own_lane = a * win + fz // 2 + 1
    side_y = own_lane + jnp.where(q % 2 == 0, -win, win)
    side_z = own_lane + jnp.where(fz % 2 == 0, -1, 1)
    up = jnp.where(source == own_lane, 1.0, 0.0)
    around = 3.0 * up + jnp.where(source == side_y, 1.0, 0.0) + jnp.where(source == side_z, 1.0, 0.0)
    zface = jnp.where((source == side_z) & ((fz == 0) | (fz == pe - 1)), 1.0, 0.0)
    table = jnp.concatenate([up, around, zface], 1).astype(BF16)
    work = [lanes_from(got, 2 * t * win) for got in cuts for t in range(tiles)]
    spread = dot2(jnp.concatenate(work, 0), table)
    low_y = jnp.where((target >= LANES - 32) & (source == fz // 2 + 1), 1.0, 0.0)
    high_y = jnp.where((target < 32) & (source == 3 * win + fz // 2 + 1), 1.0, 0.0)
    ends = [lanes_from(got, 0) for got in cuts], [lanes_from(got, 2 * (tiles - 1) * win) for got in cuts]
    lows = dot2(jnp.concatenate(ends[0], 0), low_y.astype(BF16))
    highs = dot2(jnp.concatenate(ends[1], 0), high_y.astype(BF16))
    xsel = jnp.where((source == fz // 2), 1.0, 0.0).astype(BF16)
    xfaces = dot2(
        jnp.concatenate([lanes_from(got, plan.elow + i * foot) for got in cuts for i in range(2)], 0), xsel
    )
    lane1 = iota((1, LANES), 1)
    copies = [pltpu.make_async_copy(out_ref.at[p], out_hbm.at[p], sems.at[p]) for p in range(slots)]
    lane = iota((SUB, LANES), 1)
    for p in range(slots):
        start = SUB + p * plan.fpitch
        ustart = SUB + p * (foot + SUB)
        for i, (v, k) in enumerate(((lows, 0), (highs, 1))):
            line = v[p * foot : (p + 1) * foot]
            for parity in range(2):
                yghost[k, pl.ds(start + parity, foot, stride=2), :] = line
        for t in range(tiles):
            block = spread[(p * tiles + t) * foot : (p * tiles + t + 1) * foot]
            mine = block[:, 0:LANES]
            ups[t, pl.ds(ustart, foot), :] = mine
            for i, (urow, row) in enumerate(((ustart - 1, start - 1), (ustart + foot, start + pe))):
                face = xfaces[(2 * p + i) * foot : (2 * p + i + 1) * foot]
                line = jnp.where(lane1 < 64, face[2 * t : 2 * t + 1], face[2 * t + 1 : 2 * t + 2])
                ups[t, pl.ds(urow, 1), :] = line
                first[t, pl.ds(row, 1), :] = line
            base = 0.1 * mine + 0.15 * block[:, LANES : 2 * LANES]
            for parity, shift in enumerate((-1, 1)):
                value = base + 0.15 * ups[t, pl.ds(ustart + shift, foot), :]
                first[t, pl.ds(start + parity, foot, stride=2), :] = value
                ghost[t, pl.ds(start + parity, foot, stride=2), :] = block[:, 2 * LANES :]
        alive = codes[p] >= 0
        for j in range(pe // SUB):
            rows = pl.ds(start + j * SUB, SUB)
            for t in range(tiles):
                mid = first[t, rows, :]
                side = ghost[t, rows, :]
                total = first[t, pl.ds(start + j * SUB - 1, SUB), :] + first[t, pl.ds(start + j * SUB + 1, SUB), :]
                total += jnp.where(lane % 32 == 0, side, pltpu.roll(mid, 1, 1))
                total += jnp.where(lane % 32 == 31, side, pltpu.roll(mid, LANES - 1, 1))
                before = first[t - 1, rows, :] if t else yghost[0, rows, :]
                after = first[t + 1, rows, :] if t + 1 < tiles else yghost[1, rows, :]
                total += pltpu.roll(jnp.where(lane >= LANES - 32, before, mid), 32, 1)
                total += pltpu.roll(jnp.where(lane < 32, after, mid), LANES - 32, 1)
                value = fixed[t, rows, :] + (0.1 * mid + 0.15 * total)
                out_ref[p, pl.ds(j * SUB, SUB), t * LANES : (t + 1) * LANES] = jnp.where(alive, value, 0.0)
        copies[p].start()
    for copy in copies:
        copy.wait()


VMEM = pl.BlockSpec(memory_space=pltpu.VMEM)
HBM = pl.BlockSpec(memory_space=pltpu.HBM)
SMEM = pl.BlockSpec(memory_space=pltpu.SMEM)


def call(kernel, name, outs, args, scratch=(), aliases=None, smem=0, hbm_in=0, hbm_out=0, sems=0, cost=0):
    spaces = [s if isinstance(s, pl.MemoryRef) else pltpu.VMEM(s, F32) for s in scratch]
    return pl.pallas_call(
        kernel,
        name=name,
        out_shape=[jax.ShapeDtypeStruct(s, F32) for s in outs],
        in_specs=[SMEM] * smem + [HBM] * hbm_in + [VMEM] * (len(args) - hbm_in - smem),
        out_specs=[HBM] * hbm_out + [VMEM] * (len(outs) - hbm_out),
        scratch_shapes=spaces + ([pltpu.SemaphoreType.DMA((sems,))] if sems else []),
        input_output_aliases=aliases or {},
        cost_estimate=pl.CostEstimate(flops=cost, bytes_accessed=cost, transcendentals=0) if cost else None,
        compiler_params=pltpu.CompilerParams(vmem_limit_bytes=16 << 20),
    )(*args)


def swap_pairs(axis, size, sends):
    got = []
    for start, send in enumerate(sends):
        pairs = [(i, i + 1) for i in range(start, size - 1, 2)]
        got.append(lax.ppermute(send, axis, pairs + [(b, a) for a, b in pairs]))
    return got


def per_device(fine_rhs, coarse_rhs, patch_count, patch_corner):
    plan = Plan(fine_rhs.shape, coarse_rhs.shape)
    fine_shape = (plan.tiles, plan.frows, LANES)
    block_shape = (plan.cx * plan.cy, plan.cz)
    comp_shape = (2 * plan.crows, LANES)
    third_shape = (3 * plan.crows, LANES)
    yshape, xshape = (plan.yrows + SUB, LANES), (plan.xrows + SUB, LANES)
    eshape = (plan.erows, plan.elanes)
    n_y, n_x = min(plan.ny - 1, 2), min(plan.nx - 1, 2)
    shifts = range(1, plan.nz)
    bind = functools.partial
    rhs, pre, block, *sends = call(
        bind(pre_kernel, plan),
        "pre",
        [fine_shape, fine_shape, block_shape] + [(plan.msg_rows(s), LANES) for s in shifts],
        [patch_count]
        + [
            pltpu.with_memory_space_constraint(a, pltpu.HBM)
            for a in (patch_corner, fine_rhs, coarse_rhs.reshape(block_shape))
        ],
        scratch=(fine_rhs.shape, fine_shape, pltpu.VMEM(patch_corner.shape, jnp.int32)),
        smem=1,
        hbm_in=3,
        sems=plan.slots + 2,
    )
    own = sends[0]

    def ring(s):
        return [(i, (i + s) % plan.nz) for i in range(plan.nz)]

    msgs = [lax.ppermute(m, "gz", ring(s)) for s, m in zip(shifts, sends)]
    (comp,) = call(bind(base_kernel, plan), "base", [comp_shape], (block, own), cost=4 << 20)
    (fixed,) = call(
        bind(fixed_kernel, plan), "fixed", [fine_shape], (rhs, pre), scratch=(fine_shape,), cost=4 << 20
    )
    comp, *ysends = call(
        bind(compose_kernel, plan, n_y), "compose", [comp_shape] + [yshape] * n_y, (comp, own, *msgs), aliases={0: 0}
    )
    ygot = swap_pairs("gy", plan.ny, ysends)
    (second,) = call(bind(inner_kernel, plan), "inner", [comp_shape], (comp,), cost=4 << 20)
    comp, second, *xsends = call(
        bind(xface_kernel, plan, n_y, n_x),
        "xface",
        [comp_shape, comp_shape] + [xshape] * n_x,
        (comp, second, *ygot),
        aliases={0: 0, 1: 1},
    )
    xgot = swap_pairs("gx", plan.nx, xsends)
    second, third = call(
        bind(middle_kernel, plan), "middle", [comp_shape, third_shape], (comp, second), aliases={1: 0}, cost=8 << 20
    )
    _, _, third, *cuts = call(
        bind(edge_kernel, plan, n_x),
        "edge",
        [comp_shape, comp_shape, third_shape] + [eshape] * plan.nz,
        (comp, second, third, own, *xgot, *msgs),
        aliases={0: 0, 1: 1, 2: 2},
    )
    back = [cuts[0]] + [lax.ppermute(cuts[s], "gz", ring(s)) for s in shifts]
    (out,) = call(bind(emit_kernel, plan), "emit", [block_shape], (third,), cost=2 << 20)
    (fine,) = call(
        bind(post_kernel, plan),
        "post",
        [fine_rhs.shape],
        (own, fixed, *back),
        scratch=(
            fine_rhs.shape,
            (plan.tiles, SUB + plan.slots * (plan.foot + SUB), LANES),
            fine_shape,
            fine_shape,
            (2, plan.frows, LANES),
        ),
        hbm_out=1,
        sems=plan.slots,
    )
    return fine, out.reshape(coarse_rhs.shape)


def solution(mesh):
    return jax.shard_map(
        per_device,
        mesh=mesh,
        in_specs=(
            P(("gx", "gy", "gz"), None, None),
            P("gx", "gy", "gz"),
            P(("gx", "gy", "gz")),
            P(("gx", "gy", "gz"), None),
        ),
        out_specs=(P(("gx", "gy", "gz"), None, None), P("gx", "gy", "gz")),
        check_vma=False,
    )
```

```python
import functools

import jax
import jax.numpy as jnp
from jax import lax
from jax.experimental import pallas as pl
from jax.experimental.pallas import tpu as pltpu
from jax.sharding import PartitionSpec as P


LANES = 128
SUB = 8
RIM = 3
CAP = 2
F32 = jnp.float32
BF16 = jnp.bfloat16


def iota(shape, dim):
    return lax.broadcasted_iota(jnp.int32, shape, dim)


def dot2(x, table):
    high = x.astype(BF16)
    low = (x - high.astype(F32)).astype(BF16)
    both = jnp.concatenate([high, low], 1)
    return jnp.dot(both, jnp.concatenate([table, table], 0), preferred_element_type=F32)


class Plan:
    def __init__(self, fine_shape, coarse_shape):
        self.slots, self.pe, self.merged = fine_shape
        self.foot = self.pe // 2
        self.cx, self.cy, self.cz = coarse_shape
        assert self.cz == LANES and self.merged == self.pe * self.pe
        assert self.foot * self.foot == 2 * LANES and self.pe * 4 == LANES
        self.tiles = self.merged // LANES
        self.fpitch = self.pe + SUB
        self.frows = SUB + self.slots * self.fpitch
        self.nx, self.ny, self.nz = (lax.axis_size(a) for a in ("gx", "gy", "gz"))
        self.pitch = self.cy + SUB
        self.crows = SUB + (self.cx + 2 * RIM) * self.pitch + SUB
        self.spots_y = self.cy // self.foot
        self.spots_z = self.cz // self.foot
        self.avg_rows = self.slots * 2 * self.foot
        self.zrows = self.cy
        assert self.cx * 4 == LANES
        self.erows = CAP * self.foot
        self.elanes = 3 * LANES
        self.win = self.foot + 2
        self.elow = self.win * self.win
        assert self.elow + 2 * self.foot <= self.elanes
        self.yrows = RIM * self.cx
        self.xrows = 3 * self.pitch + SUB
        assert self.xrows == LANES

    def row(self, x, y):
        return SUB + (x + RIM) * self.pitch + y

    def faces(self, shift):
        return shift == 1, shift == self.nz - 1

    def msg_rows(self, shift):
        high, low = self.faces(shift)
        return self.avg_rows + SUB + self.zrows * (int(high) + int(low))


def fine_neighbors(ref, t, row, tiles):
    lane = iota((SUB, LANES), 1)
    mid = ref[t, pl.ds(row, SUB), :]
    total = ref[t, pl.ds(row - 1, SUB), :] + ref[t, pl.ds(row + 1, SUB), :]
    total += jnp.where(lane % 32 == 0, 0.0, pltpu.roll(mid, 1, 1))
    total += jnp.where(lane % 32 == 31, 0.0, pltpu.roll(mid, LANES - 1, 1))
    before = ref[t - 1, pl.ds(row, SUB), :] if t else jnp.zeros_like(mid)
    after = ref[t + 1, pl.ds(row, SUB), :] if t + 1 < tiles else jnp.zeros_like(mid)
    total += pltpu.roll(jnp.where(lane >= LANES - 32, before, mid), 32, 1)
    total += pltpu.roll(jnp.where(lane < 32, after, mid), LANES - 32, 1)
    return mid, total


def zero_gaps(ref, plan):
    gap = jnp.zeros((SUB, LANES), F32)
    for t in range(plan.tiles):
        for p in range(plan.slots + 1):
            row = p * plan.fpitch
            if row + SUB <= plan.frows:
                ref[t, pl.ds(row, SUB), :] = gap


def pack_faces(ref, plan, starts):
    lane = iota((SUB, LANES), 1)
    count = plan.cy // SUB
    packed = [[jnp.zeros((SUB, LANES), F32)] * count for _ in starts]
    for x in range(plan.cx):
        mask = lane // 4 == x
        for j in range(count):
            v = ref[pl.ds(x * plan.cy + j * SUB, SUB), :]
            for face, start in zip(packed, starts):
                face[j] = jnp.where(mask, pltpu.roll(v, (4 * x - start) % LANES, 1), face[j])
    return packed


def patch_code(plan, count, corner_ref, p):
    spot_x = corner_ref[p, 0] % plan.cx // plan.foot
    spot_y = corner_ref[p, 1] % plan.cy // plan.foot
    spot_z = corner_ref[p, 2] // plan.foot
    code = (spot_x * plan.spots_y + spot_y) * (plan.spots_z * plan.nz) + spot_z
    return jnp.where(p < count, code, -1)


def pre_kernel(plan, count_ref, corner_hbm, fine_hbm, coarse_hbm, rhs, pre_ref, blk, *rest):
    msg_refs, (res, corner_ref, sems) = rest[:-3], rest[-3:]
    pe, foot, tiles, slots = plan.pe, plan.foot, plan.tiles, plan.slots
    copies = [
        pltpu.make_async_copy(
            fine_hbm.at[p, :, pl.ds(t * LANES, LANES)],
            rhs.at[t, pl.ds(SUB + p * plan.fpitch, pe), :],
            sems.at[p * tiles + t],
        )
        for p in range(slots)
        for t in range(tiles)
    ]
    at = slots * tiles
    copies.append(pltpu.make_async_copy(corner_hbm, corner_ref, sems.at[at]))
    copies.append(pltpu.make_async_copy(coarse_hbm, blk, sems.at[at + 1]))
    for copy in copies:
        copy.start()
    zero_gaps(rhs, plan)
    zero_gaps(pre_ref, plan)
    source, target = iota((4 * LANES, LANES), 0), iota((4 * LANES, LANES), 1)
    place = (source // LANES) * 32 + (source % LANES) // 64 * 16 + source % 32 // 2
    table = jnp.where(place == target, 0.5, 0.0).astype(BF16)
    for p in range(slots):
        for copy in copies[p * tiles : (p + 1) * tiles]:
            copy.wait()
        start = SUB + p * plan.fpitch
        for j in range(pe // SUB):
            rows = pl.ds(start + j * SUB, SUB)
            values = []
            for t in range(tiles):
                mid, total = fine_neighbors(rhs, t, start + j * SUB, tiles)
                values.append(0.165 * mid + 0.0225 * total)
            for t, v in enumerate(values):
                pre_ref[t, rows, :] = v
        for j in range(pe // SUB):
            rows = pl.ds(start + j * SUB, SUB)
            values = []
            for t in range(tiles):
                mid, total = fine_neighbors(pre_ref, t, start + j * SUB, tiles)
                values.append(rhs[t, rows, :] - (6.0 * mid - total))
            for t, v in enumerate(values):
                res[t, rows, :] = v
        lines = []
        for half in range(2):
            cols = []
            for k in range(4):
                t = 4 * half + k
                cols.append(
                    res[t, pl.ds(start, foot, stride=2), :]
                    + res[t, pl.ds(start + 1, foot, stride=2), :]
                )
            lines.append(jnp.concatenate(cols, 1))
        value = dot2(jnp.concatenate(lines, 0), table)
        for ref in msg_refs:
            ref[pl.ds(p * 2 * foot, 2 * foot), :] = value
    for copy in copies[at:]:
        copy.wait()
    lane = iota((SUB, LANES), 1)
    tags = jnp.zeros((SUB, LANES), F32)
    for p in range(slots):
        code = patch_code(plan, count_ref[0], corner_ref, p)
        tags = jnp.where(lane == p, code.astype(F32), tags)
    high, low = pack_faces(blk, plan, (plan.cz - RIM, 0))
    for shift, ref in enumerate(msg_refs, 1):
        at = plan.avg_rows
        ref[pl.ds(at, SUB), :] = tags
        at += SUB
        for face, wanted in zip((high, low), plan.faces(shift)):
            if wanted:
                for j, v in enumerate(face):
                    ref[pl.ds(at + j * SUB, SUB), :] = v
                at += plan.zrows


def decode(plan, code):
    total_z = plan.spots_z * plan.nz
    spot_z = code % total_z
    spot = code // total_z
    return (
        spot // plan.spots_y * plan.foot,
        spot % plan.spots_y * plan.foot,
        spot_z // plan.spots_z,
        spot_z * plan.foot,
    )


def message_code(plan, ref, p):
    return ref[plan.avg_rows, p].astype(jnp.int32)


def place_patch(plan, ref, base, code, comp, block=True, rims=True):
    me = lax.axis_index("gz")
    x0, y0, _, z0 = decode(plan, code)
    dz = z0 - me * plan.cz

    inside = (dz >= 0) & (dz < plan.cz)
    wanted = (code >= 0) & (dz >= -plan.foot) & (dz <= plan.cz)
    if not rims:
        wanted = wanted & inside
    if not block:
        wanted = wanted & jnp.logical_not(inside)

    @pl.when(wanted)
    def _():
        offset = jnp.where(inside, 0, plan.crows)
        lane0 = (dz + plan.cz) % plan.cz
        lane = iota((plan.foot, LANES), 1)
        window = (lane >= lane0) & (lane < lane0 + plan.foot)
        first = offset + plan.row(x0, y0)
        halves = [ref[pl.ds(base + half * plan.foot, plan.foot), :] for half in range(2)]
        values = []
        for y in range(plan.foot):
            half, k = divmod(y * plan.foot, LANES)
            v = pltpu.roll(halves[half], (lane0 + LANES - k) % LANES, 1)
            values.append(jnp.where(window, v, comp[pl.ds(first + y, plan.foot, stride=plan.pitch), :]))
        for y, v in enumerate(values):
            comp[pl.ds(first + y, plan.foot, stride=plan.pitch), :] = v


def flags(axis, size):
    index = lax.axis_index(axis)
    return index > 0, index < size - 1


def fixed_step(plan, rhs, source, target):
    def rows8(i, carry):
        p, j = i // (plan.pe // SUB), i % (plan.pe // SUB)
        row = pl.multiple_of(SUB + p * plan.fpitch + j * SUB, SUB)
        rows = pl.ds(row, SUB)
        values = []
        for t in range(plan.tiles):
            mid, total = fine_neighbors(source, t, row, plan.tiles)
            values.append(0.1 * mid + 0.15 * (rhs[t, rows, :] + total))
        for t, v in enumerate(values):
            target[t, rows, :] = v
        return carry

    lax.fori_loop(0, plan.slots * (plan.pe // SUB), rows8, 0)


def late_step(plan, rhs, source, after, target):
    del after
    fixed_step(plan, rhs, source, target)


def base_kernel(plan, blk, own_ref, rhs, pre_ref, comp, fixed):
    zero_gaps(fixed, plan)
    fixed_step(plan, rhs, pre_ref, fixed)
    cx, cy = plan.cx, plan.cy
    end = SUB + RIM * plan.pitch
    for base in (0, plan.crows):
        comp[pl.ds(base, end), :] = jnp.zeros((end, LANES), F32)
        comp[pl.ds(base + plan.crows - end, end), :] = jnp.zeros((end, LANES), F32)
        for x in range(cx):
            comp[pl.ds(base + plan.row(x, cy), SUB), :] = jnp.zeros((SUB, LANES), F32)
    for x in range(cx):
        comp[pl.ds(plan.row(x, 0), cy), :] = blk[pl.ds(x * cy, cy), :]
    for p in range(plan.slots):
        place_patch(plan, own_ref, p * 2 * plan.foot, message_code(plan, own_ref, p), comp, rims=False)


def compose_kernel(plan, comp_in, own_ref, *rest):
    msg_refs, (comp, *y_sends) = rest[: plan.nz - 1], rest[plan.nz - 1 :]
    del comp_in
    cx, cy = plan.cx, plan.cy
    lane = iota((SUB, LANES), 1)
    zero = jnp.zeros((SUB, LANES), F32)
    lo_face, hi_face = [zero] * (cy // SUB), [zero] * (cy // SUB)
    has_lo, has_hi = flags("gz", plan.nz)
    for shift, ref in enumerate(msg_refs, 1):
        at = plan.avg_rows + SUB
        for low, wanted in enumerate(plan.faces(shift)):
            if wanted:
                got = [ref[pl.ds(at + j * SUB, SUB), :] for j in range(cy // SUB)]
                if low:
                    hi_face = [jnp.where(has_hi, v, 0.0) for v in got]
                else:
                    lo_face = [jnp.where(has_lo, v, 0.0) for v in got]
                at += plan.zrows
    for x in range(cx):
        for j in range(cy // SUB):
            rows = pl.ds(plan.crows + plan.row(x, j * SUB), SUB)
            lo = pltpu.roll(lo_face[j], (plan.cz - RIM - 4 * x) % LANES, 1)
            hi = pltpu.roll(hi_face[j], (-4 * x) % LANES, 1)
            comp[rows, :] = jnp.where(lane >= plan.cz - RIM, lo, jnp.where(lane < RIM, hi, 0.0))
    for p in range(plan.slots):
        for ref in (own_ref, *msg_refs):
            code = message_code(plan, ref, p)
            place_patch(plan, ref, p * 2 * plan.foot, code, comp, block=ref is not own_ref)
    odd = lax.axis_index("gy") % 2
    for start, ref in enumerate(y_sends):
        y0 = jnp.where(odd == start, cy - RIM, 0)
        rims = []
        for k in range(RIM):
            ref[pl.ds(k * cx, cx), :] = comp[pl.ds(plan.row(0, y0 + k), cx, stride=plan.pitch), :]
            v = comp[pl.ds(plan.crows + plan.row(0, y0 + k), cx, stride=plan.pitch), :]
            rims += [v[j * SUB : (j + 1) * SUB] for j in range(cx // SUB)]
        ref[pl.ds(RIM * cx, SUB), :] = pack_rims(rims)


def pack_rims(rims):
    lane = iota((SUB, LANES), 1)
    acc = jnp.zeros((SUB, LANES), F32)
    for i, v in enumerate(rims):
        acc = jnp.where(lane // SUB == i, pltpu.roll(v, (SUB * i + 4) % LANES, 1), acc)
    return acc


def unpack_rim(packed, i):
    lane = iota((SUB, LANES), 1)
    v = pltpu.roll(packed, (-(SUB * i + 4)) % LANES, 1)
    return jnp.where((lane < RIM) | (lane >= LANES - RIM), v, 0.0)


def put_yface(plan, msg, comp, y):
    for k in range(RIM):
        comp[pl.ds(plan.row(0, y + k), plan.cx, stride=plan.pitch), :] = msg[pl.ds(k * plan.cx, plan.cx), :]
        packed = msg[pl.ds(RIM * plan.cx, SUB), :]
        n = plan.cx // SUB
        rims = jnp.concatenate([unpack_rim(packed, k * n + j) for j in range(n)], 0)
        comp[pl.ds(plan.crows + plan.row(0, y + k), plan.cx, stride=plan.pitch), :] = rims


def pack_xface(plan, comp, ref, start):
    at_high = lax.axis_index("gx") % 2 == start
    first = pl.multiple_of(plan.row(jnp.where(at_high, plan.cx - RIM, 0), 0) - SUB, SUB)
    rims = [comp[pl.ds(plan.crows + first + i * SUB, SUB), :] for i in range(plan.xrows // SUB)]
    ref[pl.ds(0, plan.xrows), :] = comp[pl.ds(first, plan.xrows), :]
    ref[pl.ds(plan.xrows, SUB), :] = pack_rims(rims)


def xface_kernel(plan, n_y, comp_in, second_in, *rest):
    y_refs, (comp, second, *x_sends) = rest[:n_y], rest[n_y:]
    del comp_in, second_in, second
    put_yfaces(plan, y_refs, comp)
    for i, ref in enumerate(x_sends):
        pack_xface(plan, comp, ref, i)


def put_yfaces(plan, y_refs, comp):
    odd = lax.axis_index("gy") % 2
    for i, ref in enumerate(y_refs):
        at_high = (odd == 0) if i == 0 else (odd == 1)
        put_yface(plan, ref, comp, jnp.where(at_high, plan.cy, -RIM))


class Sweeps:
    def __init__(self, plan, comp, second, third=None):
        self.plan, self.comp, self.second, self.third = plan, comp, second, third
        self.lane, row = iota((SUB, LANES), 1), iota((SUB, LANES), 0)
        z_lo, z_hi = flags("gz", plan.nz)
        y_lo, y_hi = flags("gy", plan.ny)
        lane = self.lane
        self.zmask = jnp.where(((lane >= LANES - RIM) & z_lo) | ((lane < RIM) & z_hi), 1.0, 0.0)
        self.ymask = jnp.where(((row >= SUB - RIM) & y_lo) | ((row < RIM) & y_hi), 1.0, 0.0)
        self.main = plan.cy // SUB

    def at(self, x, j):
        return pl.multiple_of(self.plan.row(x, j * SUB), SUB)

    def stencil(self, ref, at):
        crows, pitch, lane = self.plan.crows, self.plan.pitch, self.lane
        mids, sums = [], []
        for base in (0, crows):
            mids.append(ref[pl.ds(base + at, SUB), :])
            total = ref[pl.ds(base + at - 1, SUB), :] + ref[pl.ds(base + at + 1, SUB), :]
            total += ref[pl.ds(base + at - pitch, SUB), :] + ref[pl.ds(base + at + pitch, SUB), :]
            sums.append(total)
        for i in range(2):
            sums[i] += pltpu.roll(jnp.where(lane == LANES - 1, mids[1 - i], mids[i]), 1, 1)
            sums[i] += pltpu.roll(jnp.where(lane == 0, mids[1 - i], mids[i]), LANES - 1, 1)
        return mids, sums

    def step2(self, places):
        values = []
        for x, j in places:
            at = self.at(x, j)
            mids, sums = self.stencil(self.comp, at)
            for i in range(2):
                v = 0.165 * mids[i] + 0.0225 * sums[i]
                v = v * self.ymask if j == self.main else v
                values.append((i * self.plan.crows + at, v * self.zmask if i else v))
        for at, v in values:
            self.second[pl.ds(at, SUB), :] = v

    def step3(self, places):
        crows, lane = self.plan.crows, self.lane
        values = []
        for x, j in places:
            at = self.at(x, j)
            mids, sums = self.stencil(self.second, at)
            outs = []
            for i in range(2):
                v = 0.1 * mids[i] + 0.15 * (self.comp[pl.ds(i * crows + at, SUB), :] + sums[i])
                v = v * self.ymask if j == self.main else v
                outs.append(v * self.zmask if i else v)
            values.append((at, outs[0]))
            values.append((crows + at, jnp.where(lane >= LANES - 2, outs[1], outs[0])))
            values.append((2 * crows + at, jnp.where(lane < 2, outs[1], outs[0])))
        for at, v in values:
            self.third[pl.ds(at, SUB), :] = v

    def planes(self, step, first, last, tiles, group=2):
        whole = (last + 1 - first) // group

        def body(i, carry):
            step([(first + i * group + k, j) for k in range(group) for j in tiles])
            return carry

        lax.fori_loop(0, whole, body, 0)
        for x in range(first + whole * group, last + 1):
            step([(x, j) for j in tiles])


def inner_kernel(plan, comp, second, third):
    s = Sweeps(plan, comp, second, third)
    s.planes(s.step2, 1, plan.cx - 2, range(s.main))
    s.planes(s.step3, 2, plan.cx - 3, range(1, s.main - 1))


def middle_kernel(plan, comp, second_in, third_in, second, third):
    del second_in, third_in
    s = Sweeps(plan, comp, second, third)
    for y, rim in ((0, -1), (plan.cy - 1, plan.cy)):
        for base in (0, plan.crows):
            rows = pl.ds(base + plan.row(0, y), plan.cx, stride=plan.pitch)
            rims = pl.ds(base + plan.row(0, rim), plan.cx, stride=plan.pitch)
            second[rows, :] = second[rows, :] + 0.0225 * comp[rims, :]
    s.planes(s.step2, 0, plan.cx - 2, (s.main,), group=4)
    s.planes(s.step3, 2, plan.cx - 3, (0, s.main - 1, s.main))


def put_xfaces(plan, x_refs, comp):
    odd = lax.axis_index("gx") % 2
    has_lo, has_hi = flags("gx", plan.nx)
    for i, ref in enumerate(x_refs):
        at_high = odd == i
        has = (at_high & has_hi) | (jnp.logical_not(at_high) & has_lo)
        first = pl.multiple_of(plan.row(jnp.where(at_high, plan.cx, -RIM), 0) - SUB, SUB)
        packed = jnp.where(has, ref[pl.ds(plan.xrows, SUB), :], 0.0)
        row = iota((SUB, LANES), 0)
        n = plan.xrows // SUB
        values = []
        for k in range(n):
            for tile in range(2):
                v = jnp.where(has, ref[pl.ds(k * SUB, SUB), :], 0.0) if tile == 0 else unpack_rim(packed, k)
                rows = pl.ds(tile * plan.crows + first + k * SUB, SUB)
                if k == 0:
                    v = jnp.where(row >= SUB - RIM, v, comp[rows, :])
                if k == n - 1:
                    v = jnp.where(row < RIM, v, comp[rows, :])
                values.append((rows, v))
        for rows, v in values:
            comp[rows, :] = v


def edge_kernel(plan, n_x, comp_in, second_in, third_in, own_ref, *rest):
    x_refs, msg_refs = rest[:n_x], rest[n_x : n_x + plan.nz - 1]
    comp, second, third, *e_refs = rest[n_x + plan.nz - 1 :]
    del comp_in, second_in, third_in
    cx, pitch, crows = plan.cx, plan.pitch, plan.crows
    put_xfaces(plan, x_refs, comp)
    s = Sweeps(plan, comp, second, third)
    x_lo, x_hi = flags("gx", plan.nx)
    every = range(s.main + 1)
    s.step2([(-RIM, s.main), (cx - 2, s.main)])
    for x in (-2, -1, 0, cx - 1, cx, cx + 1):
        s.step2([(x, j) for j in every])
    for has, x in ((x_lo, 1 - RIM), (x_hi, cx)):

        @pl.when(jnp.logical_not(has))
        def _():
            for base in (0, crows):
                second[pl.ds(base + plan.row(x, -RIM), 2 * pitch), :] = jnp.zeros((2 * pitch, LANES), F32)

    s.step3([(1 - RIM, s.main), (cx - 3, s.main)])
    for x in (-1, 0, 1, cx - 2, cx - 1, cx):
        s.step3([(x, j) for j in every])
    for has, x in ((x_lo, -1), (x_hi, cx)):

        @pl.when(jnp.logical_not(has))
        def _():
            for base in (0, crows, 2 * crows):
                third[pl.ds(base + plan.row(x, -RIM), pitch), :] = jnp.zeros((pitch, LANES), F32)

    me = lax.axis_index("gz")
    for shift in range(plan.nz):
        tags = msg_refs[plan.nz - shift - 1] if shift else own_ref
        used = 0
        for p in range(plan.slots):
            code = message_code(plan, tags, p)
            x0, y0, home, z0 = decode(plan, code)
            here = (code >= 0) & (home == me)

            @pl.when(here)
            def _():
                cut_patch(
                    plan, third, e_refs[shift], jnp.minimum(used, CAP - 1) * plan.foot, x0, y0, z0 % plan.cz
                )

            used = used + here.astype(jnp.int32)


def cut_patch(plan, third, out, base, x0, y0, z0):
    foot, pitch, crows, win = plan.foot, plan.pitch, plan.crows, plan.win
    base = pl.multiple_of(base, SUB)
    lane = iota((foot, LANES), 1)
    offset = jnp.where(z0 == 0, crows, jnp.where(z0 == plan.cz - foot, 2 * crows, 0))
    outs = [jnp.zeros((foot, LANES), F32) for _ in range(plan.elanes // LANES)]

    def put(v, source, target, width):
        tile, k = divmod(target, LANES)
        v = pltpu.roll(v, (k - source + 2 * LANES) % LANES, 1)
        outs[tile] = jnp.where((lane >= k) & (lane < k + width), v, outs[tile])
        if k + width > LANES:
            outs[tile + 1] = jnp.where(lane < k + width - LANES, v, outs[tile + 1])

    for y in range(-1, foot + 1):
        v = third[pl.ds(offset + plan.row(x0, y0 + y), foot, stride=pitch), :]
        put(v, z0 - 1, (y + 1) * win, win)
    for i, x in enumerate((-1, foot)):
        v = third[pl.ds(pl.multiple_of(plan.row(x0 + x, y0), SUB), foot), :]
        put(v, z0, plan.elow + i * foot, foot)
    for i, v in enumerate(outs):
        out[pl.ds(base, foot), i * LANES : (i + 1) * LANES] = v


def emit_kernel(plan, third, out_ref):
    for x in range(plan.cx):
        out_ref[pl.ds(x * plan.cy, plan.cy), :] = third[pl.ds(plan.row(x, 0), plan.cy), :]


def post_kernel(plan, own_ref, fixed, *rest):
    e_refs, (out_hbm, out_ref, ups, first, ghost, yghost, sems) = rest[: plan.nz], rest[plan.nz :]
    pe, foot, tiles, slots, win = plan.pe, plan.foot, plan.tiles, plan.slots, plan.win
    me = lax.axis_index("gz")
    codes = [message_code(plan, own_ref, p) for p in range(slots)]
    homes = [decode(plan, c)[2] for c in codes]
    cuts = []
    for p in range(slots):
        rank = 0
        for q in range(p):
            rank = rank + ((homes[q] == homes[p]) & (codes[q] >= 0)).astype(jnp.int32)
        rank = jnp.minimum(rank, CAP - 1)
        shift = (me - homes[p] + plan.nz) % plan.nz
        got = [jnp.zeros((foot, LANES), F32)] * 3
        for s in range(plan.nz):
            rows = pl.ds(pl.multiple_of(rank * foot, SUB), foot)
            take = (shift == s) & (codes[p] >= 0)
            got = [
                jnp.where(take, e_refs[s][rows, i * LANES : (i + 1) * LANES], g)
                for i, g in enumerate(got)
            ]
        cuts.append(got)
    lane16 = iota((foot, LANES), 1)

    def lanes_from(got, at):
        tile, k = divmod(at, LANES)
        v = pltpu.roll(got[tile], (LANES - k) % LANES, 1)
        if k and tile + 1 < len(got):
            v = jnp.where(lane16 < LANES - k, v, pltpu.roll(got[tile + 1], LANES - k, 1))
        return v

    source, target = iota((LANES, LANES), 0), iota((LANES, LANES), 1)
    q, fz = target // 32, target % 32
    a = 1 + q // 2
    own_lane = a * win + fz // 2 + 1
    side_y = own_lane + jnp.where(q % 2 == 0, -win, win)
    side_z = own_lane + jnp.where(fz % 2 == 0, -1, 1)
    up = jnp.where(source == own_lane, 1.0, 0.0)
    around = 3.0 * up + jnp.where(source == side_y, 1.0, 0.0) + jnp.where(source == side_z, 1.0, 0.0)
    zface = jnp.where((source == side_z) & ((fz == 0) | (fz == pe - 1)), 1.0, 0.0)
    table = jnp.concatenate([up, around, zface], 1).astype(BF16)
    work = [lanes_from(got, 2 * t * win) for got in cuts for t in range(tiles)]
    spread = dot2(jnp.concatenate(work, 0), table)
    low_y = jnp.where((target >= LANES - 32) & (source == fz // 2 + 1), 1.0, 0.0)
    high_y = jnp.where((target < 32) & (source == 3 * win + fz // 2 + 1), 1.0, 0.0)
    ends = [lanes_from(got, 0) for got in cuts], [lanes_from(got, 2 * (tiles - 1) * win) for got in cuts]
    lows = dot2(jnp.concatenate(ends[0], 0), low_y.astype(BF16))
    highs = dot2(jnp.concatenate(ends[1], 0), high_y.astype(BF16))
    xsel = jnp.where((source == fz // 2), 1.0, 0.0).astype(BF16)
    xfaces = dot2(
        jnp.concatenate([lanes_from(got, plan.elow + i * foot) for got in cuts for i in range(2)], 0), xsel
    )
    lane1 = iota((1, LANES), 1)
    copies = [pltpu.make_async_copy(out_ref.at[p], out_hbm.at[p], sems.at[p]) for p in range(slots)]
    lane = iota((SUB, LANES), 1)
    for p in range(slots):
        start = SUB + p * plan.fpitch
        ustart = SUB + p * (foot + SUB)
        for v, k in ((lows, 0), (highs, 1)):
            line = v[p * foot : (p + 1) * foot]
            for parity in range(2):
                yghost[k, pl.ds(start + parity, foot, stride=2), :] = line
        for t in range(tiles):
            block = spread[(p * tiles + t) * foot : (p * tiles + t + 1) * foot]
            mine = block[:, 0:LANES]
            ups[t, pl.ds(ustart, foot), :] = mine
            for i, (urow, row) in enumerate(((ustart - 1, start - 1), (ustart + foot, start + pe))):
                face = xfaces[(2 * p + i) * foot : (2 * p + i + 1) * foot]
                line = jnp.where(lane1 < 64, face[2 * t : 2 * t + 1], face[2 * t + 1 : 2 * t + 2])
                ups[t, pl.ds(urow, 1), :] = line
                first[t, pl.ds(row, 1), :] = line
            base = 0.1 * mine + 0.15 * block[:, LANES : 2 * LANES]
            for parity, shift in enumerate((-1, 1)):
                value = base + 0.15 * ups[t, pl.ds(ustart + shift, foot), :]
                first[t, pl.ds(start + parity, foot, stride=2), :] = value
                ghost[t, pl.ds(start + parity, foot, stride=2), :] = block[:, 2 * LANES :]
        alive = codes[p] >= 0
        for j in range(pe // SUB):
            rows = pl.ds(start + j * SUB, SUB)
            values = []
            for t in range(tiles):
                mid = first[t, rows, :]
                side = ghost[t, rows, :]
                total = first[t, pl.ds(start + j * SUB - 1, SUB), :] + first[t, pl.ds(start + j * SUB + 1, SUB), :]
                total += jnp.where(lane % 32 == 0, side, pltpu.roll(mid, 1, 1))
                total += jnp.where(lane % 32 == 31, side, pltpu.roll(mid, LANES - 1, 1))
                before = first[t - 1, rows, :] if t else yghost[0, rows, :]
                after = first[t + 1, rows, :] if t + 1 < tiles else yghost[1, rows, :]
                total += pltpu.roll(jnp.where(lane >= LANES - 32, before, mid), 32, 1)
                total += pltpu.roll(jnp.where(lane < 32, after, mid), LANES - 32, 1)
                value = fixed[t, rows, :] + (0.1 * mid + 0.15 * total)
                values.append(jnp.where(alive, value, 0.0))
            for t, value in enumerate(values):
                out_ref[p, pl.ds(j * SUB, SUB), t * LANES : (t + 1) * LANES] = value
        copies[p].start()
    for copy in copies:
        copy.wait()


VMEM = pl.BlockSpec(memory_space=pltpu.VMEM)
HBM = pl.BlockSpec(memory_space=pltpu.HBM)
SMEM = pl.BlockSpec(memory_space=pltpu.SMEM)


def call(kernel, outs, args, scratch=(), aliases=None, smem=0, hbm_in=0, hbm_out=0, sems=0, cost=0):
    spaces = [s if isinstance(s, pl.MemoryRef) else pltpu.VMEM(s, F32) for s in scratch]
    return pl.pallas_call(
        kernel,
        out_shape=[jax.ShapeDtypeStruct(s, F32) for s in outs],
        in_specs=[SMEM] * smem + [HBM] * hbm_in + [VMEM] * (len(args) - hbm_in - smem),
        out_specs=[HBM] * hbm_out + [VMEM] * (len(outs) - hbm_out),
        scratch_shapes=spaces + ([pltpu.SemaphoreType.DMA((sems,))] if sems else []),
        input_output_aliases=aliases or {},
        cost_estimate=pl.CostEstimate(flops=cost, bytes_accessed=cost, transcendentals=0) if cost else None,
        compiler_params=pltpu.CompilerParams(vmem_limit_bytes=16 << 20),
    )(*args)


def swap_pairs(axis, size, sends, beside=None):
    got = []
    for start, send in enumerate(sends):
        pairs = [(i, i + 1) for i in range(start, size - 1, 2)]
        pairs += [(b, a) for a, b in pairs]
        names = axis
        if beside and len(pairs) < size:
            alone = set(range(size)) - {a for a, _ in pairs}
            names = (axis, "gz")
            pairs = [(a * beside + g, b * beside + g) for a, b in pairs for g in range(beside)]
            pairs += [(a * beside + g, a * beside + (g ^ 1)) for a in sorted(alone) for g in range(beside)]
        got.append(lax.ppermute(send, names, pairs))
    return got


def cycle(fine_rhs, coarse_rhs, patch_count, patch_corner):
    plan = Plan(fine_rhs.shape, coarse_rhs.shape)
    fine_shape = (plan.tiles, plan.frows, LANES)
    block_shape = (plan.cx * plan.cy, plan.cz)
    comp_shape = (2 * plan.crows, LANES)
    third_shape = (3 * plan.crows, LANES)
    yshape, xshape = (plan.yrows + SUB, LANES), (plan.xrows + SUB, LANES)
    eshape = (plan.erows, plan.elanes)
    n_y, n_x = min(plan.ny - 1, 2), min(plan.nx - 1, 2)
    shifts = range(1, plan.nz)
    bind = functools.partial
    rhs, pre, block, *sends = call(
        bind(pre_kernel, plan),
        [fine_shape, fine_shape, block_shape] + [(plan.msg_rows(s), LANES) for s in shifts],
        [patch_count]
        + [
            pltpu.with_memory_space_constraint(a, pltpu.HBM)
            for a in (patch_corner, fine_rhs, coarse_rhs.reshape(block_shape))
        ],
        scratch=(fine_shape, pltpu.VMEM(patch_corner.shape, jnp.int32)),
        smem=1,
        hbm_in=3,
        sems=plan.slots * plan.tiles + 2,
    )
    own = sends[0]

    def ring(s):
        return [(i, (i + s) % plan.nz) for i in range(plan.nz)]

    msgs = []
    for s, m in zip(shifts, sends):
        msgs.append(lax.ppermute(m, "gz", ring(s)))
    comp, fixed = call(bind(base_kernel, plan), [comp_shape, fine_shape], (block, own, rhs, pre), cost=4 << 20)
    comp, *ysends = call(bind(compose_kernel, plan), [comp_shape] + [yshape] * n_y, (comp, own, *msgs), aliases={0: 0})
    ygot = swap_pairs("gy", plan.ny, ysends)
    second, third = call(bind(inner_kernel, plan), [comp_shape, third_shape], (comp,), cost=4 << 20)
    comp, second, *xsends = call(
        bind(xface_kernel, plan, n_y),
        [comp_shape, comp_shape] + [xshape] * n_x,
        (comp, second, *ygot),
        aliases={0: 0, 1: 1},
    )
    xgot = swap_pairs("gx", plan.nx, xsends, beside=plan.nz if plan.nz % 2 == 0 else None)
    second, third = call(
        bind(middle_kernel, plan), [comp_shape, third_shape], (comp, second, third), aliases={1: 0, 2: 1}, cost=8 << 20
    )
    _, _, third, *cuts = call(
        bind(edge_kernel, plan, n_x),
        [comp_shape, comp_shape, third_shape] + [eshape] * plan.nz,
        (comp, second, third, own, *xgot, *msgs),
        aliases={0: 0, 1: 1, 2: 2},
    )
    back = [cuts[0]] + [lax.ppermute(cuts[s], "gz", ring(s)) for s in shifts]
    (out,) = call(bind(emit_kernel, plan), [block_shape], (third,), cost=2 << 20)
    tiny = lax.slice_in_dim(cuts[0], 0, SUB, axis=0)
    (fixed,) = call(bind(late_step, plan), [fine_shape], (rhs, fixed, tiny), cost=4 << 20)
    (fine,) = call(
        bind(post_kernel, plan),
        [fine_rhs.shape],
        (own, fixed, *back),
        scratch=(
            fine_rhs.shape,
            (plan.tiles, SUB + plan.slots * (plan.foot + SUB), LANES),
            fine_shape,
            fine_shape,
            (2, plan.frows, LANES),
        ),
        hbm_out=1,
        sems=plan.slots,
    )
    return fine, out.reshape(coarse_rhs.shape)


def solution(mesh):
    return jax.shard_map(
        cycle,
        mesh=mesh,
        in_specs=(
            P(("gx", "gy", "gz"), None, None),
            P("gx", "gy", "gz"),
            P(("gx", "gy", "gz")),
            P(("gx", "gy", "gz"), None),
        ),
        out_specs=(P(("gx", "gy", "gz"), None, None), P("gx", "gy", "gz")),
        check_vma=False,
    )
```

```python
import functools

import jax
import jax.numpy as jnp
from jax import lax
from jax.experimental import pallas as pl
from jax.experimental.pallas import tpu as pltpu
from jax.sharding import PartitionSpec as P


LANES = 128
SUB = 8
RIM = 3
CAP = 2
F32 = jnp.float32
BF16 = jnp.bfloat16


def iota(shape, dim):
    return lax.broadcasted_iota(jnp.int32, shape, dim)


def dot2(x, table):
    high = x.astype(BF16)
    low = (x - high.astype(F32)).astype(BF16)
    both = jnp.concatenate([high, low], 1)
    return jnp.dot(both, jnp.concatenate([table, table], 0), preferred_element_type=F32)


class Plan:
    def __init__(self, fine_shape, coarse_shape):
        self.slots, self.pe, self.merged = fine_shape
        self.foot = self.pe // 2
        self.cx, self.cy, self.cz = coarse_shape
        assert self.cz == LANES and self.merged == self.pe * self.pe
        assert self.foot * self.foot == 2 * LANES and self.pe * 4 == LANES
        self.tiles = self.merged // LANES
        self.fpitch = self.pe + SUB
        self.frows = SUB + self.slots * self.fpitch
        self.nx, self.ny, self.nz = (lax.axis_size(a) for a in ("gx", "gy", "gz"))
        self.pitch = self.cy + SUB
        self.crows = SUB + (self.cx + 2 * RIM) * self.pitch + SUB
        self.spots_y = self.cy // self.foot
        self.spots_z = self.cz // self.foot
        self.avg_rows = self.slots * 2 * self.foot
        self.zrows = self.cy
        assert self.cx * 4 == LANES
        self.erows = CAP * self.foot
        self.elanes = 3 * LANES
        self.win = self.foot + 2
        self.elow = self.win * self.win
        assert self.elow + 2 * self.foot <= self.elanes
        self.yrows = RIM * self.cx
        self.xrows = 3 * self.pitch + SUB
        assert self.xrows == LANES

    def row(self, x, y):
        return SUB + (x + RIM) * self.pitch + y

    def faces(self, shift):
        return shift == 1, shift == self.nz - 1

    def msg_rows(self, shift):
        high, low = self.faces(shift)
        return self.avg_rows + SUB + self.zrows * (int(high) + int(low))


def fine_neighbors(ref, t, row, tiles):
    lane = iota((SUB, LANES), 1)
    mid = ref[t, pl.ds(row, SUB), :]
    total = ref[t, pl.ds(row - 1, SUB), :] + ref[t, pl.ds(row + 1, SUB), :]
    total += jnp.where(lane % 32 == 0, 0.0, pltpu.roll(mid, 1, 1))
    total += jnp.where(lane % 32 == 31, 0.0, pltpu.roll(mid, LANES - 1, 1))
    before = ref[t - 1, pl.ds(row, SUB), :] if t else jnp.zeros_like(mid)
    after = ref[t + 1, pl.ds(row, SUB), :] if t + 1 < tiles else jnp.zeros_like(mid)
    total += pltpu.roll(jnp.where(lane >= LANES - 32, before, mid), 32, 1)
    total += pltpu.roll(jnp.where(lane < 32, after, mid), LANES - 32, 1)
    return mid, total


def zero_gaps(ref, plan):
    gap = jnp.zeros((SUB, LANES), F32)
    for t in range(plan.tiles):
        for p in range(plan.slots + 1):
            row = p * plan.fpitch
            if row + SUB <= plan.frows:
                ref[t, pl.ds(row, SUB), :] = gap


def pack_faces(ref, plan):
    lane = iota((SUB, LANES), 1)
    count = plan.cy // SUB
    high, low = [jnp.zeros((SUB, LANES), F32)] * count, [jnp.zeros((SUB, LANES), F32)] * count
    for x in range(plan.cx):
        low_mask, high_mask = lane // 4 == x, (lane + RIM) % LANES // 4 == x
        for j in range(count):
            v = pltpu.roll(ref[pl.ds(x * plan.cy + j * SUB, SUB), :], 4 * x, 1)
            low[j] = jnp.where(low_mask, v, low[j])
            high[j] = jnp.where(high_mask, v, high[j])
    return high, low


def patch_code(plan, count, corner_ref, p):
    spot_x = corner_ref[p, 0] % plan.cx // plan.foot
    spot_y = corner_ref[p, 1] % plan.cy // plan.foot
    spot_z = corner_ref[p, 2] // plan.foot
    code = (spot_x * plan.spots_y + spot_y) * (plan.spots_z * plan.nz) + spot_z
    return jnp.where(p < count, code, -1)


def pre_kernel(plan, count_ref, corner_hbm, fine_hbm, coarse_hbm, rhs, pre_ref, blk, *rest):
    msg_refs, (res, corner_ref, sems) = rest[:-3], rest[-3:]
    pe, foot, tiles, slots = plan.pe, plan.foot, plan.tiles, plan.slots
    copies = [
        pltpu.make_async_copy(
            fine_hbm.at[p, :, pl.ds(t * LANES, LANES)],
            rhs.at[t, pl.ds(SUB + p * plan.fpitch, pe), :],
            sems.at[p * tiles + t],
        )
        for p in range(slots)
        for t in range(tiles)
    ]
    at = slots * tiles
    copies.append(pltpu.make_async_copy(corner_hbm, corner_ref, sems.at[at]))
    copies.append(pltpu.make_async_copy(coarse_hbm, blk, sems.at[at + 1]))
    for copy in copies:
        copy.start()
    zero_gaps(rhs, plan)
    zero_gaps(pre_ref, plan)
    source, target = iota((4 * LANES, LANES), 0), iota((4 * LANES, LANES), 1)
    place = (source // LANES) * 32 + (source % LANES) // 64 * 16 + source % 32 // 2
    table = jnp.where(place == target, 0.5, 0.0).astype(BF16)
    for p in range(slots):
        for copy in copies[p * tiles : (p + 1) * tiles]:
            copy.wait()
        start = SUB + p * plan.fpitch
        for j in range(pe // SUB):
            rows = pl.ds(start + j * SUB, SUB)
            values = []
            for t in range(tiles):
                mid, total = fine_neighbors(rhs, t, start + j * SUB, tiles)
                values.append(0.165 * mid + 0.0225 * total)
            for t, v in enumerate(values):
                pre_ref[t, rows, :] = v
        for j in range(pe // SUB):
            rows = pl.ds(start + j * SUB, SUB)
            values = []
            for t in range(tiles):
                mid, total = fine_neighbors(pre_ref, t, start + j * SUB, tiles)
                values.append(rhs[t, rows, :] - (6.0 * mid - total))
            for t, v in enumerate(values):
                res[t, rows, :] = v
        lines = []
        for half in range(2):
            cols = []
            for k in range(4):
                t = 4 * half + k
                cols.append(
                    res[t, pl.ds(start, foot, stride=2), :]
                    + res[t, pl.ds(start + 1, foot, stride=2), :]
                )
            lines.append(jnp.concatenate(cols, 1))
        value = dot2(jnp.concatenate(lines, 0), table)
        for ref in msg_refs:
            ref[pl.ds(p * 2 * foot, 2 * foot), :] = value
    for copy in copies[at:]:
        copy.wait()
    lane = iota((SUB, LANES), 1)
    tags = jnp.zeros((SUB, LANES), F32)
    for p in range(slots):
        code = patch_code(plan, count_ref[0], corner_ref, p)
        tags = jnp.where(lane == p, code.astype(F32), tags)
    high, low = pack_faces(blk, plan)
    for shift, ref in enumerate(msg_refs, 1):
        at = plan.avg_rows
        ref[pl.ds(at, SUB), :] = tags
        at += SUB
        for face, wanted in zip((high, low), plan.faces(shift)):
            if wanted:
                for j, v in enumerate(face):
                    ref[pl.ds(at + j * SUB, SUB), :] = v
                at += plan.zrows


def below(value, count):
    bits = count.bit_length() - 1
    assert count == 1 << bits
    return lax.shift_right_arithmetic(value, bits), lax.bitwise_and(value, count - 1)


def decode(plan, code):
    spot, spot_z = below(code, plan.spots_z * plan.nz)
    spot_x, spot_y = below(spot, plan.spots_y)
    home, _ = below(spot_z, plan.spots_z)
    return spot_x * plan.foot, spot_y * plan.foot, home, spot_z * plan.foot


def message_code(plan, ref, p):
    return ref[plan.avg_rows, p].astype(jnp.int32)


def place_patch(plan, ref, base, code, comp, block=True, rims=True):
    me = lax.axis_index("gz")
    x0, y0, _, z0 = decode(plan, code)
    dz = z0 - me * plan.cz

    inside = (dz >= 0) & (dz < plan.cz)
    wanted = (code >= 0) & (dz >= -plan.foot) & (dz <= plan.cz)
    if not rims:
        wanted = wanted & inside
    if not block:
        wanted = wanted & jnp.logical_not(inside)

    @pl.when(wanted)
    def _():
        offset = jnp.where(inside, 0, plan.crows)
        lane0 = lax.bitwise_and(dz, plan.cz - 1)
        lane = iota((plan.foot, LANES), 1)
        window = (lane >= lane0) & (lane < lane0 + plan.foot)
        first = offset + plan.row(x0, y0)
        halves = [ref[pl.ds(base + half * plan.foot, plan.foot), :] for half in range(2)]
        values = []
        for y in range(plan.foot):
            half, k = divmod(y * plan.foot, LANES)
            v = pltpu.roll(halves[half], lax.bitwise_and(lane0 + LANES - k, LANES - 1), 1)
            values.append(jnp.where(window, v, comp[pl.ds(first + y, plan.foot, stride=plan.pitch), :]))
        for y, v in enumerate(values):
            comp[pl.ds(first + y, plan.foot, stride=plan.pitch), :] = v


def flags(axis, size):
    index = lax.axis_index(axis)
    return index > 0, index < size - 1


def fixed_step(plan, rhs, source, target):
    def rows8(i, carry):
        p, j = i // (plan.pe // SUB), i % (plan.pe // SUB)
        row = pl.multiple_of(SUB + p * plan.fpitch + j * SUB, SUB)
        rows = pl.ds(row, SUB)
        values = []
        for t in range(plan.tiles):
            mid, total = fine_neighbors(source, t, row, plan.tiles)
            values.append(0.1 * mid + 0.15 * (rhs[t, rows, :] + total))
        for t, v in enumerate(values):
            target[t, rows, :] = v
        return carry

    lax.fori_loop(0, plan.slots * (plan.pe // SUB), rows8, 0)


def late_step(plan, rhs, source, after, target):
    del after
    fixed_step(plan, rhs, source, target)


def base_kernel(plan, blk, own_ref, rhs, pre_ref, comp, fixed):
    codes = [message_code(plan, own_ref, p) for p in range(plan.slots)]
    zero_gaps(fixed, plan)
    fixed_step(plan, rhs, pre_ref, fixed)
    cx, cy = plan.cx, plan.cy
    end = SUB + RIM * plan.pitch
    for base in (0, plan.crows):
        comp[pl.ds(base, end), :] = jnp.zeros((end, LANES), F32)
        comp[pl.ds(base + plan.crows - end, end), :] = jnp.zeros((end, LANES), F32)
        for x in range(cx):
            comp[pl.ds(base + plan.row(x, cy), SUB), :] = jnp.zeros((SUB, LANES), F32)
    for x in range(cx):
        comp[pl.ds(plan.row(x, 0), cy), :] = blk[pl.ds(x * cy, cy), :]
    for p, code in enumerate(codes):
        place_patch(plan, own_ref, p * 2 * plan.foot, code, comp, rims=False)


def compose_kernel(plan, comp_in, own_ref, *rest):
    msg_refs, (comp, *y_sends) = rest[: plan.nz - 1], rest[plan.nz - 1 :]
    del comp_in
    codes = [[message_code(plan, ref, p) for ref in (own_ref, *msg_refs)] for p in range(plan.slots)]
    cx, cy = plan.cx, plan.cy
    lane = iota((SUB, LANES), 1)
    zero = jnp.zeros((SUB, LANES), F32)
    lo_face, hi_face = [zero] * (cy // SUB), [zero] * (cy // SUB)
    has_lo, has_hi = flags("gz", plan.nz)
    for shift, ref in enumerate(msg_refs, 1):
        at = plan.avg_rows + SUB
        for low, wanted in enumerate(plan.faces(shift)):
            if wanted:
                got = [ref[pl.ds(at + j * SUB, SUB), :] for j in range(cy // SUB)]
                if low:
                    hi_face = [jnp.where(has_hi, v, 0.0) for v in got]
                else:
                    lo_face = [jnp.where(has_lo, v, 0.0) for v in got]
                at += plan.zrows
    for x in range(cx):
        for j in range(cy // SUB):
            rows = pl.ds(plan.crows + plan.row(x, j * SUB), SUB)
            lo = pltpu.roll(lo_face[j], (-4 * x) % LANES, 1)
            hi = pltpu.roll(hi_face[j], (-4 * x) % LANES, 1)
            comp[rows, :] = jnp.where(lane >= plan.cz - RIM, lo, jnp.where(lane < RIM, hi, 0.0))
    for p in range(plan.slots):
        for ref, code in zip((own_ref, *msg_refs), codes[p]):
            place_patch(plan, ref, p * 2 * plan.foot, code, comp, block=ref is not own_ref)
    odd = lax.axis_index("gy") % 2
    for start, ref in enumerate(y_sends):
        y0 = jnp.where(odd == start, cy - RIM, 0)
        rims = []
        for k in range(RIM):
            ref[pl.ds(k * cx, cx), :] = comp[pl.ds(plan.row(0, y0 + k), cx, stride=plan.pitch), :]
            v = comp[pl.ds(plan.crows + plan.row(0, y0 + k), cx, stride=plan.pitch), :]
            rims += [v[j * SUB : (j + 1) * SUB] for j in range(cx // SUB)]
        ref[pl.ds(RIM * cx, SUB), :] = pack_rims(rims)


def pack_rims(rims):
    lane = iota((SUB, LANES), 1)
    acc = jnp.zeros((SUB, LANES), F32)
    for i, v in enumerate(rims):
        acc = jnp.where(lane // SUB == i, pltpu.roll(v, (SUB * i + 4) % LANES, 1), acc)
    return acc


def unpack_rim(packed, i):
    lane = iota((SUB, LANES), 1)
    v = pltpu.roll(packed, (-(SUB * i + 4)) % LANES, 1)
    return jnp.where((lane < RIM) | (lane >= LANES - RIM), v, 0.0)


def put_yface(plan, msg, comp, y):
    for k in range(RIM):
        comp[pl.ds(plan.row(0, y + k), plan.cx, stride=plan.pitch), :] = msg[pl.ds(k * plan.cx, plan.cx), :]
        packed = msg[pl.ds(RIM * plan.cx, SUB), :]
        n = plan.cx // SUB
        rims = jnp.concatenate([unpack_rim(packed, k * n + j) for j in range(n)], 0)
        comp[pl.ds(plan.crows + plan.row(0, y + k), plan.cx, stride=plan.pitch), :] = rims


def pack_xface(plan, comp, ref, start):
    at_high = lax.axis_index("gx") % 2 == start
    first = pl.multiple_of(plan.row(jnp.where(at_high, plan.cx - RIM, 0), 0) - SUB, SUB)
    rims = [comp[pl.ds(plan.crows + first + i * SUB, SUB), :] for i in range(plan.xrows // SUB)]
    ref[pl.ds(0, plan.xrows), :] = comp[pl.ds(first, plan.xrows), :]
    ref[pl.ds(plan.xrows, SUB), :] = pack_rims(rims)


def xface_kernel(plan, n_y, comp_in, second_in, *rest):
    y_refs, (comp, second, *x_sends) = rest[:n_y], rest[n_y:]
    del comp_in, second_in, second
    put_yfaces(plan, y_refs, comp)
    for i, ref in enumerate(x_sends):
        pack_xface(plan, comp, ref, i)


def put_yfaces(plan, y_refs, comp):
    odd = lax.axis_index("gy") % 2
    for i, ref in enumerate(y_refs):
        at_high = (odd == 0) if i == 0 else (odd == 1)
        put_yface(plan, ref, comp, jnp.where(at_high, plan.cy, -RIM))


class Sweeps:
    def __init__(self, plan, comp, second, third=None):
        self.plan, self.comp, self.second, self.third = plan, comp, second, third
        self.lane, row = iota((SUB, LANES), 1), iota((SUB, LANES), 0)
        z_lo, z_hi = flags("gz", plan.nz)
        y_lo, y_hi = flags("gy", plan.ny)
        lane = self.lane
        self.zmask = jnp.where(((lane >= LANES - RIM) & z_lo) | ((lane < RIM) & z_hi), 1.0, 0.0)
        self.ymask = jnp.where(((row >= SUB - RIM) & y_lo) | ((row < RIM) & y_hi), 1.0, 0.0)
        self.main = plan.cy // SUB

    def at(self, x, j):
        return pl.multiple_of(self.plan.row(x, j * SUB), SUB)

    def stencil(self, ref, at):
        crows, pitch, lane = self.plan.crows, self.plan.pitch, self.lane
        mids, sums = [], []
        for base in (0, crows):
            mids.append(ref[pl.ds(base + at, SUB), :])
            total = ref[pl.ds(base + at - 1, SUB), :] + ref[pl.ds(base + at + 1, SUB), :]
            total += ref[pl.ds(base + at - pitch, SUB), :] + ref[pl.ds(base + at + pitch, SUB), :]
            sums.append(total)
        for i in range(2):
            sums[i] += pltpu.roll(jnp.where(lane == LANES - 1, mids[1 - i], mids[i]), 1, 1)
            sums[i] += pltpu.roll(jnp.where(lane == 0, mids[1 - i], mids[i]), LANES - 1, 1)
        return mids, sums

    def step2(self, places):
        values = []
        for x, j in places:
            at = self.at(x, j)
            mids, sums = self.stencil(self.comp, at)
            for i in range(2):
                v = 0.165 * mids[i] + 0.0225 * sums[i]
                v = v * self.ymask if j == self.main else v
                values.append((i * self.plan.crows + at, v * self.zmask if i else v))
        for at, v in values:
            self.second[pl.ds(at, SUB), :] = v

    def step3(self, places):
        crows, lane = self.plan.crows, self.lane
        values = []
        for x, j in places:
            at = self.at(x, j)
            mids, sums = self.stencil(self.second, at)
            outs = []
            for i in range(2):
                v = 0.1 * mids[i] + 0.15 * (self.comp[pl.ds(i * crows + at, SUB), :] + sums[i])
                v = v * self.ymask if j == self.main else v
                outs.append(v * self.zmask if i else v)
            values.append((at, outs[0]))
            values.append((crows + at, jnp.where(lane >= LANES - 2, outs[1], outs[0])))
            values.append((2 * crows + at, jnp.where(lane < 2, outs[1], outs[0])))
        for at, v in values:
            self.third[pl.ds(at, SUB), :] = v

    def planes(self, step, first, last, tiles, group=2):
        whole = (last + 1 - first) // group

        def body(i, carry):
            step([(first + i * group + k, j) for k in range(group) for j in tiles])
            return carry

        lax.fori_loop(0, whole, body, 0)
        for x in range(first + whole * group, last + 1):
            step([(x, j) for j in tiles])


def inner_kernel(plan, comp, second, third):
    s = Sweeps(plan, comp, second, third)
    s.planes(s.step2, 1, plan.cx - 2, range(s.main))
    s.planes(s.step3, 2, plan.cx - 3, range(1, s.main - 1))


def middle_kernel(plan, comp, second_in, third_in, second, third):
    del second_in, third_in
    s = Sweeps(plan, comp, second, third)
    for y, rim in ((0, -1), (plan.cy - 1, plan.cy)):
        for base in (0, plan.crows):
            rows = pl.ds(base + plan.row(0, y), plan.cx, stride=plan.pitch)
            rims = pl.ds(base + plan.row(0, rim), plan.cx, stride=plan.pitch)
            second[rows, :] = second[rows, :] + 0.0225 * comp[rims, :]
    s.planes(s.step2, 0, plan.cx - 2, (s.main,), group=4)
    s.planes(s.step3, 2, plan.cx - 3, (0, s.main - 1, s.main))


def put_xfaces(plan, x_refs, comp):
    odd = lax.axis_index("gx") % 2
    has_lo, has_hi = flags("gx", plan.nx)
    for i, ref in enumerate(x_refs):
        at_high = odd == i
        has = (at_high & has_hi) | (jnp.logical_not(at_high) & has_lo)
        first = pl.multiple_of(plan.row(jnp.where(at_high, plan.cx, -RIM), 0) - SUB, SUB)
        packed = jnp.where(has, ref[pl.ds(plan.xrows, SUB), :], 0.0)
        row = iota((SUB, LANES), 0)
        n = plan.xrows // SUB
        values = []
        for k in range(n):
            for tile in range(2):
                v = jnp.where(has, ref[pl.ds(k * SUB, SUB), :], 0.0) if tile == 0 else unpack_rim(packed, k)
                rows = pl.ds(tile * plan.crows + first + k * SUB, SUB)
                if k == 0:
                    v = jnp.where(row >= SUB - RIM, v, comp[rows, :])
                if k == n - 1:
                    v = jnp.where(row < RIM, v, comp[rows, :])
                values.append((rows, v))
        for rows, v in values:
            comp[rows, :] = v


def edge_kernel(plan, n_x, comp_in, second_in, third_in, own_ref, *rest):
    x_refs, msg_refs = rest[:n_x], rest[n_x : n_x + plan.nz - 1]
    comp, second, third, *e_refs = rest[n_x + plan.nz - 1 :]
    del comp_in, second_in, third_in
    me = lax.axis_index("gz")
    cuts = []
    for shift in range(plan.nz):
        tags = msg_refs[plan.nz - shift - 1] if shift else own_ref
        used = 0
        for p in range(plan.slots):
            code = message_code(plan, tags, p)
            x0, y0, home, z0 = decode(plan, code)
            here = (code >= 0) & (home == me)
            base = jnp.minimum(used, CAP - 1) * plan.foot
            cuts.append((here, e_refs[shift], base, x0, y0, lax.bitwise_and(z0, plan.cz - 1)))
            used = used + here.astype(jnp.int32)
    cx, pitch, crows = plan.cx, plan.pitch, plan.crows
    put_xfaces(plan, x_refs, comp)
    s = Sweeps(plan, comp, second, third)
    x_lo, x_hi = flags("gx", plan.nx)
    every = range(s.main + 1)
    s.step2([(-2, j) for j in range(s.main + 1)] + [(cx - 2, s.main)])
    s.step2([(x, j) for x in (-1, 0) for j in every])
    s.step2([(x, j) for x in (cx - 1, cx) for j in every])
    s.step2([(cx + 1, j) for j in range(s.main)])
    for has, x in ((x_lo, 1 - RIM), (x_hi, cx)):

        @pl.when(jnp.logical_not(has))
        def _():
            for base in (0, crows):
                second[pl.ds(base + plan.row(x, -RIM), 2 * pitch), :] = jnp.zeros((2 * pitch, LANES), F32)

    s.step3([(-1, j) for j in every] + [(cx - 3, s.main)])
    s.step3([(x, j) for x in (0, 1) for j in every])
    s.step3([(x, j) for x in (cx - 2, cx - 1) for j in every])
    s.step3([(cx, j) for j in range(s.main)])
    for has, x in ((x_lo, -1), (x_hi, cx)):

        @pl.when(jnp.logical_not(has))
        def _():
            for base in (0, crows, 2 * crows):
                third[pl.ds(base + plan.row(x, -RIM), pitch), :] = jnp.zeros((pitch, LANES), F32)

    for here, out, base, x0, y0, z0 in cuts:

        @pl.when(here)
        def _():
            cut_patch(plan, third, out, base, x0, y0, z0)


def cut_patch(plan, third, out, base, x0, y0, z0):
    foot, pitch, crows, win = plan.foot, plan.pitch, plan.crows, plan.win
    base = pl.multiple_of(base, SUB)
    lane = iota((foot, LANES), 1)
    offset = jnp.where(z0 == 0, crows, jnp.where(z0 == plan.cz - foot, 2 * crows, 0))
    outs = [jnp.zeros((foot, LANES), F32) for _ in range(plan.elanes // LANES)]

    def put(v, source, target, width):
        tile, k = divmod(target, LANES)
        v = pltpu.roll(v, lax.bitwise_and(k - source + 2 * LANES, LANES - 1), 1)
        outs[tile] = jnp.where((lane >= k) & (lane < k + width), v, outs[tile])
        if k + width > LANES:
            outs[tile + 1] = jnp.where(lane < k + width - LANES, v, outs[tile + 1])

    for y in range(-1, foot + 1):
        v = third[pl.ds(offset + plan.row(x0, y0 + y), foot, stride=pitch), :]
        put(v, z0 - 1, (y + 1) * win, win)
    for i, x in enumerate((-1, foot)):
        v = third[pl.ds(pl.multiple_of(plan.row(x0 + x, y0), SUB), foot), :]
        put(v, z0, plan.elow + i * foot, foot)
    for i, v in enumerate(outs):
        out[pl.ds(base, foot), i * LANES : (i + 1) * LANES] = v


def emit_kernel(plan, third, out_ref):
    for x in range(plan.cx):
        out_ref[pl.ds(x * plan.cy, plan.cy), :] = third[pl.ds(plan.row(x, 0), plan.cy), :]


def post_kernel(plan, own_ref, fixed, *rest):
    e_refs, (out_hbm, out_ref, ups, first, ghost, yghost, sems) = rest[: plan.nz], rest[plan.nz :]
    pe, foot, tiles, slots, win = plan.pe, plan.foot, plan.tiles, plan.slots, plan.win
    me = lax.axis_index("gz")
    codes = [message_code(plan, own_ref, p) for p in range(slots)]
    homes = [decode(plan, c)[2] for c in codes]
    cuts = []
    for p in range(slots):
        rank = 0
        for q in range(p):
            rank = rank + ((homes[q] == homes[p]) & (codes[q] >= 0)).astype(jnp.int32)
        rank = jnp.minimum(rank, CAP - 1)
        shift = (me - homes[p] + plan.nz) % plan.nz
        got = [jnp.zeros((foot, LANES), F32)] * 3
        for s in range(plan.nz):
            rows = pl.ds(pl.multiple_of(rank * foot, SUB), foot)
            take = (shift == s) & (codes[p] >= 0)
            got = [
                jnp.where(take, e_refs[s][rows, i * LANES : (i + 1) * LANES], g)
                for i, g in enumerate(got)
            ]
        cuts.append(got)
    lane16 = iota((foot, LANES), 1)

    def lanes_from(got, at):
        tile, k = divmod(at, LANES)
        v = pltpu.roll(got[tile], (LANES - k) % LANES, 1)
        if k and tile + 1 < len(got):
            v = jnp.where(lane16 < LANES - k, v, pltpu.roll(got[tile + 1], LANES - k, 1))
        return v

    source, target = iota((LANES, LANES), 0), iota((LANES, LANES), 1)
    q, fz = target // 32, target % 32
    a = 1 + q // 2
    own_lane = a * win + fz // 2 + 1
    side_y = own_lane + jnp.where(q % 2 == 0, -win, win)
    side_z = own_lane + jnp.where(fz % 2 == 0, -1, 1)
    up = jnp.where(source == own_lane, 1.0, 0.0)
    around = 3.0 * up + jnp.where(source == side_y, 1.0, 0.0) + jnp.where(source == side_z, 1.0, 0.0)
    zface = jnp.where((source == side_z) & ((fz == 0) | (fz == pe - 1)), 1.0, 0.0)
    table = jnp.concatenate([up, around, zface], 1).astype(BF16)
    work = [lanes_from(got, 2 * t * win) for got in cuts for t in range(tiles)]
    spread = dot2(jnp.concatenate(work, 0), table)
    low_y = jnp.where((target >= LANES - 32) & (source == fz // 2 + 1), 1.0, 0.0)
    high_y = jnp.where((target < 32) & (source == 3 * win + fz // 2 + 1), 1.0, 0.0)
    ends = [lanes_from(got, 0) for got in cuts], [lanes_from(got, 2 * (tiles - 1) * win) for got in cuts]
    lows = dot2(jnp.concatenate(ends[0], 0), low_y.astype(BF16))
    highs = dot2(jnp.concatenate(ends[1], 0), high_y.astype(BF16))
    xsel = jnp.where((source == fz // 2), 1.0, 0.0).astype(BF16)
    xfaces = dot2(
        jnp.concatenate([lanes_from(got, plan.elow + i * foot) for got in cuts for i in range(2)], 0), xsel
    )
    lane1 = iota((1, LANES), 1)
    copies = [pltpu.make_async_copy(out_ref.at[p], out_hbm.at[p], sems.at[p]) for p in range(slots)]
    lane = iota((SUB, LANES), 1)
    for p in range(slots):
        start = SUB + p * plan.fpitch
        ustart = SUB + p * (foot + SUB)
        for v, k in ((lows, 0), (highs, 1)):
            line = v[p * foot : (p + 1) * foot]
            for parity in range(2):
                yghost[k, pl.ds(start + parity, foot, stride=2), :] = line
        for t in range(tiles):
            block = spread[(p * tiles + t) * foot : (p * tiles + t + 1) * foot]
            mine = block[:, 0:LANES]
            ups[t, pl.ds(ustart, foot), :] = mine
            for i, (urow, row) in enumerate(((ustart - 1, start - 1), (ustart + foot, start + pe))):
                face = xfaces[(2 * p + i) * foot : (2 * p + i + 1) * foot]
                line = jnp.where(lane1 < 64, face[2 * t : 2 * t + 1], face[2 * t + 1 : 2 * t + 2])
                ups[t, pl.ds(urow, 1), :] = line
                first[t, pl.ds(row, 1), :] = line
            base = 0.1 * mine + 0.15 * block[:, LANES : 2 * LANES]
            for parity, shift in enumerate((-1, 1)):
                value = base + 0.15 * ups[t, pl.ds(ustart + shift, foot), :]
                first[t, pl.ds(start + parity, foot, stride=2), :] = value
                ghost[t, pl.ds(start + parity, foot, stride=2), :] = block[:, 2 * LANES :]
        alive = codes[p] >= 0
        for j in range(pe // SUB):
            rows = pl.ds(start + j * SUB, SUB)
            values = []
            for t in range(tiles):
                mid = first[t, rows, :]
                side = ghost[t, rows, :]
                total = first[t, pl.ds(start + j * SUB - 1, SUB), :] + first[t, pl.ds(start + j * SUB + 1, SUB), :]
                total += jnp.where(lane % 32 == 0, side, pltpu.roll(mid, 1, 1))
                total += jnp.where(lane % 32 == 31, side, pltpu.roll(mid, LANES - 1, 1))
                before = first[t - 1, rows, :] if t else yghost[0, rows, :]
                after = first[t + 1, rows, :] if t + 1 < tiles else yghost[1, rows, :]
                total += pltpu.roll(jnp.where(lane >= LANES - 32, before, mid), 32, 1)
                total += pltpu.roll(jnp.where(lane < 32, after, mid), LANES - 32, 1)
                value = fixed[t, rows, :] + (0.1 * mid + 0.15 * total)
                values.append(jnp.where(alive, value, 0.0))
            for t, value in enumerate(values):
                out_ref[p, pl.ds(j * SUB, SUB), t * LANES : (t + 1) * LANES] = value
        copies[p].start()
    for copy in copies:
        copy.wait()


VMEM = pl.BlockSpec(memory_space=pltpu.VMEM)
HBM = pl.BlockSpec(memory_space=pltpu.HBM)
SMEM = pl.BlockSpec(memory_space=pltpu.SMEM)


def call(kernel, outs, args, scratch=(), aliases=None, smem=0, hbm_in=0, hbm_out=0, sems=0, cost=0):
    spaces = [s if isinstance(s, pl.MemoryRef) else pltpu.VMEM(s, F32) for s in scratch]
    return pl.pallas_call(
        kernel,
        out_shape=[jax.ShapeDtypeStruct(s, F32) for s in outs],
        in_specs=[SMEM] * smem + [HBM] * hbm_in + [VMEM] * (len(args) - hbm_in - smem),
        out_specs=[HBM] * hbm_out + [VMEM] * (len(outs) - hbm_out),
        scratch_shapes=spaces + ([pltpu.SemaphoreType.DMA((sems,))] if sems else []),
        input_output_aliases=aliases or {},
        cost_estimate=pl.CostEstimate(flops=cost, bytes_accessed=cost, transcendentals=0) if cost else None,
        compiler_params=pltpu.CompilerParams(vmem_limit_bytes=16 << 20),
    )(*args)


def swap_pairs(axis, size, sends, beside=None):
    got = []
    for start, send in enumerate(sends):
        pairs = [(i, i + 1) for i in range(start, size - 1, 2)]
        pairs += [(b, a) for a, b in pairs]
        names = axis
        if beside and len(pairs) < size:
            alone = set(range(size)) - {a for a, _ in pairs}
            names = (axis, "gz")
            pairs = [(a * beside + g, b * beside + g) for a, b in pairs for g in range(beside)]
            pairs += [(a * beside + g, a * beside + (g ^ 1)) for a in sorted(alone) for g in range(beside)]
        got.append(lax.ppermute(send, names, pairs))
    return got


def cycle(fine_rhs, coarse_rhs, patch_count, patch_corner):
    plan = Plan(fine_rhs.shape, coarse_rhs.shape)
    fine_shape = (plan.tiles, plan.frows, LANES)
    block_shape = (plan.cx * plan.cy, plan.cz)
    comp_shape = (2 * plan.crows, LANES)
    third_shape = (3 * plan.crows, LANES)
    yshape, xshape = (plan.yrows + SUB, LANES), (plan.xrows + SUB, LANES)
    eshape = (plan.erows, plan.elanes)
    n_y, n_x = min(plan.ny - 1, 2), min(plan.nx - 1, 2)
    shifts = range(1, plan.nz)
    bind = functools.partial
    rhs, pre, block, *sends = call(
        bind(pre_kernel, plan),
        [fine_shape, fine_shape, block_shape] + [(plan.msg_rows(s), LANES) for s in shifts],
        [patch_count]
        + [
            pltpu.with_memory_space_constraint(a, pltpu.HBM)
            for a in (patch_corner, fine_rhs, coarse_rhs.reshape(block_shape))
        ],
        scratch=(fine_shape, pltpu.VMEM(patch_corner.shape, jnp.int32)),
        smem=1,
        hbm_in=3,
        sems=plan.slots * plan.tiles + 2,
    )
    own = sends[0]

    def ring(s):
        return [(i, (i + s) % plan.nz) for i in range(plan.nz)]

    msgs = []
    for s, m in zip(shifts, sends):
        msgs.append(lax.ppermute(m, "gz", ring(s)))
    comp, fixed = call(bind(base_kernel, plan), [comp_shape, fine_shape], (block, own, rhs, pre), cost=4 << 20)
    comp, *ysends = call(bind(compose_kernel, plan), [comp_shape] + [yshape] * n_y, (comp, own, *msgs), aliases={0: 0})
    ygot = swap_pairs("gy", plan.ny, ysends)
    second, third = call(bind(inner_kernel, plan), [comp_shape, third_shape], (comp,), cost=4 << 20)
    comp, second, *xsends = call(
        bind(xface_kernel, plan, n_y),
        [comp_shape, comp_shape] + [xshape] * n_x,
        (comp, second, *ygot),
        aliases={0: 0, 1: 1},
    )
    xgot = swap_pairs("gx", plan.nx, xsends, beside=plan.nz if plan.nz % 2 == 0 else None)
    second, third = call(
        bind(middle_kernel, plan), [comp_shape, third_shape], (comp, second, third), aliases={1: 0, 2: 1}, cost=8 << 20
    )
    _, _, third, *cuts = call(
        bind(edge_kernel, plan, n_x),
        [comp_shape, comp_shape, third_shape] + [eshape] * plan.nz,
        (comp, second, third, own, *xgot, *msgs),
        aliases={0: 0, 1: 1, 2: 2},
    )
    back = [cuts[0]] + [lax.ppermute(cuts[s], "gz", ring(s)) for s in shifts]
    (out,) = call(bind(emit_kernel, plan), [block_shape], (third,), cost=2 << 20)
    tiny = lax.slice_in_dim(cuts[0], 0, SUB, axis=0)
    (fixed,) = call(bind(late_step, plan), [fine_shape], (rhs, fixed, tiny), cost=4 << 20)
    (fine,) = call(
        bind(post_kernel, plan),
        [fine_rhs.shape],
        (own, fixed, *back),
        scratch=(
            fine_rhs.shape,
            (plan.tiles, SUB + plan.slots * (plan.foot + SUB), LANES),
            fine_shape,
            fine_shape,
            (2, plan.frows, LANES),
        ),
        hbm_out=1,
        sems=plan.slots,
    )
    return fine, out.reshape(coarse_rhs.shape)


def solution(mesh):
    return jax.shard_map(
        cycle,
        mesh=mesh,
        in_specs=(
            P(("gx", "gy", "gz"), None, None),
            P("gx", "gy", "gz"),
            P(("gx", "gy", "gz")),
            P(("gx", "gy", "gz"), None),
        ),
        out_specs=(P(("gx", "gy", "gz"), None, None), P("gx", "gy", "gz")),
        check_vma=False,
    )
```

```python
import functools

import jax
import jax.numpy as jnp
from jax import lax
from jax.experimental import pallas as pl
from jax.experimental.pallas import tpu as pltpu
from jax.sharding import PartitionSpec as P


LANES = 128
SUB = 8
RIM = 3
CAP = 2
F32 = jnp.float32
BF16 = jnp.bfloat16


def iota(shape, dim):
    return lax.broadcasted_iota(jnp.int32, shape, dim)


def dot2(x, table):
    high = x.astype(BF16)
    low = (x - high.astype(F32)).astype(BF16)
    both = jnp.concatenate([high, low], 1)
    return jnp.dot(both, jnp.concatenate([table, table], 0), preferred_element_type=F32)


class Plan:
    def __init__(self, fine_shape, coarse_shape):
        self.slots, self.pe, self.merged = fine_shape
        self.foot = self.pe // 2
        self.cx, self.cy, self.cz = coarse_shape
        assert self.cz == LANES and self.merged == self.pe * self.pe
        assert self.foot * self.foot == 2 * LANES and self.pe * 4 == LANES
        self.tiles = self.merged // LANES
        self.fpitch = self.pe + SUB
        self.frows = SUB + self.slots * self.fpitch
        self.nx, self.ny, self.nz = (lax.axis_size(a) for a in ("gx", "gy", "gz"))
        self.pitch = self.cy + SUB
        self.crows = SUB + (self.cx + 2 * RIM) * self.pitch + SUB
        self.spots_y = self.cy // self.foot
        self.spots_z = self.cz // self.foot
        self.avg_rows = self.slots * 2 * self.foot
        self.zrows = self.cy
        assert self.cx * 4 == LANES
        self.erows = CAP * self.foot
        self.elanes = 3 * LANES
        self.win = self.foot + 2
        self.elow = self.win * self.win
        assert self.elow + 2 * self.foot <= self.elanes
        self.yrows = RIM * self.cx
        self.xrows = 3 * self.pitch + SUB
        assert self.xrows == LANES

    def row(self, x, y):
        return SUB + (x + RIM) * self.pitch + y

    def faces(self, shift):
        return shift == 1, shift == self.nz - 1

    def msg_rows(self, shift):
        high, low = self.faces(shift)
        return self.avg_rows + SUB + self.zrows * (int(high) + int(low))


def fine_neighbors(ref, t, row, tiles):
    lane = iota((SUB, LANES), 1)
    mid = ref[t, pl.ds(row, SUB), :]
    total = ref[t, pl.ds(row - 1, SUB), :] + ref[t, pl.ds(row + 1, SUB), :]
    total += jnp.where(lane % 32 == 0, 0.0, pltpu.roll(mid, 1, 1))
    total += jnp.where(lane % 32 == 31, 0.0, pltpu.roll(mid, LANES - 1, 1))
    before = ref[t - 1, pl.ds(row, SUB), :] if t else jnp.zeros_like(mid)
    after = ref[t + 1, pl.ds(row, SUB), :] if t + 1 < tiles else jnp.zeros_like(mid)
    total += pltpu.roll(jnp.where(lane >= LANES - 32, before, mid), 32, 1)
    total += pltpu.roll(jnp.where(lane < 32, after, mid), LANES - 32, 1)
    return mid, total


def zero_gaps(ref, plan):
    gap = jnp.zeros((SUB, LANES), F32)
    for t in range(plan.tiles):
        for p in range(plan.slots + 1):
            row = p * plan.fpitch
            if row + SUB <= plan.frows:
                ref[t, pl.ds(row, SUB), :] = gap


def pack_faces(ref, plan):
    lane = iota((SUB, LANES), 1)
    count = plan.cy // SUB
    high, low = [jnp.zeros((SUB, LANES), F32)] * count, [jnp.zeros((SUB, LANES), F32)] * count
    for x in range(plan.cx):
        low_mask, high_mask = lane // 4 == x, (lane + RIM) % LANES // 4 == x
        for j in range(count):
            v = pltpu.roll(ref[pl.ds(x * plan.cy + j * SUB, SUB), :], 4 * x, 1)
            low[j] = jnp.where(low_mask, v, low[j])
            high[j] = jnp.where(high_mask, v, high[j])
    return high, low


def patch_code(plan, count, corner_ref, p):
    spot_x = corner_ref[p, 0] % plan.cx // plan.foot
    spot_y = corner_ref[p, 1] % plan.cy // plan.foot
    spot_z = corner_ref[p, 2] // plan.foot
    code = (spot_x * plan.spots_y + spot_y) * (plan.spots_z * plan.nz) + spot_z
    return jnp.where(p < count, code, -1)


def pre_kernel(plan, count_ref, corner_hbm, fine_hbm, coarse_hbm, rhs, pre_ref, blk, *rest):
    msg_refs, (corner_ref, sems) = rest[:-2], rest[-2:]
    pe, foot, tiles, slots = plan.pe, plan.foot, plan.tiles, plan.slots
    copies = [
        pltpu.make_async_copy(
            fine_hbm.at[p, :, pl.ds(t * LANES, LANES)],
            rhs.at[t, pl.ds(SUB + p * plan.fpitch, pe), :],
            sems.at[p * tiles + t],
        )
        for p in range(slots)
        for t in range(tiles)
    ]
    at = slots * tiles
    copies.append(pltpu.make_async_copy(corner_hbm, corner_ref, sems.at[at]))
    copies.append(pltpu.make_async_copy(coarse_hbm, blk, sems.at[at + 1]))
    for copy in copies:
        copy.start()
    zero_gaps(rhs, plan)
    zero_gaps(pre_ref, plan)
    source, target = iota((4 * LANES, LANES), 0), iota((4 * LANES, LANES), 1)
    place = (source // LANES) * 32 + (source % LANES) // 64 * 16 + source % 32 // 2
    summed = jnp.where(place == target, 0.5, 0.0)
    source, target = iota((6 * LANES, LANES), 0), iota((6 * LANES, LANES), 1)
    dy = source // 32 - 4 - 2 * (target // foot)
    dz = source % 32 - 2 * (target % foot)
    y_in, z_in = (dy >= 0) & (dy <= 1), (dz >= 0) & (dz <= 1)
    weight = jnp.where(y_in & (dz >= -1) & (dz <= 2), 0.5, 0.0) + jnp.where(z_in & (dy >= -1) & (dy <= 2), 0.5, 0.0)
    weight = jnp.where(y_in & z_in, -1.5, weight)
    table = jnp.concatenate([summed, weight], 0).astype(BF16)
    for copy in copies:
        copy.wait()

    lines = []
    for p in range(slots):
        start = SUB + p * plan.fpitch
        for j in range(pe // SUB):
            rows = pl.ds(start + j * SUB, SUB)
            for t in range(tiles):
                mid, total = fine_neighbors(rhs, t, start + j * SUB, tiles)
                pre_ref[t, rows, :] = 0.165 * mid + 0.0225 * total

        def every(ref, t, at):
            return ref[t, pl.ds(start + at, foot, stride=2), :]

        outer, inner = [], [jnp.zeros((foot, LANES), F32)]
        for t in range(tiles):
            outer.append(every(rhs, t, 0) + every(rhs, t, 1) + (every(pre_ref, t, -1) + every(pre_ref, t, 2)))
            inner.append(every(pre_ref, t, 0) + every(pre_ref, t, 1))
        inner.append(inner[0])
        for first in range(0, tiles, 4):
            lines.append(jnp.concatenate(outer[first : first + 4] + inner[first : first + 6], 1))
    lane = iota((SUB, LANES), 1)
    tags = jnp.zeros((SUB, LANES), F32)
    for p in range(slots):
        code = patch_code(plan, count_ref[0], corner_ref, p)
        tags = jnp.where(lane == p, code.astype(F32), tags)
    high, low = pack_faces(blk, plan)
    value = dot2(jnp.concatenate(lines, 0), table)
    for ref in msg_refs:
        ref[pl.ds(0, plan.avg_rows), :] = value
    for shift, ref in enumerate(msg_refs, 1):
        at = plan.avg_rows
        ref[pl.ds(at, SUB), :] = tags
        at += SUB
        for face, wanted in zip((high, low), plan.faces(shift)):
            if wanted:
                for j, v in enumerate(face):
                    ref[pl.ds(at + j * SUB, SUB), :] = v
                at += plan.zrows


def below(value, count):
    bits = count.bit_length() - 1
    assert count == 1 << bits
    return lax.shift_right_arithmetic(value, bits), lax.bitwise_and(value, count - 1)


def decode(plan, code):
    spot, spot_z = below(code, plan.spots_z * plan.nz)
    spot_x, spot_y = below(spot, plan.spots_y)
    home, _ = below(spot_z, plan.spots_z)
    return spot_x * plan.foot, spot_y * plan.foot, home, spot_z * plan.foot


def message_code(plan, ref, p):
    return ref[plan.avg_rows, p].astype(jnp.int32)


def place_patch(plan, ref, base, code, comp, block=True, rims=True):
    me = lax.axis_index("gz")
    x0, y0, _, z0 = decode(plan, code)
    dz = z0 - me * plan.cz

    inside = (dz >= 0) & (dz < plan.cz)
    wanted = (code >= 0) & (dz >= -plan.foot) & (dz <= plan.cz)
    if not rims:
        wanted = wanted & inside
    if not block:
        wanted = wanted & jnp.logical_not(inside)

    @pl.when(wanted)
    def _():
        offset = jnp.where(inside, 0, plan.crows)
        lane0 = lax.bitwise_and(dz, plan.cz - 1)
        lane = iota((plan.foot, LANES), 1)
        window = (lane >= lane0) & (lane < lane0 + plan.foot)
        first = offset + plan.row(x0, y0)
        halves = [ref[pl.ds(base + half * plan.foot, plan.foot), :] for half in range(2)]
        values = []
        for y in range(plan.foot):
            half, k = divmod(y * plan.foot, LANES)
            v = pltpu.roll(halves[half], lax.bitwise_and(lane0 + LANES - k, LANES - 1), 1)
            values.append(jnp.where(window, v, comp[pl.ds(first + y, plan.foot, stride=plan.pitch), :]))
        for y, v in enumerate(values):
            comp[pl.ds(first + y, plan.foot, stride=plan.pitch), :] = v


def flags(axis, size):
    index = lax.axis_index(axis)
    return index > 0, index < size - 1


def fixed_step(plan, rhs, source, target):
    def rows8(i, carry):
        p, j = i // (plan.pe // SUB), i % (plan.pe // SUB)
        row = pl.multiple_of(SUB + p * plan.fpitch + j * SUB, SUB)
        rows = pl.ds(row, SUB)
        values = []
        for t in range(plan.tiles):
            mid, total = fine_neighbors(source, t, row, plan.tiles)
            values.append(0.1 * mid + 0.15 * (rhs[t, rows, :] + total))
        for t, v in enumerate(values):
            target[t, rows, :] = v
        return carry

    lax.fori_loop(0, plan.slots * (plan.pe // SUB), rows8, 0)


def base_kernel(plan, blk, own_ref, rhs, pre_ref, comp, fixed, work):
    codes = [message_code(plan, own_ref, p) for p in range(plan.slots)]
    zero_gaps(work, plan)
    fixed_step(plan, rhs, pre_ref, work)
    fixed_step(plan, rhs, work, fixed)
    cx, cy = plan.cx, plan.cy
    end = SUB + RIM * plan.pitch
    for base in (0, plan.crows):
        comp[pl.ds(base, end), :] = jnp.zeros((end, LANES), F32)
        comp[pl.ds(base + plan.crows - end, end), :] = jnp.zeros((end, LANES), F32)
        for x in range(cx):
            comp[pl.ds(base + plan.row(x, cy), SUB), :] = jnp.zeros((SUB, LANES), F32)
    for x in range(cx):
        comp[pl.ds(plan.row(x, 0), cy), :] = blk[pl.ds(x * cy, cy), :]
    for p, code in enumerate(codes):
        place_patch(plan, own_ref, p * 2 * plan.foot, code, comp, rims=False)


def compose_kernel(plan, comp_in, own_ref, *rest):
    msg_refs, (comp, *y_sends) = rest[: plan.nz - 1], rest[plan.nz - 1 :]
    del comp_in
    codes = [[message_code(plan, ref, p) for ref in (own_ref, *msg_refs)] for p in range(plan.slots)]
    cx, cy = plan.cx, plan.cy
    lane = iota((SUB, LANES), 1)
    zero = jnp.zeros((SUB, LANES), F32)
    lo_face, hi_face = [zero] * (cy // SUB), [zero] * (cy // SUB)
    has_lo, has_hi = flags("gz", plan.nz)
    for shift, ref in enumerate(msg_refs, 1):
        at = plan.avg_rows + SUB
        for low, wanted in enumerate(plan.faces(shift)):
            if wanted:
                got = [ref[pl.ds(at + j * SUB, SUB), :] for j in range(cy // SUB)]
                if low:
                    hi_face = [jnp.where(has_hi, v, 0.0) for v in got]
                else:
                    lo_face = [jnp.where(has_lo, v, 0.0) for v in got]
                at += plan.zrows
    for x in range(cx):
        for j in range(cy // SUB):
            rows = pl.ds(plan.crows + plan.row(x, j * SUB), SUB)
            lo = pltpu.roll(lo_face[j], (-4 * x) % LANES, 1)
            hi = pltpu.roll(hi_face[j], (-4 * x) % LANES, 1)
            comp[rows, :] = jnp.where(lane >= plan.cz - RIM, lo, jnp.where(lane < RIM, hi, 0.0))
    for p in range(plan.slots):
        for ref, code in zip((own_ref, *msg_refs), codes[p]):
            place_patch(plan, ref, p * 2 * plan.foot, code, comp, block=ref is not own_ref)
    odd = lax.axis_index("gy") % 2
    for start, ref in enumerate(y_sends):
        y0 = jnp.where(odd == start, cy - RIM, 0)
        rims = []
        for k in range(RIM):
            ref[pl.ds(k * cx, cx), :] = comp[pl.ds(plan.row(0, y0 + k), cx, stride=plan.pitch), :]
            v = comp[pl.ds(plan.crows + plan.row(0, y0 + k), cx, stride=plan.pitch), :]
            rims += [v[j * SUB : (j + 1) * SUB] for j in range(cx // SUB)]
        ref[pl.ds(RIM * cx, SUB), :] = pack_rims(rims)


def pack_rims(rims):
    lane = iota((SUB, LANES), 1)
    acc = jnp.zeros((SUB, LANES), F32)
    for i, v in enumerate(rims):
        acc = jnp.where(lane // SUB == i, pltpu.roll(v, (SUB * i + 4) % LANES, 1), acc)
    return acc


def unpack_rim(packed, i):
    lane = iota((SUB, LANES), 1)
    v = pltpu.roll(packed, (-(SUB * i + 4)) % LANES, 1)
    return jnp.where((lane < RIM) | (lane >= LANES - RIM), v, 0.0)


def put_yface(plan, msg, comp, y):
    for k in range(RIM):
        comp[pl.ds(plan.row(0, y + k), plan.cx, stride=plan.pitch), :] = msg[pl.ds(k * plan.cx, plan.cx), :]
        packed = msg[pl.ds(RIM * plan.cx, SUB), :]
        n = plan.cx // SUB
        rims = jnp.concatenate([unpack_rim(packed, k * n + j) for j in range(n)], 0)
        comp[pl.ds(plan.crows + plan.row(0, y + k), plan.cx, stride=plan.pitch), :] = rims


def pack_xface(plan, comp, ref, start):
    at_high = lax.axis_index("gx") % 2 == start
    first = pl.multiple_of(plan.row(jnp.where(at_high, plan.cx - RIM, 0), 0) - SUB, SUB)
    rims = [comp[pl.ds(plan.crows + first + i * SUB, SUB), :] for i in range(plan.xrows // SUB)]
    ref[pl.ds(0, plan.xrows), :] = comp[pl.ds(first, plan.xrows), :]
    ref[pl.ds(plan.xrows, SUB), :] = pack_rims(rims)


def xface_kernel(plan, n_y, comp_in, second_in, *rest):
    y_refs, (comp, second, *x_sends) = rest[:n_y], rest[n_y:]
    del comp_in, second_in, second
    put_yfaces(plan, y_refs, comp)
    for i, ref in enumerate(x_sends):
        pack_xface(plan, comp, ref, i)


def put_yfaces(plan, y_refs, comp):
    odd = lax.axis_index("gy") % 2
    for i, ref in enumerate(y_refs):
        at_high = (odd == 0) if i == 0 else (odd == 1)
        put_yface(plan, ref, comp, jnp.where(at_high, plan.cy, -RIM))


class Sweeps:
    def __init__(self, plan, comp, second, third=None):
        self.plan, self.comp, self.second, self.third = plan, comp, second, third
        self.lane, row = iota((SUB, LANES), 1), iota((SUB, LANES), 0)
        z_lo, z_hi = flags("gz", plan.nz)
        y_lo, y_hi = flags("gy", plan.ny)
        lane = self.lane
        self.zmask = jnp.where(((lane >= LANES - RIM) & z_lo) | ((lane < RIM) & z_hi), 1.0, 0.0)
        self.ymask = jnp.where(((row >= SUB - RIM) & y_lo) | ((row < RIM) & y_hi), 1.0, 0.0)
        self.main = plan.cy // SUB

    def at(self, x, j):
        return pl.multiple_of(self.plan.row(x, j * SUB), SUB)

    def stencil(self, ref, at):
        crows, pitch, lane = self.plan.crows, self.plan.pitch, self.lane
        mids, sums = [], []
        for base in (0, crows):
            mids.append(ref[pl.ds(base + at, SUB), :])
            total = ref[pl.ds(base + at - 1, SUB), :] + ref[pl.ds(base + at + 1, SUB), :]
            total += ref[pl.ds(base + at - pitch, SUB), :] + ref[pl.ds(base + at + pitch, SUB), :]
            sums.append(total)
        for i in range(2):
            sums[i] += pltpu.roll(jnp.where(lane == LANES - 1, mids[1 - i], mids[i]), 1, 1)
            sums[i] += pltpu.roll(jnp.where(lane == 0, mids[1 - i], mids[i]), LANES - 1, 1)
        return mids, sums

    def step2(self, places):
        values = []
        for x, j in places:
            at = self.at(x, j)
            mids, sums = self.stencil(self.comp, at)
            for i in range(2):
                v = 0.165 * mids[i] + 0.0225 * sums[i]
                v = v * self.ymask if j == self.main else v
                values.append((i * self.plan.crows + at, v * self.zmask if i else v))
        for at, v in values:
            self.second[pl.ds(at, SUB), :] = v

    def step3(self, places):
        crows, lane = self.plan.crows, self.lane
        values = []
        for x, j in places:
            at = self.at(x, j)
            mids, sums = self.stencil(self.second, at)
            outs = []
            for i in range(2):
                v = 0.1 * mids[i] + 0.15 * (self.comp[pl.ds(i * crows + at, SUB), :] + sums[i])
                v = v * self.ymask if j == self.main else v
                outs.append(v * self.zmask if i else v)
            values.append((at, outs[0]))
            values.append((crows + at, jnp.where(lane >= LANES - 2, outs[1], outs[0])))
            values.append((2 * crows + at, jnp.where(lane < 2, outs[1], outs[0])))
        for at, v in values:
            self.third[pl.ds(at, SUB), :] = v

    def planes(self, step, first, last, tiles, group=2):
        whole = (last + 1 - first) // group

        def body(i, carry):
            step([(first + i * group + k, j) for k in range(group) for j in tiles])
            return carry

        lax.fori_loop(0, whole, body, 0)
        for x in range(first + whole * group, last + 1):
            step([(x, j) for j in tiles])


def inner_kernel(plan, comp, second, third):
    s = Sweeps(plan, comp, second, third)
    s.planes(s.step2, 1, plan.cx - 2, range(s.main))
    s.planes(s.step3, 2, plan.cx - 3, range(1, s.main - 1))


def middle_kernel(plan, comp, second_in, third_in, second, third):
    del second_in, third_in
    s = Sweeps(plan, comp, second, third)
    for y, rim in ((0, -1), (plan.cy - 1, plan.cy)):
        for base in (0, plan.crows):
            rows = pl.ds(base + plan.row(0, y), plan.cx, stride=plan.pitch)
            rims = pl.ds(base + plan.row(0, rim), plan.cx, stride=plan.pitch)
            second[rows, :] = second[rows, :] + 0.0225 * comp[rims, :]
    s.planes(s.step2, 0, plan.cx - 2, (s.main,), group=4)
    s.planes(s.step3, 2, plan.cx - 3, (0, s.main - 1, s.main))


def put_xfaces(plan, x_refs, comp):
    odd = lax.axis_index("gx") % 2
    has_lo, has_hi = flags("gx", plan.nx)
    for i, ref in enumerate(x_refs):
        at_high = odd == i
        has = (at_high & has_hi) | (jnp.logical_not(at_high) & has_lo)
        first = pl.multiple_of(plan.row(jnp.where(at_high, plan.cx, -RIM), 0) - SUB, SUB)
        packed = jnp.where(has, ref[pl.ds(plan.xrows, SUB), :], 0.0)
        row = iota((SUB, LANES), 0)
        n = plan.xrows // SUB
        values = []
        for k in range(n):
            for tile in range(2):
                v = jnp.where(has, ref[pl.ds(k * SUB, SUB), :], 0.0) if tile == 0 else unpack_rim(packed, k)
                rows = pl.ds(tile * plan.crows + first + k * SUB, SUB)
                if k == 0:
                    v = jnp.where(row >= SUB - RIM, v, comp[rows, :])
                if k == n - 1:
                    v = jnp.where(row < RIM, v, comp[rows, :])
                values.append((rows, v))
        for rows, v in values:
            comp[rows, :] = v


def edge_kernel(plan, n_x, comp_in, second_in, third_in, own_ref, *rest):
    x_refs, msg_refs = rest[:n_x], rest[n_x : n_x + plan.nz - 1]
    comp, second, third, *e_refs = rest[n_x + plan.nz - 1 :]
    del comp_in, second_in, third_in
    me = lax.axis_index("gz")
    cuts = []
    for shift in range(plan.nz):
        tags = msg_refs[plan.nz - shift - 1] if shift else own_ref
        used = 0
        for p in range(plan.slots):
            code = message_code(plan, tags, p)
            x0, y0, home, z0 = decode(plan, code)
            here = (code >= 0) & (home == me)
            base = jnp.minimum(used, CAP - 1) * plan.foot
            cuts.append((here, e_refs[shift], base, x0, y0, lax.bitwise_and(z0, plan.cz - 1)))
            used = used + here.astype(jnp.int32)
    cx, pitch, crows = plan.cx, plan.pitch, plan.crows
    put_xfaces(plan, x_refs, comp)
    s = Sweeps(plan, comp, second, third)
    x_lo, x_hi = flags("gx", plan.nx)
    every = range(s.main + 1)
    s.step2([(-2, j) for j in range(s.main + 1)] + [(cx - 2, s.main)])
    s.step2([(x, j) for x in (-1, 0) for j in every])
    s.step2([(x, j) for x in (cx - 1, cx) for j in every])
    s.step2([(cx + 1, j) for j in range(s.main)])
    for has, x in ((x_lo, 1 - RIM), (x_hi, cx)):

        @pl.when(jnp.logical_not(has))
        def _():
            for base in (0, crows):
                second[pl.ds(base + plan.row(x, -RIM), 2 * pitch), :] = jnp.zeros((2 * pitch, LANES), F32)

    s.step3([(-1, j) for j in every] + [(cx - 3, s.main)])
    s.step3([(x, j) for x in (0, 1) for j in every])
    s.step3([(x, j) for x in (cx - 2, cx - 1) for j in every])
    s.step3([(cx, j) for j in range(s.main)])
    for has, x in ((x_lo, -1), (x_hi, cx)):

        @pl.when(jnp.logical_not(has))
        def _():
            for base in (0, crows, 2 * crows):
                third[pl.ds(base + plan.row(x, -RIM), pitch), :] = jnp.zeros((pitch, LANES), F32)

    for here, out, base, x0, y0, z0 in cuts:

        @pl.when(here)
        def _():
            cut_patch(plan, third, out, base, x0, y0, z0)


def cut_patch(plan, third, out, base, x0, y0, z0):
    foot, pitch, crows, win = plan.foot, plan.pitch, plan.crows, plan.win
    base = pl.multiple_of(base, SUB)
    lane = iota((foot, LANES), 1)
    offset = jnp.where(z0 == 0, crows, jnp.where(z0 == plan.cz - foot, 2 * crows, 0))
    outs = [jnp.zeros((foot, LANES), F32) for _ in range(plan.elanes // LANES)]

    def put(v, source, target, width):
        tile, k = divmod(target, LANES)
        v = pltpu.roll(v, lax.bitwise_and(k - source + 2 * LANES, LANES - 1), 1)
        outs[tile] = jnp.where((lane >= k) & (lane < k + width), v, outs[tile])
        if k + width > LANES:
            outs[tile + 1] = jnp.where(lane < k + width - LANES, v, outs[tile + 1])

    for y in range(-1, foot + 1):
        v = third[pl.ds(offset + plan.row(x0, y0 + y), foot, stride=pitch), :]
        put(v, z0 - 1, (y + 1) * win, win)
    for i, x in enumerate((-1, foot)):
        v = third[pl.ds(pl.multiple_of(plan.row(x0 + x, y0), SUB), foot), :]
        put(v, z0, plan.elow + i * foot, foot)
    for i, v in enumerate(outs):
        out[pl.ds(base, foot), i * LANES : (i + 1) * LANES] = v


def emit_kernel(plan, third, out_ref):
    for x in range(plan.cx):
        out_ref[pl.ds(x * plan.cy, plan.cy), :] = third[pl.ds(plan.row(x, 0), plan.cy), :]


def post_kernel(plan, own_ref, fixed, *rest):
    e_refs, (out_hbm, out_ref, ups, first, ghost, yghost, sems) = rest[: plan.nz], rest[plan.nz :]
    pe, foot, tiles, slots, win = plan.pe, plan.foot, plan.tiles, plan.slots, plan.win
    me = lax.axis_index("gz")
    codes = [message_code(plan, own_ref, p) for p in range(slots)]
    homes = [decode(plan, c)[2] for c in codes]
    cuts = []
    for p in range(slots):
        rank = 0
        for q in range(p):
            rank = rank + ((homes[q] == homes[p]) & (codes[q] >= 0)).astype(jnp.int32)
        rank = jnp.minimum(rank, CAP - 1)
        shift = (me - homes[p] + plan.nz) % plan.nz
        got = [jnp.zeros((foot, LANES), F32)] * 3
        for s in range(plan.nz):
            rows = pl.ds(pl.multiple_of(rank * foot, SUB), foot)
            take = (shift == s) & (codes[p] >= 0)
            got = [
                jnp.where(take, e_refs[s][rows, i * LANES : (i + 1) * LANES], g)
                for i, g in enumerate(got)
            ]
        cuts.append(got)
    lane16 = iota((foot, LANES), 1)

    def lanes_from(got, at):
        tile, k = divmod(at, LANES)
        v = pltpu.roll(got[tile], (LANES - k) % LANES, 1)
        if k and tile + 1 < len(got):
            v = jnp.where(lane16 < LANES - k, v, pltpu.roll(got[tile + 1], LANES - k, 1))
        return v

    source, target = iota((LANES, LANES), 0), iota((LANES, LANES), 1)
    q, fz = target // 32, target % 32
    a = 1 + q // 2
    own_lane = a * win + fz // 2 + 1
    side_y = own_lane + jnp.where(q % 2 == 0, -win, win)
    side_z = own_lane + jnp.where(fz % 2 == 0, -1, 1)
    up = jnp.where(source == own_lane, 1.0, 0.0)
    around = 3.0 * up + jnp.where(source == side_y, 1.0, 0.0) + jnp.where(source == side_z, 1.0, 0.0)
    zface = jnp.where((source == side_z) & ((fz == 0) | (fz == pe - 1)), 1.0, 0.0)
    table = jnp.concatenate([up, around, zface], 1).astype(BF16)
    low_y = jnp.where((target >= LANES - 32) & (source == fz // 2 + 1), 1.0, 0.0)
    high_y = jnp.where((target < 32) & (source == 3 * win + fz // 2 + 1), 1.0, 0.0)
    low_y, high_y = low_y.astype(BF16), high_y.astype(BF16)
    xsel = jnp.where((source == fz // 2), 1.0, 0.0).astype(BF16)

    def products(got):
        work = [lanes_from(got, 2 * t * win) for t in range(tiles)]
        sides = [lanes_from(got, plan.elow + i * foot) for i in range(2)]
        return (
            dot2(jnp.concatenate(work, 0), table),
            dot2(work[0], low_y),
            dot2(work[tiles - 1], high_y),
            dot2(jnp.concatenate(sides, 0), xsel),
        )

    ahead = products(cuts[0])
    lane1 = iota((1, LANES), 1)
    copies = [pltpu.make_async_copy(out_ref.at[p], out_hbm.at[p], sems.at[p]) for p in range(slots)]
    lane = iota((SUB, LANES), 1)
    for p in range(slots):
        start = SUB + p * plan.fpitch
        ustart = SUB + p * (foot + SUB)
        spread, lows, highs, xfaces = ahead
        if p + 1 < slots:
            ahead = products(cuts[p + 1])
        for k, line in enumerate((lows, highs)):
            for parity in range(2):
                yghost[k, pl.ds(start + parity, foot, stride=2), :] = line
        for t in range(tiles):
            block = spread[t * foot : (t + 1) * foot]
            mine = block[:, 0:LANES]
            ups[t, pl.ds(ustart, foot), :] = mine
            for i, (urow, row) in enumerate(((ustart - 1, start - 1), (ustart + foot, start + pe))):
                face = xfaces[i * foot : (i + 1) * foot]
                line = jnp.where(lane1 < 64, face[2 * t : 2 * t + 1], face[2 * t + 1 : 2 * t + 2])
                ups[t, pl.ds(urow, 1), :] = line
                first[t, pl.ds(row, 1), :] = line
            base = 0.1 * mine + 0.15 * block[:, LANES : 2 * LANES]
            for parity, shift in enumerate((-1, 1)):
                value = base + 0.15 * ups[t, pl.ds(ustart + shift, foot), :]
                first[t, pl.ds(start + parity, foot, stride=2), :] = value
                ghost[t, pl.ds(start + parity, foot, stride=2), :] = block[:, 2 * LANES :]
        alive = codes[p] >= 0
        for j in range(pe // SUB):
            rows = pl.ds(start + j * SUB, SUB)
            values = []
            for t in range(tiles):
                mid = first[t, rows, :]
                side = ghost[t, rows, :]
                total = first[t, pl.ds(start + j * SUB - 1, SUB), :] + first[t, pl.ds(start + j * SUB + 1, SUB), :]
                total += jnp.where(lane % 32 == 0, side, pltpu.roll(mid, 1, 1))
                total += jnp.where(lane % 32 == 31, side, pltpu.roll(mid, LANES - 1, 1))
                before = first[t - 1, rows, :] if t else yghost[0, rows, :]
                after = first[t + 1, rows, :] if t + 1 < tiles else yghost[1, rows, :]
                total += pltpu.roll(jnp.where(lane >= LANES - 32, before, mid), 32, 1)
                total += pltpu.roll(jnp.where(lane < 32, after, mid), LANES - 32, 1)
                value = fixed[t, rows, :] + (0.1 * mid + 0.15 * total)
                values.append(jnp.where(alive, value, 0.0))
            for t, value in enumerate(values):
                out_ref[p, pl.ds(j * SUB, SUB), t * LANES : (t + 1) * LANES] = value
        copies[p].start()
    for copy in copies:
        copy.wait()


VMEM = pl.BlockSpec(memory_space=pltpu.VMEM)
HBM = pl.BlockSpec(memory_space=pltpu.HBM)
SMEM = pl.BlockSpec(memory_space=pltpu.SMEM)


def call(kernel, outs, args, scratch=(), aliases=None, smem=0, hbm_in=0, hbm_out=0, sems=0, cost=0):
    spaces = [s if isinstance(s, pl.MemoryRef) else pltpu.VMEM(s, F32) for s in scratch]
    return pl.pallas_call(
        kernel,
        out_shape=[jax.ShapeDtypeStruct(s, F32) for s in outs],
        in_specs=[SMEM] * smem + [HBM] * hbm_in + [VMEM] * (len(args) - hbm_in - smem),
        out_specs=[HBM] * hbm_out + [VMEM] * (len(outs) - hbm_out),
        scratch_shapes=spaces + ([pltpu.SemaphoreType.DMA((sems,))] if sems else []),
        input_output_aliases=aliases or {},
        cost_estimate=pl.CostEstimate(flops=cost, bytes_accessed=cost, transcendentals=0) if cost else None,
        compiler_params=pltpu.CompilerParams(vmem_limit_bytes=16 << 20),
    )(*args)


def swap_pairs(axis, size, sends, beside=None):
    got = []
    for start, send in enumerate(sends):
        pairs = [(i, i + 1) for i in range(start, size - 1, 2)]
        pairs += [(b, a) for a, b in pairs]
        names = axis
        if beside and len(pairs) < size:
            alone = set(range(size)) - {a for a, _ in pairs}
            names = (axis, "gz")
            pairs = [(a * beside + g, b * beside + g) for a, b in pairs for g in range(beside)]
            pairs += [(a * beside + g, a * beside + (g ^ 1)) for a in sorted(alone) for g in range(beside)]
        got.append(lax.ppermute(send, names, pairs))
    return got


def cycle(fine_rhs, coarse_rhs, patch_count, patch_corner):
    plan = Plan(fine_rhs.shape, coarse_rhs.shape)
    fine_shape = (plan.tiles, plan.frows, LANES)
    block_shape = (plan.cx * plan.cy, plan.cz)
    comp_shape = (2 * plan.crows, LANES)
    third_shape = (3 * plan.crows, LANES)
    yshape, xshape = (plan.yrows + SUB, LANES), (plan.xrows + SUB, LANES)
    eshape = (plan.erows, plan.elanes)
    n_y, n_x = min(plan.ny - 1, 2), min(plan.nx - 1, 2)
    shifts = range(1, plan.nz)
    bind = functools.partial
    rhs, pre, block, *sends = call(
        bind(pre_kernel, plan),
        [fine_shape, fine_shape, block_shape] + [(plan.msg_rows(s), LANES) for s in shifts],
        [patch_count]
        + [
            pltpu.with_memory_space_constraint(a, pltpu.HBM)
            for a in (patch_corner, fine_rhs, coarse_rhs.reshape(block_shape))
        ],
        scratch=(pltpu.VMEM(patch_corner.shape, jnp.int32),),
        smem=1,
        hbm_in=3,
        sems=plan.slots * plan.tiles + 2,
    )
    own = sends[0]

    def ring(s):
        return [(i, (i + s) % plan.nz) for i in range(plan.nz)]

    msgs = []
    for s, m in zip(shifts, sends):
        msgs.append(lax.ppermute(m, "gz", ring(s)))
    comp, fixed = call(
        bind(base_kernel, plan), [comp_shape, fine_shape], (block, own, rhs, pre), scratch=(fine_shape,), cost=4 << 20
    )
    comp, *ysends = call(bind(compose_kernel, plan), [comp_shape] + [yshape] * n_y, (comp, own, *msgs), aliases={0: 0})
    ygot = swap_pairs("gy", plan.ny, ysends)
    second, third = call(bind(inner_kernel, plan), [comp_shape, third_shape], (comp,), cost=4 << 20)
    comp, second, *xsends = call(
        bind(xface_kernel, plan, n_y),
        [comp_shape, comp_shape] + [xshape] * n_x,
        (comp, second, *ygot),
        aliases={0: 0, 1: 1},
    )
    xgot = swap_pairs("gx", plan.nx, xsends, beside=plan.nz if plan.nz % 2 == 0 else None)
    second, third = call(
        bind(middle_kernel, plan), [comp_shape, third_shape], (comp, second, third), aliases={1: 0, 2: 1}, cost=8 << 20
    )
    _, _, third, *cuts = call(
        bind(edge_kernel, plan, n_x),
        [comp_shape, comp_shape, third_shape] + [eshape] * plan.nz,
        (comp, second, third, own, *xgot, *msgs),
        aliases={0: 0, 1: 1, 2: 2},
    )
    back = [cuts[0]] + [lax.ppermute(cuts[s], "gz", ring(s)) for s in shifts]
    (out,) = call(bind(emit_kernel, plan), [block_shape], (third,), cost=2 << 20)
    (fine,) = call(
        bind(post_kernel, plan),
        [fine_rhs.shape],
        (own, fixed, *back),
        scratch=(
            fine_rhs.shape,
            (plan.tiles, SUB + plan.slots * (plan.foot + SUB), LANES),
            fine_shape,
            fine_shape,
            (2, plan.frows, LANES),
        ),
        hbm_out=1,
        sems=plan.slots,
    )
    return fine, out.reshape(coarse_rhs.shape)


def solution(mesh):
    return jax.shard_map(
        cycle,
        mesh=mesh,
        in_specs=(
            P(("gx", "gy", "gz"), None, None),
            P("gx", "gy", "gz"),
            P(("gx", "gy", "gz")),
            P(("gx", "gy", "gz"), None),
        ),
        out_specs=(P(("gx", "gy", "gz"), None, None), P("gx", "gy", "gz")),
        check_vma=False,
    )
```

```python
import functools

import jax
import jax.numpy as jnp
from jax import lax
from jax.experimental import pallas as pl
from jax.experimental.pallas import tpu as pltpu
from jax.sharding import PartitionSpec as P


LANES = 128
SUB = 8
RIM = 3
CAP = 2
F32 = jnp.float32
BF16 = jnp.bfloat16


def iota(shape, dim):
    return lax.broadcasted_iota(jnp.int32, shape, dim)


def dot2(x, table):
    high = x.astype(BF16)
    low = (x - high.astype(F32)).astype(BF16)
    both = jnp.concatenate([high, low], 1)
    return jnp.dot(both, jnp.concatenate([table, table], 0), preferred_element_type=F32)


class Plan:
    def __init__(self, fine_shape, coarse_shape):
        self.slots, self.pe, self.merged = fine_shape
        self.foot = self.pe // 2
        self.cx, self.cy, self.cz = coarse_shape
        assert self.cz == LANES and self.merged == self.pe * self.pe
        assert self.foot * self.foot == 2 * LANES and self.pe * 4 == LANES
        self.tiles = self.merged // LANES
        self.fpitch = self.pe + SUB
        self.frows = SUB + self.slots * self.fpitch
        self.nx, self.ny, self.nz = (lax.axis_size(a) for a in ("gx", "gy", "gz"))
        self.pitch = self.cy + SUB
        self.crows = SUB + (self.cx + 2 * RIM) * self.pitch + SUB
        self.spots_y = self.cy // self.foot
        self.spots_z = self.cz // self.foot
        self.avg_rows = self.slots * 2 * self.foot
        self.zrows = self.cy
        assert self.cx * 4 == LANES
        self.erows = CAP * self.foot
        self.elanes = 3 * LANES
        self.win = self.foot + 2
        self.elow = self.win * self.win
        assert self.elow + 2 * self.foot <= self.elanes
        self.yrows = RIM * self.cx
        self.xrows = 3 * self.pitch + SUB
        assert self.xrows == LANES

    def row(self, x, y):
        return SUB + (x + RIM) * self.pitch + y

    def faces(self, shift):
        return shift == 1, shift == self.nz - 1

    def msg_rows(self, shift):
        high, low = self.faces(shift)
        return self.avg_rows + SUB + self.zrows * (int(high) + int(low))


def fine_neighbors(ref, t, row, tiles):
    lane = iota((SUB, LANES), 1)
    mid = ref[t, pl.ds(row, SUB), :]
    total = ref[t, pl.ds(row - 1, SUB), :] + ref[t, pl.ds(row + 1, SUB), :]
    total += jnp.where(lane % 32 == 0, 0.0, pltpu.roll(mid, 1, 1))
    total += jnp.where(lane % 32 == 31, 0.0, pltpu.roll(mid, LANES - 1, 1))
    before = ref[t - 1, pl.ds(row, SUB), :] if t else jnp.zeros_like(mid)
    after = ref[t + 1, pl.ds(row, SUB), :] if t + 1 < tiles else jnp.zeros_like(mid)
    total += pltpu.roll(jnp.where(lane >= LANES - 32, before, mid), 32, 1)
    total += pltpu.roll(jnp.where(lane < 32, after, mid), LANES - 32, 1)
    return mid, total


def zero_gaps(ref, plan):
    gap = jnp.zeros((SUB, LANES), F32)
    for t in range(plan.tiles):
        for p in range(plan.slots + 1):
            row = p * plan.fpitch
            if row + SUB <= plan.frows:
                ref[t, pl.ds(row, SUB), :] = gap


def pack_faces(ref, plan):
    lane = iota((SUB, LANES), 1)
    count = plan.cy // SUB
    high, low = [jnp.zeros((SUB, LANES), F32)] * count, [jnp.zeros((SUB, LANES), F32)] * count
    for x in range(plan.cx):
        low_mask, high_mask = lane // 4 == x, (lane + RIM) % LANES // 4 == x
        for j in range(count):
            v = pltpu.roll(ref[pl.ds(x * plan.cy + j * SUB, SUB), :], 4 * x, 1)
            low[j] = jnp.where(low_mask, v, low[j])
            high[j] = jnp.where(high_mask, v, high[j])
    return high, low


def patch_code(plan, count, corner_ref, p):
    spot_x = corner_ref[p, 0] % plan.cx // plan.foot
    spot_y = corner_ref[p, 1] % plan.cy // plan.foot
    spot_z = corner_ref[p, 2] // plan.foot
    code = (spot_x * plan.spots_y + spot_y) * (plan.spots_z * plan.nz) + spot_z
    return jnp.where(p < count, code, -1)


def pre_kernel(plan, count_ref, corner_hbm, fine_hbm, coarse_hbm, rhs, pre_ref, blk, *rest):
    msg_refs, (corner_ref, sems) = rest[:-2], rest[-2:]
    pe, foot, tiles, slots = plan.pe, plan.foot, plan.tiles, plan.slots
    copies = [
        pltpu.make_async_copy(
            fine_hbm.at[p, :, pl.ds(t * LANES, LANES)],
            rhs.at[t, pl.ds(SUB + p * plan.fpitch, pe), :],
            sems.at[p * tiles + t],
        )
        for p in range(slots)
        for t in range(tiles)
    ]
    at = slots * tiles
    copies.append(pltpu.make_async_copy(corner_hbm, corner_ref, sems.at[at]))
    copies.append(pltpu.make_async_copy(coarse_hbm, blk, sems.at[at + 1]))
    for copy in copies:
        copy.start()
    zero_gaps(rhs, plan)
    zero_gaps(pre_ref, plan)
    source, target = iota((4 * LANES, LANES), 0), iota((4 * LANES, LANES), 1)
    place = (source // LANES) * 32 + (source % LANES) // 64 * 16 + source % 32 // 2
    summed = jnp.where(place == target, 0.5, 0.0)
    source, target = iota((6 * LANES, LANES), 0), iota((6 * LANES, LANES), 1)
    dy = source // 32 - 4 - 2 * (target // foot)
    dz = source % 32 - 2 * (target % foot)
    y_in, z_in = (dy >= 0) & (dy <= 1), (dz >= 0) & (dz <= 1)
    weight = jnp.where(y_in & (dz >= -1) & (dz <= 2), 0.5, 0.0) + jnp.where(z_in & (dy >= -1) & (dy <= 2), 0.5, 0.0)
    weight = jnp.where(y_in & z_in, -1.5, weight)
    table = jnp.concatenate([summed, weight], 0).astype(BF16)
    for copy in copies:
        copy.wait()

    lines = []
    for p in range(slots):
        start = SUB + p * plan.fpitch
        for j in range(pe // SUB):
            rows = pl.ds(start + j * SUB, SUB)
            for t in range(tiles):
                mid, total = fine_neighbors(rhs, t, start + j * SUB, tiles)
                pre_ref[t, rows, :] = 0.165 * mid + 0.0225 * total

        def every(ref, t, at):
            return ref[t, pl.ds(start + at, foot, stride=2), :]

        outer, inner = [], [jnp.zeros((foot, LANES), F32)]
        for t in range(tiles):
            outer.append(every(rhs, t, 0) + every(rhs, t, 1) + (every(pre_ref, t, -1) + every(pre_ref, t, 2)))
            inner.append(every(pre_ref, t, 0) + every(pre_ref, t, 1))
        inner.append(inner[0])
        for first in range(0, tiles, 4):
            lines.append(jnp.concatenate(outer[first : first + 4] + inner[first : first + 6], 1))
    lane = iota((SUB, LANES), 1)
    tags = jnp.zeros((SUB, LANES), F32)
    for p in range(slots):
        code = patch_code(plan, count_ref[0], corner_ref, p)
        tags = jnp.where(lane == p, code.astype(F32), tags)
    high, low = pack_faces(blk, plan)
    value = dot2(jnp.concatenate(lines, 0), table)
    for ref in msg_refs:
        ref[pl.ds(0, plan.avg_rows), :] = value
    for shift, ref in enumerate(msg_refs, 1):
        at = plan.avg_rows
        ref[pl.ds(at, SUB), :] = tags
        at += SUB
        for face, wanted in zip((high, low), plan.faces(shift)):
            if wanted:
                for j, v in enumerate(face):
                    ref[pl.ds(at + j * SUB, SUB), :] = v
                at += plan.zrows


def below(value, count):
    bits = count.bit_length() - 1
    assert count == 1 << bits
    return lax.shift_right_arithmetic(value, bits), lax.bitwise_and(value, count - 1)


def decode(plan, code):
    spot, spot_z = below(code, plan.spots_z * plan.nz)
    spot_x, spot_y = below(spot, plan.spots_y)
    home, _ = below(spot_z, plan.spots_z)
    return spot_x * plan.foot, spot_y * plan.foot, home, spot_z * plan.foot


def message_code(plan, ref, p):
    return ref[plan.avg_rows, p].astype(jnp.int32)


def place_patch(plan, ref, base, code, comp, block=True, rims=True):
    me = lax.axis_index("gz")
    x0, y0, _, z0 = decode(plan, code)
    dz = z0 - me * plan.cz

    inside = (dz >= 0) & (dz < plan.cz)
    wanted = (code >= 0) & (dz >= -plan.foot) & (dz <= plan.cz)
    if not rims:
        wanted = wanted & inside
    if not block:
        wanted = wanted & jnp.logical_not(inside)

    @pl.when(wanted)
    def _():
        offset = jnp.where(inside, 0, plan.crows)
        lane0 = lax.bitwise_and(dz, plan.cz - 1)
        lane = iota((plan.foot, LANES), 1)
        window = (lane >= lane0) & (lane < lane0 + plan.foot)
        first = offset + plan.row(x0, y0)
        halves = [ref[pl.ds(base + half * plan.foot, plan.foot), :] for half in range(2)]
        values = []
        for y in range(plan.foot):
            half, k = divmod(y * plan.foot, LANES)
            v = pltpu.roll(halves[half], lax.bitwise_and(lane0 + LANES - k, LANES - 1), 1)
            values.append(jnp.where(window, v, comp[pl.ds(first + y, plan.foot, stride=plan.pitch), :]))
        for y, v in enumerate(values):
            comp[pl.ds(first + y, plan.foot, stride=plan.pitch), :] = v


def flags(axis, size):
    index = lax.axis_index(axis)
    return index > 0, index < size - 1


def fixed_step(plan, rhs, source, target):
    def rows8(i, carry):
        p, j = i // (plan.pe // SUB), i % (plan.pe // SUB)
        row = pl.multiple_of(SUB + p * plan.fpitch + j * SUB, SUB)
        rows = pl.ds(row, SUB)
        values = []
        for t in range(plan.tiles):
            mid, total = fine_neighbors(source, t, row, plan.tiles)
            values.append(0.1 * mid + 0.15 * (rhs[t, rows, :] + total))
        for t, v in enumerate(values):
            target[t, rows, :] = v
        return carry

    lax.fori_loop(0, plan.slots * (plan.pe // SUB), rows8, 0)


def base_kernel(plan, blk, own_ref, rhs, pre_ref, comp, fixed, work):
    codes = [message_code(plan, own_ref, p) for p in range(plan.slots)]
    zero_gaps(work, plan)
    fixed_step(plan, rhs, pre_ref, work)
    fixed_step(plan, rhs, work, fixed)
    cx, cy = plan.cx, plan.cy
    end = SUB + RIM * plan.pitch
    for base in (0, plan.crows):
        comp[pl.ds(base, end), :] = jnp.zeros((end, LANES), F32)
        comp[pl.ds(base + plan.crows - end, end), :] = jnp.zeros((end, LANES), F32)
        for x in range(cx):
            comp[pl.ds(base + plan.row(x, cy), SUB), :] = jnp.zeros((SUB, LANES), F32)
    for x in range(cx):
        comp[pl.ds(plan.row(x, 0), cy), :] = blk[pl.ds(x * cy, cy), :]
    for p, code in enumerate(codes):
        place_patch(plan, own_ref, p * 2 * plan.foot, code, comp, rims=False)


def compose_kernel(plan, comp_in, own_ref, *rest):
    msg_refs, (comp, *y_sends) = rest[: plan.nz - 1], rest[plan.nz - 1 :]
    del comp_in
    codes = [[message_code(plan, ref, p) for ref in (own_ref, *msg_refs)] for p in range(plan.slots)]
    cx, cy = plan.cx, plan.cy
    lane = iota((SUB, LANES), 1)
    zero = jnp.zeros((SUB, LANES), F32)
    lo_face, hi_face = [zero] * (cy // SUB), [zero] * (cy // SUB)
    has_lo, has_hi = flags("gz", plan.nz)
    for shift, ref in enumerate(msg_refs, 1):
        at = plan.avg_rows + SUB
        for low, wanted in enumerate(plan.faces(shift)):
            if wanted:
                got = [ref[pl.ds(at + j * SUB, SUB), :] for j in range(cy // SUB)]
                if low:
                    hi_face = [jnp.where(has_hi, v, 0.0) for v in got]
                else:
                    lo_face = [jnp.where(has_lo, v, 0.0) for v in got]
                at += plan.zrows
    for x in range(cx):
        for j in range(cy // SUB):
            rows = pl.ds(plan.crows + plan.row(x, j * SUB), SUB)
            lo = pltpu.roll(lo_face[j], (-4 * x) % LANES, 1)
            hi = pltpu.roll(hi_face[j], (-4 * x) % LANES, 1)
            comp[rows, :] = jnp.where(lane >= plan.cz - RIM, lo, jnp.where(lane < RIM, hi, 0.0))
    for p in range(plan.slots):
        for ref, code in zip((own_ref, *msg_refs), codes[p]):
            place_patch(plan, ref, p * 2 * plan.foot, code, comp, block=ref is not own_ref)
    odd = lax.axis_index("gy") % 2
    for start, ref in enumerate(y_sends):
        y0 = jnp.where(odd == start, cy - RIM, 0)
        rims = []
        for k in range(RIM):
            ref[pl.ds(k * cx, cx), :] = comp[pl.ds(plan.row(0, y0 + k), cx, stride=plan.pitch), :]
            v = comp[pl.ds(plan.crows + plan.row(0, y0 + k), cx, stride=plan.pitch), :]
            rims += [v[j * SUB : (j + 1) * SUB] for j in range(cx // SUB)]
        ref[pl.ds(RIM * cx, SUB), :] = pack_rims(rims)


def pack_rims(rims):
    lane = iota((SUB, LANES), 1)
    acc = jnp.zeros((SUB, LANES), F32)
    for i, v in enumerate(rims):
        acc = jnp.where(lane // SUB == i, pltpu.roll(v, (SUB * i + 4) % LANES, 1), acc)
    return acc


def unpack_rim(packed, i):
    lane = iota((SUB, LANES), 1)
    v = pltpu.roll(packed, (-(SUB * i + 4)) % LANES, 1)
    return jnp.where((lane < RIM) | (lane >= LANES - RIM), v, 0.0)


def put_yface(plan, msg, comp, y):
    for k in range(RIM):
        comp[pl.ds(plan.row(0, y + k), plan.cx, stride=plan.pitch), :] = msg[pl.ds(k * plan.cx, plan.cx), :]
        packed = msg[pl.ds(RIM * plan.cx, SUB), :]
        n = plan.cx // SUB
        rims = jnp.concatenate([unpack_rim(packed, k * n + j) for j in range(n)], 0)
        comp[pl.ds(plan.crows + plan.row(0, y + k), plan.cx, stride=plan.pitch), :] = rims


def pack_xface(plan, comp, ref, start):
    at_high = lax.axis_index("gx") % 2 == start
    first = pl.multiple_of(plan.row(jnp.where(at_high, plan.cx - RIM, 0), 0) - SUB, SUB)
    rims = [comp[pl.ds(plan.crows + first + i * SUB, SUB), :] for i in range(plan.xrows // SUB)]
    ref[pl.ds(0, plan.xrows), :] = comp[pl.ds(first, plan.xrows), :]
    ref[pl.ds(plan.xrows, SUB), :] = pack_rims(rims)


def xface_kernel(plan, n_y, comp_in, second_in, *rest):
    y_refs, (comp, second, *x_sends) = rest[:n_y], rest[n_y:]
    del comp_in, second_in, second
    put_yfaces(plan, y_refs, comp)
    for i, ref in enumerate(x_sends):
        pack_xface(plan, comp, ref, i)


def put_yfaces(plan, y_refs, comp):
    odd = lax.axis_index("gy") % 2
    for i, ref in enumerate(y_refs):
        at_high = (odd == 0) if i == 0 else (odd == 1)
        put_yface(plan, ref, comp, jnp.where(at_high, plan.cy, -RIM))


class Sweeps:
    def __init__(self, plan, comp, second, third=None):
        self.plan, self.comp, self.second, self.third = plan, comp, second, third
        self.lane, row = iota((SUB, LANES), 1), iota((SUB, LANES), 0)
        z_lo, z_hi = flags("gz", plan.nz)
        y_lo, y_hi = flags("gy", plan.ny)
        lane = self.lane
        self.zmask = jnp.where(((lane >= LANES - RIM) & z_lo) | ((lane < RIM) & z_hi), 1.0, 0.0)
        self.ymask = jnp.where(((row >= SUB - RIM) & y_lo) | ((row < RIM) & y_hi), 1.0, 0.0)
        self.main = plan.cy // SUB

    def at(self, x, j):
        return pl.multiple_of(self.plan.row(x, j * SUB), SUB)

    def stencil(self, ref, at):
        crows, pitch, lane = self.plan.crows, self.plan.pitch, self.lane
        mids, sums = [], []
        for base in (0, crows):
            mids.append(ref[pl.ds(base + at, SUB), :])
            total = ref[pl.ds(base + at - 1, SUB), :] + ref[pl.ds(base + at + 1, SUB), :]
            total += ref[pl.ds(base + at - pitch, SUB), :] + ref[pl.ds(base + at + pitch, SUB), :]
            sums.append(total)
        for i in range(2):
            sums[i] += pltpu.roll(jnp.where(lane == LANES - 1, mids[1 - i], mids[i]), 1, 1)
            sums[i] += pltpu.roll(jnp.where(lane == 0, mids[1 - i], mids[i]), LANES - 1, 1)
        return mids, sums

    def step2(self, places):
        values = []
        for x, j in places:
            at = self.at(x, j)
            mids, sums = self.stencil(self.comp, at)
            for i in range(2):
                v = 0.165 * mids[i] + 0.0225 * sums[i]
                v = v * self.ymask if j == self.main else v
                values.append((i * self.plan.crows + at, v * self.zmask if i else v))
        for at, v in values:
            self.second[pl.ds(at, SUB), :] = v

    def step3(self, places):
        crows, lane = self.plan.crows, self.lane
        values = []
        for x, j in places:
            at = self.at(x, j)
            mids, sums = self.stencil(self.second, at)
            outs = []
            for i in range(2):
                v = 0.1 * mids[i] + 0.15 * (self.comp[pl.ds(i * crows + at, SUB), :] + sums[i])
                v = v * self.ymask if j == self.main else v
                outs.append(v * self.zmask if i else v)
            values.append((at, outs[0]))
            values.append((crows + at, jnp.where(lane >= LANES - 2, outs[1], outs[0])))
            values.append((2 * crows + at, jnp.where(lane < 2, outs[1], outs[0])))
        for at, v in values:
            self.third[pl.ds(at, SUB), :] = v

    def planes(self, step, first, last, tiles, group=2):
        whole = (last + 1 - first) // group

        def body(i, carry):
            step([(first + i * group + k, j) for k in range(group) for j in tiles])
            return carry

        lax.fori_loop(0, whole, body, 0)
        for x in range(first + whole * group, last + 1):
            step([(x, j) for j in tiles])


def inner_kernel(plan, comp, second, third):
    s = Sweeps(plan, comp, second, third)
    s.planes(s.step2, 1, plan.cx - 2, range(s.main), group=3)
    s.planes(s.step3, 2, plan.cx - 3, range(1, s.main - 1))


def middle_kernel(plan, comp, second_in, third_in, second, third):
    del second_in, third_in
    s = Sweeps(plan, comp, second, third)
    for y, rim in ((0, -1), (plan.cy - 1, plan.cy)):
        for base in (0, plan.crows):
            rows = pl.ds(base + plan.row(0, y), plan.cx, stride=plan.pitch)
            rims = pl.ds(base + plan.row(0, rim), plan.cx, stride=plan.pitch)
            second[rows, :] = second[rows, :] + 0.0225 * comp[rims, :]
    s.planes(s.step2, 0, plan.cx - 2, (s.main,), group=4)
    s.planes(s.step3, 2, plan.cx - 3, (0, s.main - 1, s.main), group=4)


def put_xfaces(plan, x_refs, comp):
    odd = lax.axis_index("gx") % 2
    has_lo, has_hi = flags("gx", plan.nx)
    for i, ref in enumerate(x_refs):
        at_high = odd == i
        has = (at_high & has_hi) | (jnp.logical_not(at_high) & has_lo)
        first = pl.multiple_of(plan.row(jnp.where(at_high, plan.cx, -RIM), 0) - SUB, SUB)
        packed = jnp.where(has, ref[pl.ds(plan.xrows, SUB), :], 0.0)
        row = iota((SUB, LANES), 0)
        n = plan.xrows // SUB
        values = []
        for k in range(n):
            for tile in range(2):
                v = jnp.where(has, ref[pl.ds(k * SUB, SUB), :], 0.0) if tile == 0 else unpack_rim(packed, k)
                rows = pl.ds(tile * plan.crows + first + k * SUB, SUB)
                if k == 0:
                    v = jnp.where(row >= SUB - RIM, v, comp[rows, :])
                if k == n - 1:
                    v = jnp.where(row < RIM, v, comp[rows, :])
                values.append((rows, v))
        for rows, v in values:
            comp[rows, :] = v


def edge_kernel(plan, n_x, comp_in, second_in, third_in, own_ref, *rest):
    x_refs, msg_refs = rest[:n_x], rest[n_x : n_x + plan.nz - 1]
    comp, second, third, *e_refs = rest[n_x + plan.nz - 1 :]
    del comp_in, second_in, third_in
    me = lax.axis_index("gz")
    cuts = []
    for shift in range(plan.nz):
        tags = msg_refs[plan.nz - shift - 1] if shift else own_ref
        used = 0
        for p in range(plan.slots):
            code = message_code(plan, tags, p)
            x0, y0, home, z0 = decode(plan, code)
            here = (code >= 0) & (home == me)
            base = jnp.minimum(used, CAP - 1) * plan.foot
            cuts.append((here, e_refs[shift], base, x0, y0, lax.bitwise_and(z0, plan.cz - 1)))
            used = used + here.astype(jnp.int32)
    cx, pitch, crows = plan.cx, plan.pitch, plan.crows
    put_xfaces(plan, x_refs, comp)
    s = Sweeps(plan, comp, second, third)
    x_lo, x_hi = flags("gx", plan.nx)
    every = range(s.main + 1)
    s.step2([(-2, j) for j in range(s.main + 1)] + [(cx - 2, s.main)])
    s.step2([(x, j) for x in (-1, 0) for j in every])
    s.step2([(x, j) for x in (cx - 1, cx) for j in every])
    s.step2([(cx + 1, j) for j in range(s.main)])
    for has, x in ((x_lo, 1 - RIM), (x_hi, cx)):

        @pl.when(jnp.logical_not(has))
        def _():
            for base in (0, crows):
                second[pl.ds(base + plan.row(x, -RIM), 2 * pitch), :] = jnp.zeros((2 * pitch, LANES), F32)

    s.step3([(-1, j) for j in every] + [(cx - 3, s.main)])
    s.step3([(x, j) for x in (0, 1) for j in every])
    s.step3([(x, j) for x in (cx - 2, cx - 1) for j in every])
    s.step3([(cx, j) for j in range(s.main)])
    for has, x in ((x_lo, -1), (x_hi, cx)):

        @pl.when(jnp.logical_not(has))
        def _():
            for base in (0, crows, 2 * crows):
                third[pl.ds(base + plan.row(x, -RIM), pitch), :] = jnp.zeros((pitch, LANES), F32)

    for here, out, base, x0, y0, z0 in cuts:

        @pl.when(here)
        def _():
            cut_patch(plan, third, out, base, x0, y0, z0)


def cut_patch(plan, third, out, base, x0, y0, z0):
    foot, pitch, crows, win = plan.foot, plan.pitch, plan.crows, plan.win
    base = pl.multiple_of(base, SUB)
    lane = iota((foot, LANES), 1)
    offset = jnp.where(z0 == 0, crows, jnp.where(z0 == plan.cz - foot, 2 * crows, 0))
    outs = [jnp.zeros((foot, LANES), F32) for _ in range(plan.elanes // LANES)]

    def put(v, source, target, width):
        tile, k = divmod(target, LANES)
        v = pltpu.roll(v, lax.bitwise_and(k - source + 2 * LANES, LANES - 1), 1)
        outs[tile] = jnp.where((lane >= k) & (lane < k + width), v, outs[tile])
        if k + width > LANES:
            outs[tile + 1] = jnp.where(lane < k + width - LANES, v, outs[tile + 1])

    for y in range(-1, foot + 1):
        v = third[pl.ds(offset + plan.row(x0, y0 + y), foot, stride=pitch), :]
        put(v, z0 - 1, (y + 1) * win, win)
    for i, x in enumerate((-1, foot)):
        v = third[pl.ds(pl.multiple_of(plan.row(x0 + x, y0), SUB), foot), :]
        put(v, z0, plan.elow + i * foot, foot)
    for i, v in enumerate(outs):
        out[pl.ds(base, foot), i * LANES : (i + 1) * LANES] = v


def emit_kernel(plan, third, out_ref):
    for x in range(plan.cx):
        out_ref[pl.ds(x * plan.cy, plan.cy), :] = third[pl.ds(plan.row(x, 0), plan.cy), :]


def post_kernel(plan, own_ref, fixed, *rest):
    e_refs, (out_hbm, out_ref, ups, first, ghost, yghost, sems) = rest[: plan.nz], rest[plan.nz :]
    pe, foot, tiles, slots, win = plan.pe, plan.foot, plan.tiles, plan.slots, plan.win
    me = lax.axis_index("gz")
    codes = [message_code(plan, own_ref, p) for p in range(slots)]
    homes = [decode(plan, c)[2] for c in codes]
    cuts = []
    for p in range(slots):
        rank = 0
        for q in range(p):
            rank = rank + ((homes[q] == homes[p]) & (codes[q] >= 0)).astype(jnp.int32)
        rank = jnp.minimum(rank, CAP - 1)
        shift = (me - homes[p] + plan.nz) % plan.nz
        got = [jnp.zeros((foot, LANES), F32)] * 3
        for s in range(plan.nz):
            rows = pl.ds(pl.multiple_of(rank * foot, SUB), foot)
            take = (shift == s) & (codes[p] >= 0)
            got = [
                jnp.where(take, e_refs[s][rows, i * LANES : (i + 1) * LANES], g)
                for i, g in enumerate(got)
            ]
        cuts.append(got)
    lane16 = iota((foot, LANES), 1)

    def lanes_from(got, at):
        tile, k = divmod(at, LANES)
        v = pltpu.roll(got[tile], (LANES - k) % LANES, 1)
        if k and tile + 1 < len(got):
            v = jnp.where(lane16 < LANES - k, v, pltpu.roll(got[tile + 1], LANES - k, 1))
        return v

    source, target = iota((LANES, LANES), 0), iota((LANES, LANES), 1)
    q, fz = target // 32, target % 32
    a = 1 + q // 2
    own_lane = a * win + fz // 2 + 1
    side_y = own_lane + jnp.where(q % 2 == 0, -win, win)
    side_z = own_lane + jnp.where(fz % 2 == 0, -1, 1)
    up = jnp.where(source == own_lane, 1.0, 0.0)
    around = 3.0 * up + jnp.where(source == side_y, 1.0, 0.0) + jnp.where(source == side_z, 1.0, 0.0)
    zface = jnp.where((source == side_z) & ((fz == 0) | (fz == pe - 1)), 1.0, 0.0)
    table = jnp.concatenate([up, around, zface], 1).astype(BF16)
    low_y = jnp.where((target >= LANES - 32) & (source == fz // 2 + 1), 1.0, 0.0)
    high_y = jnp.where((target < 32) & (source == 3 * win + fz // 2 + 1), 1.0, 0.0)
    low_y, high_y = low_y.astype(BF16), high_y.astype(BF16)
    xsel = jnp.where((source == fz // 2), 1.0, 0.0).astype(BF16)

    def products(got):
        work = [lanes_from(got, 2 * t * win) for t in range(tiles)]
        sides = [lanes_from(got, plan.elow + i * foot) for i in range(2)]
        return (
            dot2(jnp.concatenate(work, 0), table),
            dot2(work[0], low_y),
            dot2(work[tiles - 1], high_y),
            dot2(jnp.concatenate(sides, 0), xsel),
        )

    ahead = products(cuts[0])
    lane1 = iota((1, LANES), 1)
    copies = [pltpu.make_async_copy(out_ref.at[p], out_hbm.at[p], sems.at[p]) for p in range(slots)]
    lane = iota((SUB, LANES), 1)
    for p in range(slots):
        start = SUB + p * plan.fpitch
        ustart = SUB + p * (foot + SUB)
        spread, lows, highs, xfaces = ahead
        if p + 1 < slots:
            ahead = products(cuts[p + 1])
        for k, line in enumerate((lows, highs)):
            for parity in range(2):
                yghost[k, pl.ds(start + parity, foot, stride=2), :] = line
        for t in range(tiles):
            block = spread[t * foot : (t + 1) * foot]
            mine = block[:, 0:LANES]
            ups[t, pl.ds(ustart, foot), :] = mine
            for i, (urow, row) in enumerate(((ustart - 1, start - 1), (ustart + foot, start + pe))):
                face = xfaces[i * foot : (i + 1) * foot]
                line = jnp.where(lane1 < 64, face[2 * t : 2 * t + 1], face[2 * t + 1 : 2 * t + 2])
                ups[t, pl.ds(urow, 1), :] = line
                first[t, pl.ds(row, 1), :] = line
            base = 0.1 * mine + 0.15 * block[:, LANES : 2 * LANES]
            for parity, shift in enumerate((-1, 1)):
                value = base + 0.15 * ups[t, pl.ds(ustart + shift, foot), :]
                first[t, pl.ds(start + parity, foot, stride=2), :] = value
                ghost[t, pl.ds(start + parity, foot, stride=2), :] = block[:, 2 * LANES :]
        alive = codes[p] >= 0
        for j in range(pe // SUB):
            rows = pl.ds(start + j * SUB, SUB)
            values = []
            for t in range(tiles):
                mid = first[t, rows, :]
                side = ghost[t, rows, :]
                total = first[t, pl.ds(start + j * SUB - 1, SUB), :] + first[t, pl.ds(start + j * SUB + 1, SUB), :]
                total += jnp.where(lane % 32 == 0, side, pltpu.roll(mid, 1, 1))
                total += jnp.where(lane % 32 == 31, side, pltpu.roll(mid, LANES - 1, 1))
                before = first[t - 1, rows, :] if t else yghost[0, rows, :]
                after = first[t + 1, rows, :] if t + 1 < tiles else yghost[1, rows, :]
                total += pltpu.roll(jnp.where(lane >= LANES - 32, before, mid), 32, 1)
                total += pltpu.roll(jnp.where(lane < 32, after, mid), LANES - 32, 1)
                value = fixed[t, rows, :] + (0.1 * mid + 0.15 * total)
                values.append(jnp.where(alive, value, 0.0))
            for t, value in enumerate(values):
                out_ref[p, pl.ds(j * SUB, SUB), t * LANES : (t + 1) * LANES] = value
        copies[p].start()
    for copy in copies:
        copy.wait()


VMEM = pl.BlockSpec(memory_space=pltpu.VMEM)
HBM = pl.BlockSpec(memory_space=pltpu.HBM)
SMEM = pl.BlockSpec(memory_space=pltpu.SMEM)


def call(kernel, outs, args, scratch=(), aliases=None, smem=0, hbm_in=0, hbm_out=0, sems=0, cost=0):
    spaces = [s if isinstance(s, pl.MemoryRef) else pltpu.VMEM(s, F32) for s in scratch]
    return pl.pallas_call(
        kernel,
        out_shape=[jax.ShapeDtypeStruct(s, F32) for s in outs],
        in_specs=[SMEM] * smem + [HBM] * hbm_in + [VMEM] * (len(args) - hbm_in - smem),
        out_specs=[HBM] * hbm_out + [VMEM] * (len(outs) - hbm_out),
        scratch_shapes=spaces + ([pltpu.SemaphoreType.DMA((sems,))] if sems else []),
        input_output_aliases=aliases or {},
        cost_estimate=pl.CostEstimate(flops=cost, bytes_accessed=cost, transcendentals=0) if cost else None,
        compiler_params=pltpu.CompilerParams(vmem_limit_bytes=16 << 20),
    )(*args)


def swap_pairs(axis, size, sends, beside=None):
    got = []
    for start, send in enumerate(sends):
        pairs = [(i, i + 1) for i in range(start, size - 1, 2)]
        pairs += [(b, a) for a, b in pairs]
        names = axis
        if beside and len(pairs) < size:
            alone = set(range(size)) - {a for a, _ in pairs}
            names = (axis, "gz")
            pairs = [(a * beside + g, b * beside + g) for a, b in pairs for g in range(beside)]
            pairs += [(a * beside + g, a * beside + (g ^ 1)) for a in sorted(alone) for g in range(beside)]
        got.append(lax.ppermute(send, names, pairs))
    return got


def cycle(fine_rhs, coarse_rhs, patch_count, patch_corner):
    plan = Plan(fine_rhs.shape, coarse_rhs.shape)
    fine_shape = (plan.tiles, plan.frows, LANES)
    block_shape = (plan.cx * plan.cy, plan.cz)
    comp_shape = (2 * plan.crows, LANES)
    third_shape = (3 * plan.crows, LANES)
    yshape, xshape = (plan.yrows + SUB, LANES), (plan.xrows + SUB, LANES)
    eshape = (plan.erows, plan.elanes)
    n_y, n_x = min(plan.ny - 1, 2), min(plan.nx - 1, 2)
    shifts = range(1, plan.nz)
    bind = functools.partial
    rhs, pre, block, *sends = call(
        bind(pre_kernel, plan),
        [fine_shape, fine_shape, block_shape] + [(plan.msg_rows(s), LANES) for s in shifts],
        [patch_count]
        + [
            pltpu.with_memory_space_constraint(a, pltpu.HBM)
            for a in (patch_corner, fine_rhs, coarse_rhs.reshape(block_shape))
        ],
        scratch=(pltpu.VMEM(patch_corner.shape, jnp.int32),),
        smem=1,
        hbm_in=3,
        sems=plan.slots * plan.tiles + 2,
    )
    own = sends[0]

    def ring(s):
        return [(i, (i + s) % plan.nz) for i in range(plan.nz)]

    msgs = []
    for s, m in zip(shifts, sends):
        msgs.append(lax.ppermute(m, "gz", ring(s)))
    comp, fixed = call(
        bind(base_kernel, plan), [comp_shape, fine_shape], (block, own, rhs, pre), scratch=(fine_shape,), cost=4 << 20
    )
    comp, *ysends = call(bind(compose_kernel, plan), [comp_shape] + [yshape] * n_y, (comp, own, *msgs), aliases={0: 0})
    ygot = swap_pairs("gy", plan.ny, ysends)
    second, third = call(bind(inner_kernel, plan), [comp_shape, third_shape], (comp,), cost=4 << 20)
    comp, second, *xsends = call(
        bind(xface_kernel, plan, n_y),
        [comp_shape, comp_shape] + [xshape] * n_x,
        (comp, second, *ygot),
        aliases={0: 0, 1: 1},
    )
    xgot = swap_pairs("gx", plan.nx, xsends, beside=plan.nz if plan.nz % 2 == 0 else None)
    second, third = call(
        bind(middle_kernel, plan), [comp_shape, third_shape], (comp, second, third), aliases={1: 0, 2: 1}, cost=8 << 20
    )
    _, _, third, *cuts = call(
        bind(edge_kernel, plan, n_x),
        [comp_shape, comp_shape, third_shape] + [eshape] * plan.nz,
        (comp, second, third, own, *xgot, *msgs),
        aliases={0: 0, 1: 1, 2: 2},
    )
    back = [cuts[0]]
    for s in shifts:
        back.append(lax.ppermute(cuts[s], "gz", ring(s)))
    (out,) = call(bind(emit_kernel, plan), [block_shape], (third,), cost=2 << 20)
    (fine,) = call(
        bind(post_kernel, plan),
        [fine_rhs.shape],
        (own, fixed, *back),
        scratch=(
            fine_rhs.shape,
            (plan.tiles, SUB + plan.slots * (plan.foot + SUB), LANES),
            fine_shape,
            fine_shape,
            (2, plan.frows, LANES),
        ),
        hbm_out=1,
        sems=plan.slots,
    )
    return fine, out.reshape(coarse_rhs.shape)


def solution(mesh):
    return jax.shard_map(
        cycle,
        mesh=mesh,
        in_specs=(
            P(("gx", "gy", "gz"), None, None),
            P("gx", "gy", "gz"),
            P(("gx", "gy", "gz")),
            P(("gx", "gy", "gz"), None),
        ),
        out_specs=(P(("gx", "gy", "gz"), None, None), P("gx", "gy", "gz")),
        check_vma=False,
    )
```
